32 devices in a mesh: rep: 16 (over z, y, core), fsdp: 2 (over x).
Axes of the slice: x: 2, y: 2, z: 4, core: 2. Of those that a mesh axis runs over, the one named last changes fastest.
Arguments:
- tokens: bfloat16 [256, 197, 384], P(('rep', 'fsdp')), may hold values from -6 to 6
- gain_one: bfloat16 [384], P('fsdp'), may hold values from 0.25 to 1.75
- shift_one: bfloat16 [384], P('fsdp'), may hold values from -1.75 to 1.75
- qkv_weight: bfloat16 [384, 1152], P('fsdp'), may hold values from -0.3125 to 0.3125
- query_bias: bfloat16 [384], P('fsdp'), may hold values from -3 to 3
- value_bias: bfloat16 [384], P('fsdp'), may hold values from -3 to 3
- out_weight: bfloat16 [384, 384], P('fsdp'), may hold values from -1.25 to 1.25
- out_bias: bfloat16 [384], P('fsdp'), may hold values from -1.75 to 1.75
- gain_two: bfloat16 [384], P('fsdp'), may hold values from 0.25 to 1.75
- shift_two: bfloat16 [384], P('fsdp'), may hold values from -1.75 to 1.75
- lift_weight: bfloat16 [384, 1536], P('fsdp'), may hold values from -0.3125 to 0.3125
- lift_bias: bfloat16 [1536], P('fsdp'), may hold values from -3 to 3
- drop_weight: bfloat16 [1536, 384], P('fsdp'), may hold values from -0.15625 to 0.15625
- drop_bias: bfloat16 [384], P('fsdp'), may hold values from -1.75 to 1.75
- cotangent: bfloat16 [256, 197, 384], P(('rep', 'fsdp')), may hold values from -12 to 12
Outputs:
- output: bfloat16 [256, 197, 384], P(('rep', 'fsdp'))
- input_grad: bfloat16 [256, 197, 384], P(('rep', 'fsdp'))
- grad_gain_one: float32 [384], P('fsdp')
- grad_shift_one: float32 [384], P('fsdp')
- grad_qkv_weight: float32 [384, 1152], P('fsdp')
- grad_query_bias: float32 [384], P('fsdp')
- grad_value_bias: float32 [384], P('fsdp')
- grad_out_weight: float32 [384, 384], P('fsdp')
- grad_out_bias: float32 [384], P('fsdp')
- grad_gain_two: float32 [384], P('fsdp')
- grad_shift_two: float32 [384], P('fsdp')
- grad_lift_weight: float32 [384, 1536], P('fsdp')
- grad_lift_bias: float32 [1536], P('fsdp')
- grad_drop_weight: float32 [1536, 384], P('fsdp')
- grad_drop_bias: float32 [384], P('fsdp')
The draws below stay inside these ranges and needn't reach their ends.
All inputs are finite; a program needn't handle non-finite values.
Results may differ from the reference program's by a relative error of at most 0.023.
Values may be sent and summed in bfloat16 or wider, within the bound.
No kernel may reach another device: no remote copies, remote signals or barrier semaphores. Data moves between devices by JAX's collectives and lax.ppermute only.
A program may use at most 128 MiB of HBM per device.

```python
import jax
import jax.numpy as jnp
from jax import lax

HEADS = 6
HEAD_DIM = 64
FF = 1536
SEQ = 197
IMG_DEV = 8
D = 384
IMAGES = 256


def raised(drawn, stream_key, source, target, shards_of, factor):
    owner, partner = [(jnp.arange(drawn.shape[dim]) // (drawn.shape[dim] // shards_of)).reshape([-1 if axis == dim else 1 for axis in range(drawn.ndim)]) for dim in (source, target)]
    chosen = jax.random.permutation(stream_key, shards_of)[partner]
    strong = (owner == chosen) | (owner == (partner + shards_of // 2) % shards_of)
    return jnp.where(strong, factor * drawn, drawn)


def block_levels(own_key, extent, split, smallest, high):
    factor_of, own = 1.0, jax.random.fold_in(own_key, 6)
    for position, shards_of in split:
        draws = jnp.exp(jax.random.uniform(jax.random.fold_in(own, position), (shards_of,), jnp.float32, smallest / len(split), high / len(split)))
        factor_of = factor_of * jnp.repeat(draws, extent[position] // shards_of).reshape([-1 if axis == position else 1 for axis in range(len(extent))])
    return factor_of


def noise(stream_key, extent, spread, reach, shards=(), kind=jnp.bfloat16):
    entries = jax.random.normal(stream_key, extent, jnp.float32) * spread
    if len(shards) > 0:
        entries = block_levels(stream_key, extent, shards, -0.22, 0.18) * entries
    return jnp.clip(entries, min=-reach, max=reach).astype(kind)


def heavy_noise(rng, extent, spread, reach, split, heavy, dtype=jnp.bfloat16):
    drawn = spread * jax.random.normal(rng, extent, jnp.float32)
    if split:
        drawn = drawn * block_levels(rng, extent, split, -0.22, 0.18)
    return jnp.clip(raised(drawn, jax.random.fold_in(rng, 3), *heavy), -reach, reach).astype(dtype)


def setup_inputs(seed: int = 0) -> dict:
    splits = jax.random.split(jax.random.key(seed), 16)
    return {
        "tokens": noise(splits[0], (IMAGES, SEQ, D), 1.0, 6.0, ((0, 32),)),
        "gain_one": jnp.clip(1.0 + 0.15 * jax.random.normal(splits[1], (D,), jnp.float32), 0.25, 1.75).astype(jnp.bfloat16),
        "shift_one": noise(splits[2], (D,), 0.3, 1.75, ((0, 2),)),
        "qkv_weight": noise(splits[3], (D, 3 * D), D ** -0.5, 0.3125, ((0, 2),)),
        "query_bias": noise(splits[4], (D,), 0.5, 3.0, ((0, 2),)),
        "value_bias": noise(splits[5], (D,), 0.5, 3.0, ((0, 2),)),
        "out_weight": noise(splits[6], (D, D), (D // 16) ** -0.5, 1.25, ((0, 2),)),
        "out_bias": noise(splits[7], (D,), 0.3, 1.75, ((0, 2),)),
        "gain_two": jnp.clip(1.0 + 0.15 * jax.random.normal(splits[8], (D,), jnp.float32), 0.25, 1.75).astype(jnp.bfloat16),
        "shift_two": noise(splits[9], (D,), 0.3, 1.75, ((0, 2),)),
        "lift_weight": noise(splits[10], (D, FF), D ** -0.5, 0.3125, ((0, 2),)),
        "lift_bias": noise(splits[11], (FF,), 0.5, 3.0, ((0, 2),)),
        "drop_weight": noise(splits[12], (FF, D), FF ** -0.5, 0.15625, ((0, 2),)),
        "drop_bias": noise(splits[13], (D,), 0.3, 1.75, ((0, 2),)),
        "cotangent": heavy_noise(splits[14], (IMAGES, SEQ, D), 1.0, 12.0, ((0, 32),), (0, 2, 32, 2.75)),
    }


@jax.custom_vjp
def low(v):
    return lax.optimization_barrier(v.astype(jnp.bfloat16)).astype(jnp.float32)

@jax.custom_vjp
def low_back(v):
    return v

def low_keep(v):
    return (low(v), None)

def low_pass(kept, grad):
    return (grad,)

def back_keep(v):
    return (v, None)

def back_low(kept, grad):
    return (low(grad),)
low.defvjp(low_keep, low_pass)
low_back.defvjp(back_keep, back_low)
epsilon = 1e-06
highest = lax.Precision.HIGHEST

def norm_rows(inputs, gain_vec, shift_vec):
    average = lax.optimization_barrier(jnp.mean(inputs, axis=-1, keepdims=True))
    centred = inputs - average
    variance = lax.optimization_barrier(jnp.mean(centred * centred, axis=-1, keepdims=True))
    return centred * lax.rsqrt(variance + epsilon) * gain_vec + shift_vec

def matmul(left, right):
    return jnp.einsum('gsd,de->gse', left, right, precision=highest)

def layer(inputs, params):
    gain_one, shift_one, qkv_weight, query_bias, value_bias, out_weight, out_bias, gain_two, shift_two, lift_weight, lift_bias, drop_weight, drop_bias = params
    images, length, width = inputs.shape
    normed = low(norm_rows(inputs, gain_one, shift_one))
    qkv_bias = jnp.concatenate([query_bias, jnp.zeros_like(query_bias), value_bias])
    projected = low_back(low(matmul(normed, qkv_weight) + qkv_bias))
    split_heads = projected.reshape(images, length, 3, HEADS, HEAD_DIM)
    query_part = split_heads[:, :, 0]
    key_part = split_heads[:, :, 1]
    value_part = split_heads[:, :, 2]
    scores = low_back(jnp.einsum('iqhe,ikhe->ihqk', query_part, key_part, precision=highest) * HEAD_DIM ** (-0.5))
    top_score = lax.optimization_barrier(jnp.max(scores, axis=-1, keepdims=True))
    exponent = jnp.exp(scores - top_score)
    soft_weights = low(exponent / lax.optimization_barrier(jnp.sum(exponent, axis=-1, keepdims=True)))
    mixed = jnp.einsum('ihqk,ikhe->iqhe', soft_weights, value_part, precision=highest).reshape(images, length, width)
    mixed = low_back(low(mixed))
    attended = low_back(matmul(mixed, out_weight) + out_bias)
    middle = inputs + attended
    normed_two = low(norm_rows(middle, gain_two, shift_two))
    hidden = low_back(matmul(normed_two, lift_weight) + lift_bias)
    active = low(jax.nn.gelu(hidden, approximate=False))
    branch = low_back(matmul(active, drop_weight) + drop_bias)
    return middle + branch

def add_up(first, second):
    return first + second

def reference(tokens, gain_one, shift_one, qkv_weight, query_bias, value_bias, out_weight, out_bias, gain_two, shift_two, lift_weight, lift_bias, drop_weight, drop_bias, cotangent):
    params = tuple((tensor.astype(jnp.float32) for tensor in (gain_one, shift_one, qkv_weight, query_bias, value_bias, out_weight, out_bias, gain_two, shift_two, lift_weight, lift_bias, drop_weight, drop_bias)))
    group_size = 4 * IMG_DEV
    blocks = IMAGES // group_size
    inputs = tokens.astype(jnp.float32).reshape(blocks, group_size, SEQ, D)
    cotangents = cotangent.astype(jnp.float32).reshape(blocks, group_size, SEQ, D)

    def one_block(summed, pair_in):
        block_in, block_cot = pair_in
        result, pullback = jax.vjp(layer, block_in, params)
        grad_in, grad_params = pullback(block_cot)
        summed = jax.tree.map(add_up, summed, grad_params)
        return (summed, (result, grad_in))
    initial = jax.tree.map(jnp.zeros_like, params)
    summed, (results, grads_in) = lax.scan(one_block, initial, (inputs, cotangents))
    output = results.reshape(IMAGES, SEQ, D).astype(jnp.bfloat16)
    input_grad = grads_in.reshape(IMAGES, SEQ, D).astype(jnp.bfloat16)
    return (output, input_grad, summed[0], summed[1], summed[2], summed[3], summed[4], summed[5], summed[6], summed[7], summed[8], summed[9], summed[10], summed[11], summed[12])
```

```python
import functools

import jax
import jax.numpy as jnp
from jax import lax
from jax.experimental import pallas as pl
from jax.experimental.pallas import tpu as pltpu
from jax.sharding import PartitionSpec as P

HEADS = 6
HEAD_DIM = 64
PAIR = 2 * HEAD_DIM
LANE = 128
EPS = 1e-06
ROOT_HALF = 0.7071067811865476
GAUSS = 0.3989422804014327
LOG2E = 1.4426950408889634
SCALE = HEAD_DIM ** (-0.5)
F32 = jnp.float32
BF16 = jnp.bfloat16


def nn(a, b):
    return lax.dot_general(a, b, (((1,), (0,)), ((), ())), preferred_element_type=F32)


def nt(a, b):
    return lax.dot_general(a, b, (((1,), (1,)), ((), ())), preferred_element_type=F32)


def tn(a, b):
    return lax.dot_general(a, b, (((0,), (0,)), ((), ())), preferred_element_type=F32)


def normalise(v):
    mean = jnp.mean(v, axis=-1, keepdims=True)
    centred = v - mean
    var = jnp.mean(centred * centred, axis=-1, keepdims=True)
    inverse = lax.rsqrt(var + EPS)
    return centred * inverse, inverse


def norm_back(grad, normal, inverse, gain):
    scaled = grad * gain
    return inverse * (
        scaled
        - jnp.mean(scaled, axis=-1, keepdims=True)
        - normal * jnp.mean(scaled * normal, axis=-1, keepdims=True)
    )


def fold(v):
    return jnp.sum(v.reshape(v.shape[0] // 8, 8, v.shape[1]), axis=0)


def pad_rows(scratch, ref, length):
    for j in range(ref.shape[0]):
        scratch[j, 0:length, :] = ref[j].astype(scratch.dtype)


def zero_tail(scratch, length):
    images, rows, columns = scratch.shape
    low = (length // 16) * 16
    scratch[:, low:rows, :] = jnp.zeros((images, rows - low, columns), scratch.dtype)


def lane_masks(rows, dtype):
    lane = lax.broadcasted_iota(jnp.int32, (rows, PAIR), 1)
    return lane < HEAD_DIM


def split_pair(v):
    first = lax.broadcasted_iota(jnp.int32, v.shape, 1) < HEAD_DIM
    zero = jnp.zeros_like(v)
    return jnp.concatenate([jnp.where(first, v, zero), jnp.where(first, zero, v)], axis=0)


def join_pair(v):
    rows = v.shape[0] // 2
    first = lax.broadcasted_iota(jnp.int32, (rows, PAIR), 1) < HEAD_DIM
    return jnp.where(first, v[:rows], v[rows:])


def attend_kernel(length, tok_ref, gain_ref, shift_ref, w_ref, bias_ref, normed_ref, proj_ref, mixed_ref, n_s):
    images, rows, width = n_s.shape
    zero_tail(n_s, length)
    for j in range(images):
        normal, _ = normalise(tok_ref[j].astype(F32))
        n_s[j, 0:length, :] = (normal * gain_ref[...] + shift_ref[...]).astype(BF16)
    normed_ref[...] = n_s[...]
    flat = n_s[...].reshape(images * rows, width)
    proj_ref[...] = (
        (nn(flat, w_ref[...]) + bias_ref[...]).astype(BF16).reshape(images, rows, 3 * width)
    )
    live = lax.broadcasted_iota(jnp.int32, (2 * rows, rows), 1) < length
    ones = jnp.ones((rows, PAIR), BF16)
    for j in range(images):
        for c in range(0, width, PAIR):
            query = split_pair(proj_ref[j, :, c : c + PAIR] * jnp.asarray(SCALE, BF16))
            key = proj_ref[j, :, width + c : width + c + PAIR]
            value = proj_ref[j, :, 2 * width + c : 2 * width + c + PAIR]
            scores = jnp.where(live, nt(query, key), -1e30)
            top = jnp.max(scores, axis=-1, keepdims=True)
            weights = jnp.exp(scores - top).astype(BF16)
            both = nn(weights, jnp.concatenate([value, ones], axis=1))
            mixed_ref[j, :, c : c + PAIR] = join_pair(both[:, :PAIR] / both[:, PAIR:]).astype(BF16)


def mlp_kernel(
    length,
    chunk,
    tok_ref,
    cot_ref,
    mixed_ref,
    w_out_ref,
    w_lift_ref,
    w_drop_ref,
    vec_ref,
    lift_bias_ref,
    out_ref,
    d_middle_ref,
    d_mixed_ref,
    g_drop_ref,
    g_lift_ref,
    g_out_ref,
    g_vec_ref,
    g_bias_ref,
    x_s,
    z_s,
    a_drop,
    a_lift,
    a_out,
    a_vec,
    a_bias,
):
    step = pl.program_id(0)
    images, rows, width = x_s.shape
    total = images * rows
    hidden_width = w_lift_ref.shape[1]

    @pl.when(step == 0)
    def _():
        zero_tail(x_s, length)
        zero_tail(z_s, length)
        for acc in (a_drop, a_lift, a_out, a_vec, a_bias):
            acc[...] = jnp.zeros_like(acc)

    pad_rows(x_s, tok_ref, length)
    pad_rows(z_s, cot_ref, length)
    out_bias, gain, shift, drop_bias = (vec_ref[i : i + 1, :] for i in range(4))
    mixed = mixed_ref[...].reshape(total, width)
    dz = z_s[...].reshape(total, width)
    dz_f = dz.astype(F32)
    middle = x_s[...].reshape(total, width).astype(F32) + nn(mixed, w_out_ref[...]) + out_bias
    normal, inverse = normalise(middle)
    normed = (normal * gain + shift).astype(BF16)
    result = middle + drop_bias
    d_normed = jnp.zeros((total, width), F32)
    for c in range(0, hidden_width, chunk):
        part = slice(c, c + chunk)
        hidden = nn(normed, w_lift_ref[:, part]) + lift_bias_ref[:, part]
        cdf = 0.5 + 0.5 * lax.erf(hidden * ROOT_HALF)
        bell = jnp.exp(hidden * hidden * -0.5) * GAUSS
        active = (hidden * cdf).astype(BF16)
        d_active = nt(dz, w_drop_ref[part, :])
        d_hidden_f = d_active * (cdf + hidden * bell)
        d_hidden = d_hidden_f.astype(BF16)
        result = result + nn(active, w_drop_ref[part, :])
        d_normed = d_normed + nt(d_hidden, w_lift_ref[:, part])
        a_drop[part, :] += tn(active, dz)
        a_lift[:, part] += tn(normed, d_hidden)
        a_bias[:, part] += fold(d_hidden.astype(F32))
    out = result.astype(BF16)
    for j in range(images):
        out_ref[j] = out[j * rows : j * rows + length]
    d_middle = dz_f + norm_back(d_normed, normal, inverse, gain)
    d_middle_ref[...] = d_middle.reshape(images, rows, width)
    d_attended = d_middle.astype(BF16)
    d_mixed_ref[...] = nt(d_attended, w_out_ref[...]).astype(BF16).reshape(images, rows, width)
    a_out[...] += tn(mixed, d_attended)
    a_vec[0] += fold(d_attended.astype(F32))
    a_vec[1] += fold(d_normed * normal)
    a_vec[2] += fold(d_normed)
    a_vec[3] += fold(dz_f)

    @pl.when(step == pl.num_programs(0) - 1)
    def _():
        g_drop_ref[...] = a_drop[...].astype(BF16)
        g_lift_ref[...] = a_lift[...].astype(BF16)
        g_out_ref[...] = a_out[...].astype(BF16)
        g_vec_ref[...] = jnp.sum(a_vec[...], axis=1)
        g_bias_ref[...] = jnp.sum(a_bias[...], axis=0, keepdims=True)


def back_kernel(
    length,
    tok_ref,
    proj_ref,
    normed_ref,
    d_mixed_ref,
    d_middle_ref,
    w_ref,
    gain_ref,
    in_grad_ref,
    g_qkv_ref,
    g_vec_ref,
    d_s,
    a_qkv,
    a_proj,
    a_vec,
):
    step = pl.program_id(0)
    images, rows, wide = d_s.shape
    width = wide // 3
    total = images * rows

    @pl.when(step == 0)
    def _():
        for acc in (a_qkv, a_proj, a_vec):
            acc[...] = jnp.zeros_like(acc)

    live = lax.broadcasted_iota(jnp.int32, (rows, 2 * rows), 0) < length
    for j in range(images):
        for c in range(0, width, PAIR):
            query = split_pair(proj_ref[j, :, c : c + PAIR] * jnp.asarray(SCALE, BF16))
            key = proj_ref[j, :, width + c : width + c + PAIR]
            value = proj_ref[j, :, 2 * width + c : 2 * width + c + PAIR]
            d_mixed = split_pair(d_mixed_ref[j, :, c : c + PAIR])
            scores = jnp.where(live, nt(key, query), -1e30)
            top = jnp.max(scores, axis=0, keepdims=True)
            weights = jnp.exp(scores - top)
            probs = weights * (1.0 / jnp.sum(weights, axis=0, keepdims=True))
            d_probs = nt(value, d_mixed)
            delta = jnp.sum(probs * d_probs, axis=0, keepdims=True)
            d_scores = (probs * (d_probs - delta)).astype(BF16)
            d_value = nn(probs.astype(BF16), d_mixed)
            d_key = nn(d_scores, query)
            d_query = join_pair(tn(d_scores, key)) * SCALE
            d_s[j, :, c : c + PAIR] = d_query.astype(BF16)
            d_s[j, :, width + c : width + c + PAIR] = d_key.astype(BF16)
            d_s[j, :, 2 * width + c : 2 * width + c + PAIR] = d_value.astype(BF16)
    d_proj = d_s[...].reshape(total, wide)
    a_qkv[...] += tn(normed_ref[...].reshape(total, width), d_proj)
    a_proj[...] += fold(d_proj.astype(F32))
    d_normed = nt(d_proj, w_ref[...])
    gain = gain_ref[...]
    for j in range(images):
        normal, inverse = normalise(tok_ref[j].astype(F32))
        grad = d_normed[j * rows : j * rows + length]
        in_grad_ref[j] = (
            d_middle_ref[j, 0:length, :] + norm_back(grad, normal, inverse, gain)
        ).astype(BF16)
        a_vec[0:1, :] += jnp.sum(grad * normal, axis=0, keepdims=True)
        a_vec[1:2, :] += jnp.sum(grad, axis=0, keepdims=True)

    @pl.when(step == pl.num_programs(0) - 1)
    def _():
        g_qkv_ref[...] = a_qkv[...].astype(BF16)
        columns = jnp.sum(a_proj[...], axis=0, keepdims=True)
        g_vec_ref[0:2, :] = a_vec[...]
        g_vec_ref[2:3, :] = columns[:, :width]
        g_vec_ref[3:4, :] = columns[:, 2 * width :]


VMEM_LIMIT = 60 * 1024 * 1024


def whole(*shape):
    return pl.BlockSpec(shape, lambda i: (0,) * len(shape))


def per_step(*shape):
    return pl.BlockSpec(shape, lambda i: (i,) + (0,) * (len(shape) - 1))


def forward_attention(tokens, gain, shift, w_qkv, bias):
    images, length, width = tokens.shape
    rows = -(-length // 16) * 16
    group = 2 if images % 2 == 0 else 1
    return pl.pallas_call(
        functools.partial(attend_kernel, length),
        grid=(images // group,),
        in_specs=[
            per_step(group, length, width),
            whole(1, width),
            whole(1, width),
            whole(width, 3 * width),
            whole(1, 3 * width),
        ],
        out_specs=[
            per_step(group, rows, width),
            per_step(group, rows, 3 * width),
            per_step(group, rows, width),
        ],
        out_shape=[
            jax.ShapeDtypeStruct((images, rows, width), BF16),
            jax.ShapeDtypeStruct((images, rows, 3 * width), BF16),
            jax.ShapeDtypeStruct((images, rows, width), BF16),
        ],
        scratch_shapes=[pltpu.VMEM((group, rows, width), BF16)],
        compiler_params=pltpu.CompilerParams(vmem_limit_bytes=VMEM_LIMIT),
        name="attend",
    )(tokens, gain, shift, w_qkv, bias)


def mlp_both_ways(tokens, cotangent, mixed, w_out, w_lift, w_drop, vectors, lift_bias):
    images, length, width = tokens.shape
    rows = mixed.shape[1]
    ff = w_lift.shape[1]
    group = 2 if images % 2 == 0 else 1
    return pl.pallas_call(
        functools.partial(mlp_kernel, length, 256),
        grid=(images // group,),
        in_specs=[
            per_step(group, length, width),
            per_step(group, length, width),
            per_step(group, rows, width),
            whole(width, width),
            whole(width, ff),
            whole(ff, width),
            whole(4, width),
            whole(1, ff),
        ],
        out_specs=[
            per_step(group, length, width),
            per_step(group, rows, width),
            per_step(group, rows, width),
            whole(ff, width),
            whole(width, ff),
            whole(width, width),
            whole(4, width),
            whole(1, ff),
        ],
        out_shape=[
            jax.ShapeDtypeStruct((images, length, width), BF16),
            jax.ShapeDtypeStruct((images, rows, width), F32),
            jax.ShapeDtypeStruct((images, rows, width), BF16),
            jax.ShapeDtypeStruct((ff, width), BF16),
            jax.ShapeDtypeStruct((width, ff), BF16),
            jax.ShapeDtypeStruct((width, width), BF16),
            jax.ShapeDtypeStruct((4, width), F32),
            jax.ShapeDtypeStruct((1, ff), F32),
        ],
        scratch_shapes=[
            pltpu.VMEM((group, rows, width), BF16),
            pltpu.VMEM((group, rows, width), BF16),
            pltpu.VMEM((ff, width), F32),
            pltpu.VMEM((width, ff), F32),
            pltpu.VMEM((width, width), F32),
            pltpu.VMEM((4, 8, width), F32),
            pltpu.VMEM((8, ff), F32),
        ],
        compiler_params=pltpu.CompilerParams(vmem_limit_bytes=VMEM_LIMIT),
        name="mlp",
    )(tokens, cotangent, mixed, w_out, w_lift, w_drop, vectors, lift_bias)


def attention_backward(tokens, projected, normed, d_mixed, d_middle, w_qkv, gain):
    images, length, width = tokens.shape
    rows = normed.shape[1]
    group = 2 if images % 2 == 0 else 1
    return pl.pallas_call(
        functools.partial(back_kernel, length),
        grid=(images // group,),
        in_specs=[
            per_step(group, length, width),
            per_step(group, rows, 3 * width),
            per_step(group, rows, width),
            per_step(group, rows, width),
            per_step(group, rows, width),
            whole(width, 3 * width),
            whole(1, width),
        ],
        out_specs=[
            per_step(group, length, width),
            whole(width, 3 * width),
            whole(4, width),
        ],
        out_shape=[
            jax.ShapeDtypeStruct((images, length, width), BF16),
            jax.ShapeDtypeStruct((width, 3 * width), BF16),
            jax.ShapeDtypeStruct((4, width), F32),
        ],
        scratch_shapes=[
            pltpu.VMEM((group, rows, 3 * width), BF16),
            pltpu.VMEM((width, 3 * width), F32),
            pltpu.VMEM((8, 3 * width), F32),
            pltpu.VMEM((2, width), F32),
        ],
        compiler_params=pltpu.CompilerParams(vmem_limit_bytes=VMEM_LIMIT),
        name="back",
    )(tokens, projected, normed, d_mixed, d_middle, w_qkv, gain)


def per_device(
    tokens,
    gain_one,
    shift_one,
    qkv_weight,
    query_bias,
    value_bias,
    out_weight,
    out_bias,
    gain_two,
    shift_two,
    lift_weight,
    lift_bias,
    drop_weight,
    drop_bias,
    cotangent,
):
    def gather(v):
        return lax.all_gather(v, "fsdp", axis=0, tiled=True)

    width = tokens.shape[-1]
    vectors = gather(
        jnp.stack(
            [gain_one, shift_one, query_bias, value_bias, out_bias, gain_two, shift_two, drop_bias],
            axis=1,
        )
    ).T.astype(F32)
    full_qkv, full_out, full_lift, full_drop = (
        gather(w) for w in (qkv_weight, out_weight, lift_weight, drop_weight)
    )
    full_lift_bias = gather(lift_bias).astype(F32)[None]
    gain, shift = vectors[0:1], vectors[1:2]
    qkv_bias = jnp.concatenate([vectors[2], jnp.zeros((width,), F32), vectors[3]])[None]
    normed, projected, mixed = forward_attention(tokens, gain, shift, full_qkv, qkv_bias)
    outer = jnp.stack([vectors[4], vectors[5], vectors[6], vectors[7]])
    output, d_middle, d_mixed, g_drop, g_lift, g_out, g_vec, g_bias = mlp_both_ways(
        tokens, cotangent, mixed, full_out, full_lift, full_drop, outer, full_lift_bias
    )
    input_grad, g_qkv, g_vec_one = attention_backward(
        tokens, projected, normed, d_mixed, d_middle, full_qkv, gain
    )

    def reduced(v):
        owned = lax.psum_scatter(v.astype(BF16), "fsdp", scatter_dimension=0, tiled=True)
        return lax.psum(owned, "rep").astype(F32)

    return (
        output,
        input_grad,
        reduced(g_vec_one[0]),
        reduced(g_vec_one[1]),
        reduced(g_qkv),
        reduced(g_vec_one[2]),
        reduced(g_vec_one[3]),
        reduced(g_out),
        reduced(g_vec[0]),
        reduced(g_vec[1]),
        reduced(g_vec[2]),
        reduced(g_lift),
        reduced(g_bias[0]),
        reduced(g_drop),
        reduced(g_vec[3]),
    )


def solution(mesh):
    spread = P(("rep", "fsdp"), None, None)
    vector, matrix = P("fsdp"), P("fsdp", None)
    in_specs = (
        spread,
        vector,
        vector,
        matrix,
        vector,
        vector,
        matrix,
        vector,
        vector,
        vector,
        matrix,
        vector,
        matrix,
        vector,
        spread,
    )
    out_specs = (
        spread,
        spread,
        vector,
        vector,
        matrix,
        vector,
        vector,
        matrix,
        vector,
        vector,
        vector,
        matrix,
        vector,
        matrix,
        vector,
    )
    return jax.shard_map(
        per_device, mesh=mesh, in_specs=in_specs, out_specs=out_specs, check_vma=False
    )
```

```python
import functools

import jax
import jax.numpy as jnp
from jax import lax
from jax.experimental import pallas as pl
from jax.experimental.pallas import tpu as pltpu
from jax.sharding import PartitionSpec as P

HEADS = 6
HEAD_DIM = 64
PAIR = 2 * HEAD_DIM
LANE = 128
EPS = 1e-06
ROOT_HALF = 0.7071067811865476
GAUSS = 0.3989422804014327
LOG2E = 1.4426950408889634
SCALE = HEAD_DIM ** (-0.5)
F32 = jnp.float32
BF16 = jnp.bfloat16


def nn(a, b):
    return lax.dot_general(a, b, (((1,), (0,)), ((), ())), preferred_element_type=F32)


def nt(a, b):
    return lax.dot_general(a, b, (((1,), (1,)), ((), ())), preferred_element_type=F32)


def tn(a, b):
    return lax.dot_general(a, b, (((0,), (0,)), ((), ())), preferred_element_type=F32)


def normalise(v):
    mean = jnp.mean(v, axis=-1, keepdims=True)
    centred = v - mean
    var = jnp.mean(centred * centred, axis=-1, keepdims=True)
    inverse = lax.rsqrt(var + EPS)
    return centred * inverse, inverse


def norm_back(grad, normal, inverse, gain):
    scaled = grad * gain
    return inverse * (
        scaled
        - jnp.mean(scaled, axis=-1, keepdims=True)
        - normal * jnp.mean(scaled * normal, axis=-1, keepdims=True)
    )


def fold(v):
    return jnp.sum(v.reshape(v.shape[0] // 8, 8, v.shape[1]), axis=0)


def pad_rows(scratch, ref, length):
    for j in range(ref.shape[0]):
        scratch[j, 0:length, :] = ref[j].astype(scratch.dtype)


def zero_tail(scratch, length):
    images, rows, columns = scratch.shape
    low = (length // 16) * 16
    scratch[:, low:rows, :] = jnp.zeros((images, rows - low, columns), scratch.dtype)


def split_pair(v):
    first = lax.broadcasted_iota(jnp.int32, v.shape, 1) < HEAD_DIM
    zero = jnp.zeros_like(v)
    return jnp.concatenate([jnp.where(first, v, zero), jnp.where(first, zero, v)], axis=0)


def join_pair(v):
    rows = v.shape[0] // 2
    first = lax.broadcasted_iota(jnp.int32, (rows, PAIR), 1) < HEAD_DIM
    return jnp.where(first, v[:rows], v[rows:])


def join_pieces(full, own, near, far, index):
    block = own.shape[0]
    half = block // 2
    x, core = index[0], index[1]
    other = (1 - x) * block
    full[pl.ds(pl.multiple_of(x * block, 16), block), :] = own[...]
    full[pl.ds(pl.multiple_of(other + core * half, 16), half), :] = near[...]
    full[pl.ds(pl.multiple_of(other + (1 - core) * half, 16), half), :] = far[...]


def quarters(index, keep, send):
    x, core = index[0], index[1]
    for slot, half in ((0, x), (1, 1 - x)):
        yield keep, slot, half, core
        yield send, slot, half, 1 - core


def attend_kernel(
    length, index, tok_ref, vec_ref, own, near, far, normed_ref, proj_ref, mixed_ref, w_ref, n_s
):
    images, rows, width = n_s.shape

    @pl.when(pl.program_id(0) == 0)
    def _():
        zero_tail(n_s, length)
        join_pieces(w_ref, own, near, far, index)

    gain, shift = vec_ref[0:1, :], vec_ref[1:2, :]
    bias = jnp.concatenate([vec_ref[2:3, :], jnp.zeros((1, width), F32), vec_ref[3:4, :]], axis=1)
    for j in range(images):
        normal, _ = normalise(tok_ref[j].astype(F32))
        n_s[j, 0:length, :] = (normal * gain + shift).astype(BF16)
    normed_ref[...] = n_s[...]
    flat = n_s[...].reshape(images * rows, width)
    proj_ref[...] = (nn(flat, w_ref[...]) + bias).astype(BF16).reshape(images, rows, 3 * width)
    live = lax.broadcasted_iota(jnp.int32, (2 * rows, rows), 1) < length
    ones = jnp.ones((rows, PAIR), BF16)
    for j in range(images):
        for c in range(0, width, PAIR):
            query = split_pair(proj_ref[j, :, c : c + PAIR] * jnp.asarray(SCALE, BF16))
            key = proj_ref[j, :, width + c : width + c + PAIR]
            value = proj_ref[j, :, 2 * width + c : 2 * width + c + PAIR]
            scores = jnp.where(live, nt(query, key), -1e30)
            top = jnp.max(scores, axis=-1, keepdims=True)
            weights = jnp.exp(scores - top).astype(BF16)
            both = nn(weights, jnp.concatenate([value, ones], axis=1))
            mixed_ref[j, :, c : c + PAIR] = join_pair(both[:, :PAIR] / both[:, PAIR:]).astype(BF16)


def mlp_kernel(
    length,
    chunk,
    index,
    tok_ref,
    cot_ref,
    mixed_ref,
    vec_ref,
    lift_bias_ref,
    out_own,
    out_near,
    out_far,
    lift_own,
    lift_near,
    lift_far,
    drop_own,
    drop_near,
    drop_far,
    out_ref,
    d_middle_ref,
    d_mixed_ref,
    keep_a,
    send_a,
    keep_b,
    send_b,
    x_s,
    z_s,
    w_out_ref,
    w_lift_ref,
    w_drop_ref,
    a_drop,
    a_lift,
    a_out,
    a_vec,
    a_bias,
):
    step = pl.program_id(0)
    images, rows, width = x_s.shape
    total = images * rows
    hidden_width = w_lift_ref.shape[1]

    @pl.when(step == 0)
    def _():
        zero_tail(x_s, length)
        zero_tail(z_s, length)
        join_pieces(w_out_ref, out_own, out_near, out_far, index)
        join_pieces(w_lift_ref, lift_own, lift_near, lift_far, index)
        join_pieces(w_drop_ref, drop_own, drop_near, drop_far, index)
        for acc in (a_drop, a_lift, a_out, a_vec, a_bias):
            acc[...] = jnp.zeros_like(acc)

    pad_rows(x_s, tok_ref, length)
    pad_rows(z_s, cot_ref, length)
    out_bias, gain, shift, drop_bias = (vec_ref[i : i + 1, :] for i in range(4, 8))
    mixed = mixed_ref[...].reshape(total, width)
    dz = z_s[...].reshape(total, width)
    dz_f = dz.astype(F32)
    middle = x_s[...].reshape(total, width).astype(F32) + nn(mixed, w_out_ref[...]) + out_bias
    normal, inverse = normalise(middle)
    normed = (normal * gain + shift).astype(BF16)
    result = middle + drop_bias
    d_normed = jnp.zeros((total, width), F32)
    for c in range(0, hidden_width, chunk):
        part = slice(c, c + chunk)
        hidden = nn(normed, w_lift_ref[:, part]) + lift_bias_ref[:, part]
        cdf = 0.5 + 0.5 * lax.erf(hidden * ROOT_HALF)
        bell = jnp.exp(hidden * hidden * -0.5) * GAUSS
        active = (hidden * cdf).astype(BF16)
        d_active = nt(dz, w_drop_ref[part, :])
        d_hidden_f = d_active * (cdf + hidden * bell)
        d_hidden = d_hidden_f.astype(BF16)
        result = result + nn(active, w_drop_ref[part, :])
        d_normed = d_normed + nt(d_hidden, w_lift_ref[:, part])
        a_drop[part, :] += tn(active, dz)
        a_lift[:, part] += tn(normed, d_hidden)
        a_bias[:, part] += fold(d_hidden.astype(F32))
    out = result.astype(BF16)
    for j in range(images):
        out_ref[j] = out[j * rows : j * rows + length]
    d_middle = dz_f + norm_back(d_normed, normal, inverse, gain)
    d_middle_ref[...] = d_middle.reshape(images, rows, width)
    d_attended = d_middle.astype(BF16)
    d_mixed_ref[...] = nt(d_attended, w_out_ref[...]).astype(BF16).reshape(images, rows, width)
    a_out[...] += tn(mixed, d_attended)
    a_vec[0] += fold(d_attended.astype(F32))
    a_vec[1] += fold(d_normed * normal)
    a_vec[2] += fold(d_normed)
    a_vec[3] += fold(dz_f)

    @pl.when(step == pl.num_programs(0) - 1)
    def _():
        columns = jnp.sum(a_bias[...], axis=0, keepdims=True)
        vector_rows = [jnp.sum(a_vec[...], axis=1)]
        vector_rows += [columns[:, c : c + width] for c in range(0, hidden_width, width)]
        vector_rows += [jnp.zeros((VEC_ROWS - 4 - hidden_width // width, width), F32)]
        vectors = jnp.concatenate(vector_rows, axis=0).astype(BF16)
        deep, tall = a_drop.shape[0] // 4, width // 4
        for dest, slot, half, core in quarters(index, keep_a, send_a):
            first = pl.multiple_of((2 * half + core) * deep, 8)
            dest[slot, 0:deep, :] = a_drop[pl.ds(first, deep), :].astype(BF16)
            dest[slot, deep : deep + VEC_ROWS, :] = vectors
        for dest, slot, half, core in quarters(index, keep_b, send_b):
            rows_of = pl.ds(pl.multiple_of((2 * half + core) * tall, 8), tall)
            blocks = hidden_width // width
            for k in range(blocks):
                dest[slot, k * tall : (k + 1) * tall, :] = a_lift[
                    rows_of, k * width : (k + 1) * width
                ].astype(BF16)
            dest[slot, blocks * tall : (blocks + 1) * tall, :] = a_out[rows_of, :].astype(BF16)


def back_kernel(length, *refs):
    proj_ref, d_mixed_ref = refs[:2]
    d_proj_ref = refs[-1]
    images, rows, wide = d_proj_ref.shape
    width = wide // 3
    live = lax.broadcasted_iota(jnp.int32, (rows, 2 * rows), 0) < length
    for j in range(images):
        for c in range(0, width, PAIR):
            query = split_pair(proj_ref[j, :, c : c + PAIR] * jnp.asarray(SCALE, BF16))
            key = proj_ref[j, :, width + c : width + c + PAIR]
            value = proj_ref[j, :, 2 * width + c : 2 * width + c + PAIR]
            d_mixed = split_pair(d_mixed_ref[j, :, c : c + PAIR])
            scores = jnp.where(live, nt(key, query), -1e30)
            top = jnp.max(scores, axis=0, keepdims=True)
            weights = jnp.exp(scores - top)
            probs = weights * (1.0 / jnp.sum(weights, axis=0, keepdims=True))
            d_probs = nt(value, d_mixed)
            delta = jnp.sum(probs * d_probs, axis=0, keepdims=True)
            d_scores = (probs * (d_probs - delta)).astype(BF16)
            d_value = nn(probs.astype(BF16), d_mixed)
            d_key = nn(d_scores, query)
            d_query = join_pair(tn(d_scores, key)) * SCALE
            d_proj_ref[j, :, c : c + PAIR] = d_query.astype(BF16)
            d_proj_ref[j, :, width + c : width + c + PAIR] = d_key.astype(BF16)
            d_proj_ref[j, :, 2 * width + c : 2 * width + c + PAIR] = d_value.astype(BF16)


def weight_kernel(index, normed_ref, d_proj_ref, keep, send, a_qkv, a_proj):
    step = pl.program_id(0)
    images, rows, wide = d_proj_ref.shape
    width = wide // 3
    total = images * rows

    @pl.when(step == 0)
    def _():
        for acc in (a_qkv, a_proj):
            acc[...] = jnp.zeros_like(acc)

    d_proj = d_proj_ref[...].reshape(total, wide)
    a_qkv[...] += tn(normed_ref[...].reshape(total, width), d_proj)
    a_proj[...] += fold(d_proj.astype(F32))

    @pl.when(step == pl.num_programs(0) - 1)
    def _():
        columns = jnp.sum(a_proj[...], axis=0, keepdims=True)
        vectors = jnp.concatenate(
            [columns[:, :width], columns[:, 2 * width :], jnp.zeros((VEC_ROWS - 2, width), F32)], axis=0
        ).astype(BF16)
        tall = width // 4
        for dest, slot, half, core in quarters(index, keep, send):
            rows_of = pl.ds(pl.multiple_of((2 * half + core) * tall, 8), tall)
            for k in range(3):
                dest[slot, k * tall : (k + 1) * tall, :] = a_qkv[
                    rows_of, k * width : (k + 1) * width
                ].astype(BF16)
            dest[slot, 3 * tall : 3 * tall + VEC_ROWS, :] = vectors


def input_kernel(length, tok_ref, d_proj_ref, d_middle_ref, w_ref, vec_ref, in_grad_ref, g_vec_ref):
    images, rows, wide = d_proj_ref.shape

    @pl.when(pl.program_id(0) == 0)
    def _():
        g_vec_ref[...] = jnp.zeros_like(g_vec_ref)

    d_normed = nt(d_proj_ref[...].reshape(images * rows, wide), w_ref[...])
    gain = vec_ref[0:1, :]
    for j in range(images):
        normal, inverse = normalise(tok_ref[j].astype(F32))
        grad = d_normed[j * rows : j * rows + length]
        in_grad_ref[j] = (
            d_middle_ref[j, 0:length, :] + norm_back(grad, normal, inverse, gain)
        ).astype(BF16)
        g_vec_ref[0:1, :] += jnp.sum(grad * normal, axis=0, keepdims=True)
        g_vec_ref[1:2, :] += jnp.sum(grad, axis=0, keepdims=True)


def placed(full, index, pieces):
    half = pieces[0].shape[0]
    core, y = index[1], index[2]
    spots = ((core, y), (core, 1 - y), (1 - core, y), (1 - core, 1 - y))
    for (where, side), piece in zip(spots, pieces):
        full[where, pl.ds(pl.multiple_of(side * half, 8), half), :] = piece[...].astype(F32)


def own_half(index, row):
    half = row.shape[-1] // 2
    return jnp.where(index[0] == 0, row[:, :half], row[:, half:])[0]


def unpack_outer_kernel(index, *refs):
    a_pieces, b_pieces = refs[0:4], refs[4:8]
    g_drop, g_lift, g_out, g_out_bias, g_gain, g_shift, g_drop_bias, g_lift_bias, a_s, b_s = refs[8:]
    placed(a_s, index, a_pieces)
    placed(b_s, index, b_pieces)
    width = g_out.shape[1]
    deep, tall = g_drop.shape[0] // 2, g_out.shape[0] // 2
    blocks = g_lift.shape[1] // width
    for core in range(2):
        g_drop[core * deep : (core + 1) * deep, :] = a_s[core, 0:deep, :]
        for k in range(blocks):
            g_lift[core * tall : (core + 1) * tall, k * width : (k + 1) * width] = b_s[
                core, k * tall : (k + 1) * tall, :
            ]
        g_out[core * tall : (core + 1) * tall, :] = b_s[core, blocks * tall : (blocks + 1) * tall, :]
    vectors = a_s[0, deep : deep + VEC_ROWS, :]
    for i, ref in enumerate((g_out_bias, g_gain, g_shift, g_drop_bias)):
        ref[...] = own_half(index, vectors[i : i + 1, :])
    for k in range(blocks // 2):
        row = jnp.where(
            index[0] == 0,
            vectors[4 + k : 5 + k, :],
            vectors[4 + blocks // 2 + k : 5 + blocks // 2 + k, :],
        )
        g_lift_bias[k * width : (k + 1) * width] = row[0]


def unpack_inner_kernel(index, *refs):
    pieces, late = refs[0:4], refs[4]
    g_qkv, g_query, g_value, g_gain, g_shift, c_s = refs[5:]
    placed(c_s, index, pieces)
    width = late.shape[1]
    tall = g_qkv.shape[0] // 2
    for core in range(2):
        for k in range(3):
            g_qkv[core * tall : (core + 1) * tall, k * width : (k + 1) * width] = c_s[
                core, k * tall : (k + 1) * tall, :
            ]
    vectors = c_s[0, 3 * tall : 3 * tall + VEC_ROWS, :]
    g_query[...] = own_half(index, vectors[0:1, :])
    g_value[...] = own_half(index, vectors[1:2, :])
    g_gain[...] = own_half(index, late[0:1, :])
    g_shift[...] = own_half(index, late[1:2, :])


VEC_ROWS = 16


VMEM_LIMIT = 60 * 1024 * 1024
PARAMS = pltpu.CompilerParams(vmem_limit_bytes=VMEM_LIMIT)
SCALARS = pl.BlockSpec(memory_space=pltpu.SMEM)


def whole(*shape):
    return pl.BlockSpec(shape, lambda i: (0,) * len(shape))


def whole_like(arrays):
    return [whole(*a.shape) for a in arrays]


def per_step(*shape):
    return pl.BlockSpec(shape, lambda i: (i,) + (0,) * (len(shape) - 1))


def shape_of(dtype, *shape):
    return jax.ShapeDtypeStruct(shape, dtype)


def cost(microseconds):
    return pl.CostEstimate(flops=int(microseconds * 1e3), bytes_accessed=1, transcendentals=0)


def forward_attention(index, tokens, vectors, pieces):
    images, length, width = tokens.shape
    rows = -(-length // 16) * 16
    group = 2 if images % 2 == 0 else 1
    return pl.pallas_call(
        functools.partial(attend_kernel, length),
        grid=(images // group,),
        in_specs=[SCALARS, per_step(group, length, width), *whole_like((vectors, *pieces))],
        out_specs=[
            per_step(group, rows, width),
            per_step(group, rows, 3 * width),
            per_step(group, rows, width),
            whole(width, 3 * width),
        ],
        out_shape=[
            shape_of(BF16, images, rows, width),
            shape_of(BF16, images, rows, 3 * width),
            shape_of(BF16, images, rows, width),
            shape_of(BF16, width, 3 * width),
        ],
        scratch_shapes=[pltpu.VMEM((group, rows, width), BF16)],
        compiler_params=PARAMS,
        cost_estimate=cost(1),
        name="attend",
    )(index, tokens, vectors, *pieces)


def mlp_both_ways(index, tokens, cotangent, mixed, vectors, lift_bias, pieces):
    images, length, width = tokens.shape
    rows = mixed.shape[1]
    ff = lift_bias.shape[1]
    group = 2 if images % 2 == 0 else 1
    a_rows = ff // 4 + VEC_ROWS
    b_rows = (width // 4) * (ff // width + 1)
    return pl.pallas_call(
        functools.partial(mlp_kernel, length, 256),
        grid=(images // group,),
        in_specs=[
            SCALARS,
            per_step(group, length, width),
            per_step(group, length, width),
            per_step(group, rows, width),
            *whole_like((vectors, lift_bias, *pieces)),
        ],
        out_specs=[
            per_step(group, length, width),
            per_step(group, rows, width),
            per_step(group, rows, width),
            whole(2, a_rows, width),
            whole(2, a_rows, width),
            whole(2, b_rows, width),
            whole(2, b_rows, width),
        ],
        out_shape=[
            shape_of(BF16, images, length, width),
            shape_of(F32, images, rows, width),
            shape_of(BF16, images, rows, width),
            shape_of(BF16, 2, a_rows, width),
            shape_of(BF16, 2, a_rows, width),
            shape_of(BF16, 2, b_rows, width),
            shape_of(BF16, 2, b_rows, width),
        ],
        scratch_shapes=[
            pltpu.VMEM((group, rows, width), BF16),
            pltpu.VMEM((group, rows, width), BF16),
            pltpu.VMEM((width, width), BF16),
            pltpu.VMEM((width, ff), BF16),
            pltpu.VMEM((ff, width), BF16),
            pltpu.VMEM((ff, width), F32),
            pltpu.VMEM((width, ff), F32),
            pltpu.VMEM((width, width), F32),
            pltpu.VMEM((4, 8, width), F32),
            pltpu.VMEM((8, ff), F32),
        ],
        compiler_params=PARAMS,
        cost_estimate=cost(1),
        name="mlp",
    )(index, tokens, cotangent, mixed, vectors, lift_bias, *pieces)


def attention_backward(projected, d_mixed, length, first, count, earlier):
    images, rows, wide = projected.shape
    group = 2 if images % 2 == 0 else 1
    start = first // group

    def at(*shape):
        return pl.BlockSpec(shape, lambda i: (i + start if start else i, 0, 0))

    more = [] if earlier is None else [earlier]
    return pl.pallas_call(
        functools.partial(back_kernel, length),
        grid=(count // group,),
        in_specs=[at(group, rows, wide), at(group, rows, wide // 3)]
        + [pl.BlockSpec(memory_space=pl.ANY)] * len(more),
        out_specs=at(group, rows, wide),
        out_shape=shape_of(BF16, images, rows, wide),
        input_output_aliases={2: 0} if more else {},
        compiler_params=PARAMS,
        cost_estimate=cost(count / 2),
        name="back",
    )(projected, d_mixed, *more)


def qkv_weight_gradient(index, normed, d_proj):
    images, rows, width = normed.shape
    group = 2 if images % 2 == 0 else 1
    c_rows = 3 * width // 4 + VEC_ROWS
    return pl.pallas_call(
        weight_kernel,
        grid=(images // group,),
        in_specs=[SCALARS, per_step(group, rows, width), per_step(group, rows, 3 * width)],
        out_specs=[whole(2, c_rows, width)] * 2,
        out_shape=[shape_of(BF16, 2, c_rows, width)] * 2,
        scratch_shapes=[
            pltpu.VMEM((width, 3 * width), F32),
            pltpu.VMEM((8, 3 * width), F32),
        ],
        compiler_params=PARAMS,
        cost_estimate=cost(1),
        name="qkv_weight_gradient",
    )(index, normed, d_proj)


def input_gradient(tokens, d_proj, d_middle, w_qkv, vectors):
    images, length, width = tokens.shape
    rows = d_proj.shape[1]
    group = 2 if images % 2 == 0 else 1
    return pl.pallas_call(
        functools.partial(input_kernel, length),
        grid=(images // group,),
        in_specs=[
            per_step(group, length, width),
            per_step(group, rows, 3 * width),
            per_step(group, rows, width),
            *whole_like((w_qkv, vectors)),
        ],
        out_specs=[per_step(group, length, width), whole(8, width)],
        out_shape=[shape_of(BF16, images, length, width), shape_of(F32, 8, width)],
        compiler_params=PARAMS,
        cost_estimate=cost(1),
        name="input_gradient",
    )(tokens, d_proj, d_middle, w_qkv, vectors)


def unpack_outer(index, a_pieces, b_pieces, width, ff):
    half = width // 2
    return pl.pallas_call(
        unpack_outer_kernel,
        in_specs=[SCALARS] + [pl.BlockSpec(memory_space=pltpu.VMEM)] * 8,
        out_shape=[
            shape_of(F32, ff // 2, width),
            shape_of(F32, half, ff),
            shape_of(F32, half, width),
            *[shape_of(F32, half)] * 4,
            shape_of(F32, ff // 2),
        ],
        scratch_shapes=[
            pltpu.VMEM((2, 2 * a_pieces[0].shape[0], width), F32),
            pltpu.VMEM((2, 2 * b_pieces[0].shape[0], width), F32),
        ],
        compiler_params=PARAMS,
        cost_estimate=cost(3),
        name="unpack_outer",
    )(index, *a_pieces, *b_pieces)


def unpack_inner(index, pieces, late):
    width = late.shape[1]
    half = width // 2
    return pl.pallas_call(
        unpack_inner_kernel,
        in_specs=[SCALARS] + [pl.BlockSpec(memory_space=pltpu.VMEM)] * 5,
        out_shape=[shape_of(F32, half, 3 * width), *[shape_of(F32, half)] * 4],
        scratch_shapes=[pltpu.VMEM((2, 2 * pieces[0].shape[0], width), F32)],
        compiler_params=PARAMS,
        cost_estimate=cost(2),
        name="unpack_inner",
    )(index, *pieces, late)


AXES = ("rep", "fsdp")


class Butterfly:
    def __init__(self):
        rep, x = lax.axis_index("rep"), lax.axis_index("fsdp")
        self.x, self.core, self.y = x, rep & 1, (rep >> 1) & 1
        self.index = jnp.stack([self.x, self.core, self.y]).astype(jnp.int32)

    def swap(self, v, rep_mask, x_mask=0):
        pairs = [
            (rep * 2 + x, (rep ^ rep_mask) * 2 + (x ^ x_mask)) for rep in range(16) for x in range(2)
        ]
        return lax.ppermute(v, AXES, pairs)

    def over_x(self, v):
        return self.swap(v, 0, 1)

    def over_core(self, v):
        return self.swap(v, 1)

    def over_y(self, v):
        return self.swap(v, 2)

    def over_z(self, v, mask):
        return self.swap(v, 4 * mask)

    def gather_weight(self, own):
        half = own.shape[0] // 2
        near = self.over_x(lax.dynamic_slice_in_dim(own, self.core * half, half, 0))
        return own, near, self.over_core(near)

    def gather_vectors(self, own):
        other = self.over_x(own)
        first = self.x == 0
        return jnp.where(first, own, other), jnp.where(first, other, own)

    def halves(self, v):
        return v.reshape(2, v.shape[0] // 2, v.shape[1])

    def to_send(self, v):
        return lax.dynamic_index_in_dim(self.halves(v), 1 - self.y, 0, keepdims=False)

    def to_keep(self, v):
        return lax.dynamic_index_in_dim(self.halves(v), self.y, 0, keepdims=False)

    def over_both_z(self, part):
        part = part + self.over_z(part, 1)
        return part + self.over_z(part, 2)

    def pieces(self, part):
        across = self.over_y(part)
        return part, across, self.over_core(part), self.over_core(across)

    def reduce_late(self, v):
        v = v + self.over_core(v)
        v = v + self.over_x(v)
        v = v + self.over_y(v)
        v = v + self.over_z(v, 1)
        return v + self.over_z(v, 2)


class Collective:
    def __init__(self):
        self.index = jnp.zeros((3,), jnp.int32)

    def gather_weight(self, own):
        full = lax.all_gather(own, "fsdp", axis=0, tiled=True)
        quarter = full.shape[0] // 4
        return full[: 2 * quarter], full[2 * quarter : 3 * quarter], full[3 * quarter :]

    def gather_vectors(self, own):
        full = lax.all_gather(own, "fsdp", axis=0)
        shards, rows, columns = full.shape
        halves = full.reshape(2, shards // 2, rows, columns)
        both = halves.transpose(0, 2, 1, 3).reshape(2, rows, shards // 2 * columns)
        return both[0], both[1]

    def reduce(self, v):
        owned = lax.psum_scatter(v.astype(BF16), "fsdp", scatter_dimension=0, tiled=True)
        return lax.psum(owned, "rep").astype(F32)


def after(*arrays):
    return lax.optimization_barrier(arrays)


def assembled(keep, send, first, tall, blocks):
    order = (keep[0], send[0], keep[1], send[1])
    return jnp.concatenate(
        [
            jnp.concatenate(
                [q[first + k * tall : first + (k + 1) * tall] for k in range(blocks)], axis=1
            )
            for q in order
        ],
        axis=0,
    )


def per_device(
    tokens,
    gain_one,
    shift_one,
    qkv_weight,
    query_bias,
    value_bias,
    out_weight,
    out_bias,
    gain_two,
    shift_two,
    lift_weight,
    lift_bias,
    drop_weight,
    drop_bias,
    cotangent,
    swaps,
):
    length, width = tokens.shape[1:]
    plan = Butterfly() if swaps else Collective()
    shard = gain_one.shape[0]
    own = jnp.concatenate(
        [
            v.reshape(-1, shard)
            for v in (
                gain_one,
                shift_one,
                query_bias,
                value_bias,
                out_bias,
                gain_two,
                shift_two,
                drop_bias,
                lift_bias,
            )
        ],
        axis=0,
    )
    low, high = plan.gather_vectors(own)
    vectors = jnp.concatenate([low[:8], high[:8]], axis=1).astype(F32)
    parts = 2 * width // (2 * shard)
    full_lift_bias = (
        jnp.stack([low[8:], high[8:]])
        .reshape(2, lift_bias.shape[0] // shard, parts // 2, shard)
        .transpose(0, 2, 1, 3)
        .reshape(1, -1)
        .astype(F32)
    )
    qkv = plan.gather_weight(qkv_weight)
    outer = [
        piece for w in (out_weight, lift_weight, drop_weight) for piece in plan.gather_weight(w)
    ]
    index = plan.index
    normed, projected, mixed, full_qkv = forward_attention(index, tokens, vectors, qkv)
    output, d_middle, d_mixed, keep_a, send_a, keep_b, send_b = mlp_both_ways(
        index, tokens, cotangent, mixed, vectors, full_lift_bias, outer
    )
    ff = full_lift_bias.shape[1]
    images = tokens.shape[0]
    backward = functools.partial(attention_backward, projected, d_mixed, length)
    if swaps:
        got_a, got_b = plan.over_core(send_a), plan.over_core(send_b)
        d_proj = backward(0, 2, None)
        d_proj, keep_a, keep_b = after(d_proj, keep_a, keep_b)
        other_a, other_b = keep_a[1] + got_a[1], keep_b[1] + got_b[1]
        d_proj, other_a, other_b = after(d_proj, other_a, other_b)
        over_a, over_b = plan.over_x(other_a), plan.over_x(other_b)
        d_proj = backward(2, images - 4, d_proj)
        d_proj, keep_a = after(d_proj, keep_a)
        mine_a = keep_a[0] + got_a[0] + over_a
        d_proj, out_a = after(d_proj, plan.to_send(mine_a))
        low_a = plan.over_y(out_a)
        d_proj = backward(images - 2, 2, d_proj)
        d_proj, keep_b, mine_a = after(d_proj, keep_b, mine_a)
        mine_b = keep_b[0] + got_b[0] + over_b
        d_proj, out_b = after(d_proj, plan.to_send(mine_b))
        low_b = plan.over_y(out_b)
        part_a = plan.to_keep(mine_a) + low_a
        d_proj, part_a = after(d_proj, part_a)
        keep_c, send_c = qkv_weight_gradient(index, normed, d_proj)
        got_c = plan.over_core(send_c)
        d_proj, other_c = after(d_proj, keep_c[1] + got_c[1])
        over_c = plan.over_x(other_c)
        input_grad, g_first = input_gradient(tokens, d_proj, d_middle, full_qkv, vectors)
        g_first, keep_c = after(g_first, keep_c)
        mine_c = keep_c[0] + got_c[0] + over_c
        part_c = plan.to_keep(mine_c) + plan.over_y(plan.to_send(mine_c))
        part_b = plan.to_keep(mine_b) + low_b
        c_pieces = plan.pieces(plan.over_both_z(part_c))
        a_pieces = plan.pieces(plan.over_both_z(part_a))
        b_pieces = plan.pieces(plan.over_both_z(part_b))
        late = plan.reduce_late(g_first)
        g_drop, g_lift, g_out, g_out_bias, g_gain_two, g_shift_two, g_drop_bias, g_lift_bias = (
            unpack_outer(index, a_pieces, b_pieces, width, ff)
        )
        g_qkv, g_query, g_value, g_gain_one, g_shift_one = unpack_inner(index, c_pieces, late)
    else:
        d_proj = backward(0, images, None)
        keep_c, send_c = qkv_weight_gradient(index, normed, d_proj)
        input_grad, g_first = input_gradient(tokens, d_proj, d_middle, full_qkv, vectors)
        tall = width // 4
        g_drop = plan.reduce(assembled(keep_a, send_a, 0, ff // 4, 1))
        g_lift = plan.reduce(assembled(keep_b, send_b, 0, tall, ff // width))
        g_out = plan.reduce(assembled(keep_b, send_b, ff // width * tall, tall, 1))
        g_qkv = plan.reduce(assembled(keep_c, send_c, 0, tall, 3))
        rows_a = keep_a[0, ff // 4 :]
        rows_c = keep_c[0, 3 * tall :]
        g_out_bias, g_gain_two, g_shift_two, g_drop_bias = (plan.reduce(rows_a[i]) for i in range(4))
        g_lift_bias = plan.reduce(rows_a[4 : 4 + ff // width].reshape(-1))
        g_query, g_value = plan.reduce(rows_c[0]), plan.reduce(rows_c[1])
        g_gain_one, g_shift_one = plan.reduce(g_first[0]), plan.reduce(g_first[1])
    return (
        output,
        input_grad,
        g_gain_one,
        g_shift_one,
        g_qkv,
        g_query,
        g_value,
        g_out,
        g_out_bias,
        g_gain_two,
        g_shift_two,
        g_lift,
        g_lift_bias,
        g_drop,
        g_drop_bias,
    )


def solution(mesh):
    spread = P(("rep", "fsdp"), None, None)
    vector, matrix = P("fsdp"), P("fsdp", None)
    in_specs = (
        spread,
        vector,
        vector,
        matrix,
        vector,
        vector,
        matrix,
        vector,
        vector,
        vector,
        matrix,
        vector,
        matrix,
        vector,
        spread,
    )
    out_specs = (
        spread,
        spread,
        vector,
        vector,
        matrix,
        vector,
        vector,
        matrix,
        vector,
        vector,
        vector,
        matrix,
        vector,
        matrix,
        vector,
    )
    swaps = mesh.shape["rep"] == 16 and mesh.shape["fsdp"] == 2
    return jax.shard_map(
        functools.partial(per_device, swaps=swaps),
        mesh=mesh,
        in_specs=in_specs,
        out_specs=out_specs,
        check_vma=False,
    )
```

```python
import functools

import jax
import jax.numpy as jnp
from jax import lax
from jax.experimental import pallas as pl
from jax.experimental.pallas import tpu as pltpu
from jax.sharding import PartitionSpec as P

HEADS = 6
HEAD_DIM = 64
PAIR = 2 * HEAD_DIM
LANE = 128
EPS = 1e-06
ROOT_HALF = 0.7071067811865476
GAUSS = 0.3989422804014327
LOG2E = 1.4426950408889634
SCALE = HEAD_DIM ** (-0.5)
F32 = jnp.float32
BF16 = jnp.bfloat16


def nn(a, b):
    return lax.dot_general(a, b, (((1,), (0,)), ((), ())), preferred_element_type=F32)


def nt(a, b):
    return lax.dot_general(a, b, (((1,), (1,)), ((), ())), preferred_element_type=F32)


def tn(a, b):
    return lax.dot_general(a, b, (((0,), (0,)), ((), ())), preferred_element_type=F32)


def normalise(v):
    mean = jnp.mean(v, axis=-1, keepdims=True)
    centred = v - mean
    var = jnp.mean(centred * centred, axis=-1, keepdims=True)
    inverse = lax.rsqrt(var + EPS)
    return centred * inverse, inverse


def norm_back(grad, normal, inverse, gain):
    scaled = grad * gain
    return inverse * (
        scaled
        - jnp.mean(scaled, axis=-1, keepdims=True)
        - normal * jnp.mean(scaled * normal, axis=-1, keepdims=True)
    )


def fold(v):
    return jnp.sum(v.reshape(v.shape[0] // 8, 8, v.shape[1]), axis=0)


def pad_rows(scratch, ref, length):
    for j in range(ref.shape[0]):
        scratch[j, 0:length, :] = ref[j].astype(scratch.dtype)


def zero_tail(scratch, length):
    images, rows, columns = scratch.shape
    low = (length // 16) * 16
    scratch[:, low:rows, :] = jnp.zeros((images, rows - low, columns), scratch.dtype)


def split_pair(v):
    first = lax.broadcasted_iota(jnp.int32, v.shape, 1) < HEAD_DIM
    zero = jnp.zeros_like(v)
    return jnp.concatenate([jnp.where(first, v, zero), jnp.where(first, zero, v)], axis=0)


def join_pair(v):
    rows = v.shape[0] // 2
    first = lax.broadcasted_iota(jnp.int32, (rows, PAIR), 1) < HEAD_DIM
    return jnp.where(first, v[:rows], v[rows:])


def join_pieces(full, own, near, far, index):
    block = own.shape[0]
    half = block // 2
    x, core = index[0], index[1]
    other = (1 - x) * block
    full[pl.ds(pl.multiple_of(x * block, 16), block), :] = own[...]
    full[pl.ds(pl.multiple_of(other + core * half, 16), half), :] = near[0:half, :]
    full[pl.ds(pl.multiple_of(other + (1 - core) * half, 16), half), :] = far[0:half, :]


def quarters(index, keep, send):
    x, core = index[0], index[1]
    for slot, half in ((0, x), (1, 1 - x)):
        yield keep, slot, half, core
        yield send, slot, half, 1 - core


def pack_first_kernel(index, *refs):
    vectors, lift_bias, weight, packed = refs[:8], *refs[8:]
    half = weight.shape[0] // 2
    shard, width = vectors[0].shape[0], weight.shape[1] // 3
    packed[0:half, :] = weight[pl.ds(pl.multiple_of(index[1] * half, 16), half), :]
    packed[half:, :] = jnp.zeros((8, 3 * width), BF16)
    for i, ref in enumerate(vectors):
        row = ref[...].astype(F32).reshape(1, shard)
        packed[half + i : half + i + 1, 0:shard] = row.astype(BF16)
    bias = lift_bias[...].astype(F32).reshape(1, lift_bias.shape[0]).astype(BF16)
    for k in range(lift_bias.shape[0] // width):
        packed[half + k : half + k + 1, width : 2 * width] = bias[:, k * width : (k + 1) * width]


def pack_rest_kernel(index, *refs):
    for weight, half_out in zip(refs[:3], refs[3:]):
        half = half_out.shape[0]
        half_out[...] = weight[pl.ds(pl.multiple_of(index[1] * half, 16), half), :]


def join_vectors(vec_ref, own, other, index):
    width = vec_ref.shape[1]
    half = width // 2
    mine, theirs = own[-8:, :].astype(F32), other[-8:, :].astype(F32)
    first = index[0] == 0
    low, high = jnp.where(first, mine, theirs), jnp.where(first, theirs, mine)
    vec_ref[0:8, :] = jnp.concatenate([low[:, :half], high[:, :half]], axis=1)
    blocks = vec_ref.shape[0] // 2 - 4
    vec_ref[8 : 8 + blocks, :] = low[:blocks, width : 2 * width]
    vec_ref[8 + blocks :, :] = high[:blocks, width : 2 * width]


def attend_kernel(
    length,
    index,
    tok_ref,
    packed,
    own,
    near,
    far,
    normed_ref,
    proj_ref,
    mixed_ref,
    w_ref,
    vec_ref,
    n_s,
):
    images, rows, width = n_s.shape

    @pl.when(pl.program_id(0) == 0)
    def _():
        zero_tail(n_s, length)
        join_pieces(w_ref, own, near, far, index)
        join_vectors(vec_ref, packed, near, index)

    gain, shift = vec_ref[0:1, :], vec_ref[1:2, :]
    bias = jnp.concatenate([vec_ref[2:3, :], jnp.zeros((1, width), F32), vec_ref[3:4, :]], axis=1)
    for j in range(images):
        normal, _ = normalise(tok_ref[j].astype(F32))
        n_s[j, 0:length, :] = (normal * gain + shift).astype(BF16)
    normed_ref[...] = n_s[...]
    flat = n_s[...].reshape(images * rows, width)
    proj_ref[...] = (nn(flat, w_ref[...]) + bias).astype(BF16).reshape(images, rows, 3 * width)
    live = lax.broadcasted_iota(jnp.int32, (2 * rows, rows), 1) < length
    ones = jnp.ones((rows, PAIR), BF16)
    for j in range(images):
        for c in range(0, width, PAIR):
            query = split_pair(proj_ref[j, :, c : c + PAIR] * jnp.asarray(SCALE, BF16))
            key = proj_ref[j, :, width + c : width + c + PAIR]
            value = proj_ref[j, :, 2 * width + c : 2 * width + c + PAIR]
            scores = jnp.where(live, nt(query, key), -1e30)
            top = jnp.max(scores, axis=-1, keepdims=True)
            weights = jnp.exp(scores - top).astype(BF16)
            both = nn(weights, jnp.concatenate([value, ones], axis=1))
            mixed_ref[j, :, c : c + PAIR] = join_pair(both[:, :PAIR] / both[:, PAIR:]).astype(BF16)


def mlp_kernel(
    length,
    chunk,
    index,
    tok_ref,
    cot_ref,
    mixed_ref,
    vec_ref,
    out_own,
    out_near,
    out_far,
    lift_own,
    lift_near,
    lift_far,
    drop_own,
    drop_near,
    drop_far,
    out_ref,
    d_middle_ref,
    d_mixed_ref,
    keep_a,
    send_a,
    keep_b,
    send_b,
    x_s,
    z_s,
    w_out_ref,
    w_lift_ref,
    w_drop_ref,
    lift_bias_ref,
    a_drop,
    a_lift,
    a_out,
    a_vec,
    a_bias,
):
    step = pl.program_id(0)
    images, rows, width = x_s.shape
    total = images * rows
    hidden_width = w_lift_ref.shape[1]

    @pl.when(step == 0)
    def _():
        zero_tail(x_s, length)
        zero_tail(z_s, length)
        join_pieces(w_out_ref, out_own, out_near, out_far, index)
        join_pieces(w_lift_ref, lift_own, lift_near, lift_far, index)
        join_pieces(w_drop_ref, drop_own, drop_near, drop_far, index)
        for k in range(hidden_width // width):
            lift_bias_ref[:, k * width : (k + 1) * width] = vec_ref[8 + k : 9 + k, :]
        for acc in (a_drop, a_lift, a_out, a_vec, a_bias):
            acc[...] = jnp.zeros_like(acc)

    pad_rows(x_s, tok_ref, length)
    pad_rows(z_s, cot_ref, length)
    out_bias, gain, shift, drop_bias = (vec_ref[i : i + 1, :] for i in range(4, 8))
    mixed = mixed_ref[...].reshape(total, width)
    dz = z_s[...].reshape(total, width)
    dz_f = dz.astype(F32)
    middle = x_s[...].reshape(total, width).astype(F32) + nn(mixed, w_out_ref[...]) + out_bias
    normal, inverse = normalise(middle)
    normed = (normal * gain + shift).astype(BF16)
    result = middle + drop_bias
    d_normed = jnp.zeros((total, width), F32)
    for c in range(0, hidden_width, chunk):
        part = slice(c, c + chunk)
        hidden = nn(normed, w_lift_ref[:, part]) + lift_bias_ref[:, part]
        cdf = 0.5 + 0.5 * lax.erf(hidden * ROOT_HALF)
        bell = jnp.exp(hidden * hidden * -0.5) * GAUSS
        active = (hidden * cdf).astype(BF16)
        d_active = nt(dz, w_drop_ref[part, :])
        d_hidden_f = d_active * (cdf + hidden * bell)
        d_hidden = d_hidden_f.astype(BF16)
        result = result + nn(active, w_drop_ref[part, :])
        d_normed = d_normed + nt(d_hidden, w_lift_ref[:, part])
        a_drop[part, :] += tn(active, dz)
        a_lift[:, part] += tn(normed, d_hidden)
        a_bias[:, part] += fold(d_hidden.astype(F32))
    out = result.astype(BF16)
    for j in range(images):
        out_ref[j] = out[j * rows : j * rows + length]
    d_middle = dz_f + norm_back(d_normed, normal, inverse, gain)
    d_middle_ref[...] = d_middle.reshape(images, rows, width)
    d_attended = d_middle.astype(BF16)
    d_mixed_ref[...] = nt(d_attended, w_out_ref[...]).astype(BF16).reshape(images, rows, width)
    a_out[...] += tn(mixed, d_attended)
    a_vec[0] += fold(d_attended.astype(F32))
    a_vec[1] += fold(d_normed * normal)
    a_vec[2] += fold(d_normed)
    a_vec[3] += fold(dz_f)

    @pl.when(step == pl.num_programs(0) - 1)
    def _():
        columns = jnp.sum(a_bias[...], axis=0, keepdims=True)
        vector_rows = [jnp.sum(a_vec[...], axis=1)]
        vector_rows += [columns[:, c : c + width] for c in range(0, hidden_width, width)]
        vector_rows += [jnp.zeros((VEC_ROWS - 4 - hidden_width // width, width), F32)]
        vectors = jnp.concatenate(vector_rows, axis=0).astype(BF16)
        deep, tall = a_drop.shape[0] // 4, width // 4
        for dest, slot, half, core in quarters(index, keep_a, send_a):
            first = pl.multiple_of((2 * half + core) * deep, 8)
            dest[slot, 0:deep, :] = a_drop[pl.ds(first, deep), :].astype(BF16)
            dest[slot, deep : deep + VEC_ROWS, :] = vectors
        for dest, slot, half, core in quarters(index, keep_b, send_b):
            rows_of = pl.ds(pl.multiple_of((2 * half + core) * tall, 8), tall)
            blocks = hidden_width // width
            for k in range(blocks):
                dest[slot, k * tall : (k + 1) * tall, :] = a_lift[
                    rows_of, k * width : (k + 1) * width
                ].astype(BF16)
            dest[slot, blocks * tall : (blocks + 1) * tall, :] = a_out[rows_of, :].astype(BF16)


def back_kernel(length, *refs):
    proj_ref, d_mixed_ref = refs[:2]
    d_proj_ref = refs[-1]
    images, rows, wide = d_proj_ref.shape
    width = wide // 3
    live = lax.broadcasted_iota(jnp.int32, (rows, 2 * rows), 0) < length
    for j in range(images):
        for c in range(0, width, PAIR):
            query = split_pair(proj_ref[j, :, c : c + PAIR] * jnp.asarray(SCALE, BF16))
            key = proj_ref[j, :, width + c : width + c + PAIR]
            value = proj_ref[j, :, 2 * width + c : 2 * width + c + PAIR]
            d_mixed = split_pair(d_mixed_ref[j, :, c : c + PAIR])
            scores = jnp.where(live, nt(key, query), -1e30)
            top = jnp.max(scores, axis=0, keepdims=True)
            weights = jnp.exp(scores - top)
            probs = weights * (1.0 / jnp.sum(weights, axis=0, keepdims=True))
            d_probs = nt(value, d_mixed)
            delta = jnp.sum(probs * d_probs, axis=0, keepdims=True)
            d_scores = (probs * (d_probs - delta)).astype(BF16)
            d_value = nn(probs.astype(BF16), d_mixed)
            d_key = nn(d_scores, query)
            d_query = join_pair(tn(d_scores, key)) * SCALE
            d_proj_ref[j, :, c : c + PAIR] = d_query.astype(BF16)
            d_proj_ref[j, :, width + c : width + c + PAIR] = d_key.astype(BF16)
            d_proj_ref[j, :, 2 * width + c : 2 * width + c + PAIR] = d_value.astype(BF16)


def weight_kernel(index, normed_ref, d_proj_ref, keep, send, a_qkv, a_proj):
    step = pl.program_id(0)
    images, rows, wide = d_proj_ref.shape
    width = wide // 3
    total = images * rows

    @pl.when(step == 0)
    def _():
        for acc in (a_qkv, a_proj):
            acc[...] = jnp.zeros_like(acc)

    d_proj = d_proj_ref[...].reshape(total, wide)
    a_qkv[...] += tn(normed_ref[...].reshape(total, width), d_proj)
    a_proj[...] += fold(d_proj.astype(F32))

    @pl.when(step == pl.num_programs(0) - 1)
    def _():
        columns = jnp.sum(a_proj[...], axis=0, keepdims=True)
        vectors = jnp.concatenate(
            [columns[:, :width], columns[:, 2 * width :], jnp.zeros((VEC_ROWS - 2, width), F32)], axis=0
        ).astype(BF16)
        tall = width // 4
        for dest, slot, half, core in quarters(index, keep, send):
            rows_of = pl.ds(pl.multiple_of((2 * half + core) * tall, 8), tall)
            for k in range(3):
                dest[slot, k * tall : (k + 1) * tall, :] = a_qkv[
                    rows_of, k * width : (k + 1) * width
                ].astype(BF16)
            dest[slot, 3 * tall : 3 * tall + VEC_ROWS, :] = vectors


def input_kernel(length, tok_ref, d_proj_ref, d_middle_ref, w_ref, vec_ref, in_grad_ref, g_vec_ref):
    images, rows, wide = d_proj_ref.shape

    @pl.when(pl.program_id(0) == 0)
    def _():
        g_vec_ref[...] = jnp.zeros_like(g_vec_ref)

    d_normed = nt(d_proj_ref[...].reshape(images * rows, wide), w_ref[...])
    gain = vec_ref[0:1, :]
    for j in range(images):
        normal, inverse = normalise(tok_ref[j].astype(F32))
        grad = d_normed[j * rows : j * rows + length]
        in_grad_ref[j] = (
            d_middle_ref[j, 0:length, :] + norm_back(grad, normal, inverse, gain)
        ).astype(BF16)
        g_vec_ref[0:1, :] += jnp.sum(grad * normal, axis=0, keepdims=True)
        g_vec_ref[1:2, :] += jnp.sum(grad, axis=0, keepdims=True)


def placed(full, index, pieces):
    half = pieces[0].shape[0]
    core, y = index[1], index[2]
    spots = ((core, y), (core, 1 - y), (1 - core, y), (1 - core, 1 - y))
    for (where, side), piece in zip(spots, pieces):
        full[where, pl.ds(pl.multiple_of(side * half, 8), half), :] = piece[...].astype(F32)


def own_half(index, row):
    half = row.shape[-1] // 2
    return jnp.where(index[0] == 0, row[:, :half], row[:, half:])[0]


def unpack_outer_kernel(index, *refs):
    a_pieces, b_pieces = refs[0:4], refs[4:8]
    g_drop, g_lift, g_out, g_out_bias, g_gain, g_shift, g_drop_bias, g_lift_bias, a_s, b_s = refs[8:]
    placed(a_s, index, a_pieces)
    placed(b_s, index, b_pieces)
    width = g_out.shape[1]
    deep, tall = g_drop.shape[0] // 2, g_out.shape[0] // 2
    blocks = g_lift.shape[1] // width
    for core in range(2):
        g_drop[core * deep : (core + 1) * deep, :] = a_s[core, 0:deep, :]
        for k in range(blocks):
            g_lift[core * tall : (core + 1) * tall, k * width : (k + 1) * width] = b_s[
                core, k * tall : (k + 1) * tall, :
            ]
        g_out[core * tall : (core + 1) * tall, :] = b_s[core, blocks * tall : (blocks + 1) * tall, :]
    vectors = a_s[0, deep : deep + VEC_ROWS, :]
    for i, ref in enumerate((g_out_bias, g_gain, g_shift, g_drop_bias)):
        ref[...] = own_half(index, vectors[i : i + 1, :])
    for k in range(blocks // 2):
        row = jnp.where(
            index[0] == 0,
            vectors[4 + k : 5 + k, :],
            vectors[4 + blocks // 2 + k : 5 + blocks // 2 + k, :],
        )
        g_lift_bias[k * width : (k + 1) * width] = row[0]


def unpack_inner_kernel(index, *refs):
    pieces, late = refs[0:4], refs[4]
    g_qkv, g_query, g_value, g_gain, g_shift, c_s = refs[5:]
    placed(c_s, index, pieces)
    width = late.shape[1]
    tall = g_qkv.shape[0] // 2
    for core in range(2):
        for k in range(3):
            g_qkv[core * tall : (core + 1) * tall, k * width : (k + 1) * width] = c_s[
                core, k * tall : (k + 1) * tall, :
            ]
    vectors = c_s[0, 3 * tall : 3 * tall + VEC_ROWS, :]
    g_query[...] = own_half(index, vectors[0:1, :])
    g_value[...] = own_half(index, vectors[1:2, :])
    g_gain[...] = own_half(index, late[0:1, :])
    g_shift[...] = own_half(index, late[1:2, :])


VEC_ROWS = 16


VMEM_LIMIT = 60 * 1024 * 1024
PARAMS = pltpu.CompilerParams(vmem_limit_bytes=VMEM_LIMIT)
SCALARS = pl.BlockSpec(memory_space=pltpu.SMEM)


def whole(*shape):
    return pl.BlockSpec(shape, lambda i: (0,) * len(shape))


def whole_like(arrays):
    return [whole(*a.shape) for a in arrays]


def per_step(*shape):
    return pl.BlockSpec(shape, lambda i: (i,) + (0,) * (len(shape) - 1))


def shape_of(dtype, *shape):
    return jax.ShapeDtypeStruct(shape, dtype)


def cost(microseconds):
    return pl.CostEstimate(flops=int(microseconds * 1e3), bytes_accessed=1, transcendentals=0)


def pack_first(index, vectors, lift_bias, weight):
    rows, columns = weight.shape
    return pl.pallas_call(
        pack_first_kernel,
        grid=(1,),
        in_specs=[SCALARS, *whole_like((*vectors, lift_bias, weight))],
        out_specs=whole(rows // 2 + 8, columns),
        out_shape=shape_of(BF16, rows // 2 + 8, columns),
        compiler_params=PARAMS,
        cost_estimate=cost(1),
        name="pack_first",
    )(index, *vectors, lift_bias, weight)


def pack_rest(index, weights):
    return pl.pallas_call(
        pack_rest_kernel,
        grid=(1,),
        in_specs=[SCALARS, *whole_like(weights)],
        out_specs=[whole(w.shape[0] // 2, w.shape[1]) for w in weights],
        out_shape=[shape_of(BF16, w.shape[0] // 2, w.shape[1]) for w in weights],
        compiler_params=PARAMS,
        cost_estimate=cost(1),
        name="pack_rest",
    )(index, *weights)


def forward_attention(index, tokens, ff, packed, pieces):
    images, length, width = tokens.shape
    rows = -(-length // 16) * 16
    group = 2 if images % 2 == 0 else 1
    return pl.pallas_call(
        functools.partial(attend_kernel, length),
        grid=(images // group,),
        in_specs=[SCALARS, per_step(group, length, width), *whole_like((packed, *pieces))],
        out_specs=[
            per_step(group, rows, width),
            per_step(group, rows, 3 * width),
            per_step(group, rows, width),
            whole(width, 3 * width),
            whole(8 + ff // width, width),
        ],
        out_shape=[
            shape_of(BF16, images, rows, width),
            shape_of(BF16, images, rows, 3 * width),
            shape_of(BF16, images, rows, width),
            shape_of(BF16, width, 3 * width),
            shape_of(F32, 8 + ff // width, width),
        ],
        scratch_shapes=[pltpu.VMEM((group, rows, width), BF16)],
        compiler_params=PARAMS,
        cost_estimate=cost(1),
        name="attend",
    )(index, tokens, packed, *pieces)


def mlp_both_ways(index, tokens, cotangent, mixed, vectors, ff, pieces):
    images, length, width = tokens.shape
    rows = mixed.shape[1]
    group = 2 if images % 2 == 0 else 1
    a_rows = ff // 4 + VEC_ROWS
    b_rows = (width // 4) * (ff // width + 1)
    return pl.pallas_call(
        functools.partial(mlp_kernel, length, 256),
        grid=(images // group,),
        in_specs=[
            SCALARS,
            per_step(group, length, width),
            per_step(group, length, width),
            per_step(group, rows, width),
            *whole_like((vectors, *pieces)),
        ],
        out_specs=[
            per_step(group, length, width),
            per_step(group, rows, width),
            per_step(group, rows, width),
            whole(2, a_rows, width),
            whole(2, a_rows, width),
            whole(2, b_rows, width),
            whole(2, b_rows, width),
        ],
        out_shape=[
            shape_of(BF16, images, length, width),
            shape_of(F32, images, rows, width),
            shape_of(BF16, images, rows, width),
            shape_of(BF16, 2, a_rows, width),
            shape_of(BF16, 2, a_rows, width),
            shape_of(BF16, 2, b_rows, width),
            shape_of(BF16, 2, b_rows, width),
        ],
        scratch_shapes=[
            pltpu.VMEM((group, rows, width), BF16),
            pltpu.VMEM((group, rows, width), BF16),
            pltpu.VMEM((width, width), BF16),
            pltpu.VMEM((width, ff), BF16),
            pltpu.VMEM((ff, width), BF16),
            pltpu.VMEM((1, ff), F32),
            pltpu.VMEM((ff, width), F32),
            pltpu.VMEM((width, ff), F32),
            pltpu.VMEM((width, width), F32),
            pltpu.VMEM((4, 8, width), F32),
            pltpu.VMEM((8, ff), F32),
        ],
        compiler_params=PARAMS,
        cost_estimate=cost(1),
        name="mlp",
    )(index, tokens, cotangent, mixed, vectors, *pieces)


def attention_backward(projected, d_mixed, length, first, count, earlier):
    images, rows, wide = projected.shape
    group = 2 if images % 2 == 0 else 1
    start = first // group

    def at(*shape):
        return pl.BlockSpec(shape, lambda i: (i + start if start else i, 0, 0))

    more = [] if earlier is None else [earlier]
    return pl.pallas_call(
        functools.partial(back_kernel, length),
        grid=(count // group,),
        in_specs=[at(group, rows, wide), at(group, rows, wide // 3)]
        + [pl.BlockSpec(memory_space=pl.ANY)] * len(more),
        out_specs=at(group, rows, wide),
        out_shape=shape_of(BF16, images, rows, wide),
        input_output_aliases={2: 0} if more else {},
        compiler_params=PARAMS,
        cost_estimate=cost(count / 2),
        name="back",
    )(projected, d_mixed, *more)


def qkv_weight_gradient(index, normed, d_proj):
    images, rows, width = normed.shape
    group = 2 if images % 2 == 0 else 1
    c_rows = 3 * width // 4 + VEC_ROWS
    return pl.pallas_call(
        weight_kernel,
        grid=(images // group,),
        in_specs=[SCALARS, per_step(group, rows, width), per_step(group, rows, 3 * width)],
        out_specs=[whole(2, c_rows, width)] * 2,
        out_shape=[shape_of(BF16, 2, c_rows, width)] * 2,
        scratch_shapes=[
            pltpu.VMEM((width, 3 * width), F32),
            pltpu.VMEM((8, 3 * width), F32),
        ],
        compiler_params=PARAMS,
        cost_estimate=cost(1),
        name="qkv_weight_gradient",
    )(index, normed, d_proj)


def input_gradient(tokens, d_proj, d_middle, w_qkv, vectors):
    images, length, width = tokens.shape
    rows = d_proj.shape[1]
    group = 2 if images % 2 == 0 else 1
    return pl.pallas_call(
        functools.partial(input_kernel, length),
        grid=(images // group,),
        in_specs=[
            per_step(group, length, width),
            per_step(group, rows, 3 * width),
            per_step(group, rows, width),
            *whole_like((w_qkv, vectors)),
        ],
        out_specs=[per_step(group, length, width), whole(8, width)],
        out_shape=[shape_of(BF16, images, length, width), shape_of(F32, 8, width)],
        compiler_params=PARAMS,
        cost_estimate=cost(1),
        name="input_gradient",
    )(tokens, d_proj, d_middle, w_qkv, vectors)


def unpack_outer(index, a_pieces, b_pieces, width, ff):
    half = width // 2
    return pl.pallas_call(
        unpack_outer_kernel,
        grid=(1,),
        in_specs=[SCALARS, *whole_like((*a_pieces, *b_pieces))],
        out_specs=[
            whole(ff // 2, width),
            whole(half, ff),
            whole(half, width),
            *[whole(half)] * 4,
            whole(ff // 2),
        ],
        out_shape=[
            shape_of(F32, ff // 2, width),
            shape_of(F32, half, ff),
            shape_of(F32, half, width),
            *[shape_of(F32, half)] * 4,
            shape_of(F32, ff // 2),
        ],
        scratch_shapes=[
            pltpu.VMEM((2, 2 * a_pieces[0].shape[0], width), F32),
            pltpu.VMEM((2, 2 * b_pieces[0].shape[0], width), F32),
        ],
        compiler_params=PARAMS,
        cost_estimate=cost(3),
        name="unpack_outer",
    )(index, *a_pieces, *b_pieces)


def unpack_inner(index, pieces, late):
    width = late.shape[1]
    half = width // 2
    return pl.pallas_call(
        unpack_inner_kernel,
        grid=(1,),
        in_specs=[SCALARS, *whole_like((*pieces, late))],
        out_specs=[whole(half, 3 * width), *[whole(half)] * 4],
        out_shape=[shape_of(F32, half, 3 * width), *[shape_of(F32, half)] * 4],
        scratch_shapes=[pltpu.VMEM((2, 2 * pieces[0].shape[0], width), F32)],
        compiler_params=PARAMS,
        cost_estimate=cost(2),
        name="unpack_inner",
    )(index, *pieces, late)


AXES = ("rep", "fsdp")


class Butterfly:
    def __init__(self):
        rep, x = lax.axis_index("rep"), lax.axis_index("fsdp")
        self.x, self.core, self.y = x, rep & 1, (rep >> 1) & 1
        self.index = jnp.stack([self.x, self.core, self.y]).astype(jnp.int32)

    def swap(self, v, rep_mask, x_mask=0):
        pairs = [
            (rep * 2 + x, (rep ^ rep_mask) * 2 + (x ^ x_mask)) for rep in range(16) for x in range(2)
        ]
        return lax.ppermute(v, AXES, pairs)

    def over_x(self, v):
        return self.swap(v, 0, 1)

    def over_core(self, v):
        return self.swap(v, 1)

    def over_y(self, v):
        return self.swap(v, 2)

    def over_z(self, v, mask):
        return self.swap(v, 4 * mask)

    def half_of(self, v, which):
        rows = v.shape[-2] // 2
        return lax.dynamic_slice_in_dim(v, which * rows, rows, v.ndim - 2)

    def to_send(self, v):
        return self.half_of(v, 1 - self.y)

    def to_keep(self, v):
        return self.half_of(v, self.y)


class Collective:
    def __init__(self):
        self.index = jnp.zeros((3,), jnp.int32)

    def gather_weight(self, own):
        full = lax.all_gather(own, "fsdp", axis=0, tiled=True)
        quarter = full.shape[0] // 4
        return full[: 2 * quarter], full[2 * quarter : 3 * quarter], full[3 * quarter :]

    def gather_vectors(self, vectors, lift_bias):
        whole_vectors = [lax.all_gather(v, "fsdp", axis=0, tiled=True) for v in vectors]
        whole_bias = lax.all_gather(lift_bias, "fsdp", axis=0, tiled=True)
        width = whole_vectors[0].shape[0]
        table = jnp.stack(whole_vectors).reshape(8, 2, width // 2)
        bias = whole_bias.reshape(2, -1, width)
        return (
            jnp.zeros((2, 8, 3 * width), BF16)
            .at[:, :, : width // 2]
            .set(table.transpose(1, 0, 2))
            .at[:, : bias.shape[1], width : 2 * width]
            .set(bias)
        )

    def reduce(self, v):
        owned = lax.psum_scatter(v.astype(BF16), "fsdp", scatter_dimension=0, tiled=True)
        return lax.psum(owned, "rep").astype(F32)


def after(*arrays):
    return lax.optimization_barrier(arrays)


def assembled(keep, send, first, tall, blocks):
    order = (keep[0], send[0], keep[1], send[1])
    return jnp.concatenate(
        [
            jnp.concatenate(
                [q[first + k * tall : first + (k + 1) * tall] for k in range(blocks)], axis=1
            )
            for q in order
        ],
        axis=0,
    )


def per_device(
    tokens,
    gain_one,
    shift_one,
    qkv_weight,
    query_bias,
    value_bias,
    out_weight,
    out_bias,
    gain_two,
    shift_two,
    lift_weight,
    lift_bias,
    drop_weight,
    drop_bias,
    cotangent,
    swaps,
):
    length, width = tokens.shape[1:]
    plan = Butterfly() if swaps else Collective()
    index = plan.index
    small = (
        gain_one,
        shift_one,
        query_bias,
        value_bias,
        out_bias,
        gain_two,
        shift_two,
        drop_bias,
    )
    ff = lift_weight.shape[1]
    rest = (out_weight, lift_weight, drop_weight)
    if swaps:
        packed = pack_first(index, small, lift_bias, qkv_weight)
        near = plan.over_x(packed)
        qkv = (qkv_weight, near, plan.over_core(near))
        rest_then, packed = after(rest, packed)
        nears = [plan.over_x(half) for half in pack_rest(index, rest_then)]
    else:
        packed, theirs = plan.gather_vectors(small, lift_bias)
        own, near, far = plan.gather_weight(qkv_weight)
        qkv = (own, jnp.concatenate([near, theirs]), far)
    normed, projected, mixed, full_qkv, vectors = forward_attention(
        index, tokens, ff, packed, qkv
    )
    if swaps:
        mixed, nears = after(mixed, nears)
        outer = [
            piece for w, near in zip(rest, nears) for piece in (w, near, plan.over_core(near))
        ]
    else:
        outer = [piece for w in rest for piece in plan.gather_weight(w)]
    output, d_middle, d_mixed, keep_a, send_a, keep_b, send_b = mlp_both_ways(
        index, tokens, cotangent, mixed, vectors, ff, outer
    )
    images = tokens.shape[0]
    backward = functools.partial(attention_backward, projected, d_mixed, length)
    if swaps:
        got_a, got_b = plan.over_core(send_a), plan.over_core(send_b)
        d_proj, got_a, got_b = after(backward(0, 2, None), got_a, got_b)
        other_a = keep_a[1] + got_a[1]
        sum_b = keep_b + got_b
        d_proj, other_a, other_b, sum_b = after(d_proj, other_a, plan.to_send(sum_b), sum_b)
        over_a, over_b = plan.over_x(other_a), plan.over_y(other_b)
        d_proj, over_a, over_b = after(backward(2, images - 4, d_proj), over_a, over_b)
        mine_a = keep_a[0] + got_a[0] + over_a
        both_b = plan.to_keep(sum_b) + over_b
        d_proj, other_a, other_b, mine_a, both_b = after(
            d_proj, plan.to_send(mine_a), both_b[1], mine_a, both_b
        )
        over_a, over_b = plan.over_y(other_a), plan.over_x(other_b)
        d_proj, over_a, over_b = after(backward(images - 2, 2, d_proj), over_a, over_b)
        part_a = plan.to_keep(mine_a) + over_a
        part_b = both_b[0] + over_b
        d_proj, part_a, part_b = after(d_proj, part_a, part_b)
        over_a, over_b = plan.over_z(part_a, 1), plan.over_z(part_b, 1)
        keep_c, send_c = qkv_weight_gradient(index, normed, d_proj)
        send_c, over_a = after(send_c, over_a)
        got_c = plan.over_core(send_c)
        over_b, got_c = after(over_b, got_c)
        part_a, part_b, other_c = part_a + over_a, part_b + over_b, keep_c[1] + got_c[1]
        d_proj, part_a, part_b, other_c = after(d_proj, part_a, part_b, other_c)
        over_c, over_a, over_b = (
            plan.over_x(other_c),
            plan.over_z(part_a, 2),
            plan.over_z(part_b, 2),
        )
        input_grad, late = input_gradient(tokens, d_proj, d_middle, full_qkv, vectors)
        late, over_c = after(late, over_c)
        mine_c = keep_c[0] + got_c[0] + over_c
        other_c, mine_c, late = after(plan.to_send(mine_c), mine_c, late)
        over_c, more = plan.over_y(other_c), plan.over_core(late)
        over_c, more, over_a = after(over_c, more, over_a)
        part_c, late, part_a = plan.to_keep(mine_c) + over_c, late + more, part_a + over_a
        part_c, late, part_a = after(part_c, late, part_a)
        over_c, more = plan.over_z(part_c, 1), plan.over_x(late)
        across_a, beside_a = plan.over_y(part_a), plan.over_core(part_a)
        over_c, more, over_b = after(over_c, more, over_b)
        part_c, late, part_b = part_c + over_c, late + more, part_b + over_b
        part_c, late, part_b = after(part_c, late, part_b)
        over_c, more = plan.over_z(part_c, 2), plan.over_y(late)
        across_b, beside_b = plan.over_y(part_b), plan.over_core(part_b)
        over_c, more, across_a, across_b = after(over_c, more, across_a, across_b)
        a_pieces = (part_a, across_a, beside_a, plan.over_core(across_a))
        b_pieces = (part_b, across_b, beside_b, plan.over_core(across_b))
        part_c, late = part_c + over_c, late + more
        part_c, late, a_pieces, b_pieces = after(part_c, late, a_pieces, b_pieces)
        across_c, beside_c, more = plan.over_y(part_c), plan.over_core(part_c), plan.over_z(late, 1)
        outer_grads = unpack_outer(index, a_pieces, b_pieces, width, ff)
        across_c, beside_c, more, outer_grads = after(across_c, beside_c, more, outer_grads)
        late = late + more
        c_pieces = (part_c, across_c, beside_c, plan.over_core(across_c))
        late = late + plan.over_z(late, 2)
        g_drop, g_lift, g_out, g_out_bias, g_gain_two, g_shift_two, g_drop_bias, g_lift_bias = (
            outer_grads
        )
        g_qkv, g_query, g_value, g_gain_one, g_shift_one = unpack_inner(index, c_pieces, late)
    else:
        d_proj = backward(0, images, None)
        keep_c, send_c = qkv_weight_gradient(index, normed, d_proj)
        input_grad, g_first = input_gradient(tokens, d_proj, d_middle, full_qkv, vectors)
        tall = width // 4
        g_drop = plan.reduce(assembled(keep_a, send_a, 0, ff // 4, 1))
        g_lift = plan.reduce(assembled(keep_b, send_b, 0, tall, ff // width))
        g_out = plan.reduce(assembled(keep_b, send_b, ff // width * tall, tall, 1))
        g_qkv = plan.reduce(assembled(keep_c, send_c, 0, tall, 3))
        rows_a = keep_a[0, ff // 4 :]
        rows_c = keep_c[0, 3 * tall :]
        g_out_bias, g_gain_two, g_shift_two, g_drop_bias = (plan.reduce(rows_a[i]) for i in range(4))
        g_lift_bias = plan.reduce(rows_a[4 : 4 + ff // width].reshape(-1))
        g_query, g_value = plan.reduce(rows_c[0]), plan.reduce(rows_c[1])
        g_gain_one, g_shift_one = plan.reduce(g_first[0]), plan.reduce(g_first[1])
    return (
        output,
        input_grad,
        g_gain_one,
        g_shift_one,
        g_qkv,
        g_query,
        g_value,
        g_out,
        g_out_bias,
        g_gain_two,
        g_shift_two,
        g_lift,
        g_lift_bias,
        g_drop,
        g_drop_bias,
    )


def solution(mesh):
    spread = P(("rep", "fsdp"), None, None)
    vector, matrix = P("fsdp"), P("fsdp", None)
    in_specs = (
        spread,
        vector,
        vector,
        matrix,
        vector,
        vector,
        matrix,
        vector,
        vector,
        vector,
        matrix,
        vector,
        matrix,
        vector,
        spread,
    )
    out_specs = (
        spread,
        spread,
        vector,
        vector,
        matrix,
        vector,
        vector,
        matrix,
        vector,
        vector,
        vector,
        matrix,
        vector,
        matrix,
        vector,
    )
    swaps = mesh.shape["rep"] == 16 and mesh.shape["fsdp"] == 2
    return jax.shard_map(
        functools.partial(per_device, swaps=swaps),
        mesh=mesh,
        in_specs=in_specs,
        out_specs=out_specs,
        check_vma=False,
    )
```

```python
import functools

import jax
import jax.numpy as jnp
from jax import lax
from jax.experimental import pallas as pl
from jax.experimental.pallas import tpu as pltpu
from jax.sharding import PartitionSpec as P

HEADS = 6
HEAD_DIM = 64
PAIR = 2 * HEAD_DIM
LANE = 128
EPS = 1e-06
ROOT_HALF = 0.7071067811865476
GAUSS = 0.3989422804014327
LOG2E = 1.4426950408889634
SCALE = HEAD_DIM ** (-0.5)
F32 = jnp.float32
BF16 = jnp.bfloat16


def nn(a, b):
    return lax.dot_general(a, b, (((1,), (0,)), ((), ())), preferred_element_type=F32)


def nt(a, b):
    return lax.dot_general(a, b, (((1,), (1,)), ((), ())), preferred_element_type=F32)


def tn(a, b):
    return lax.dot_general(a, b, (((0,), (0,)), ((), ())), preferred_element_type=F32)


def normalise(v):
    mean = jnp.mean(v, axis=-1, keepdims=True)
    centred = v - mean
    var = jnp.mean(centred * centred, axis=-1, keepdims=True)
    inverse = lax.rsqrt(var + EPS)
    return centred * inverse, inverse


def norm_back(grad, normal, inverse, gain):
    scaled = grad * gain
    return inverse * (
        scaled
        - jnp.mean(scaled, axis=-1, keepdims=True)
        - normal * jnp.mean(scaled * normal, axis=-1, keepdims=True)
    )


def fold(v):
    return jnp.sum(v.reshape(v.shape[0] // 8, 8, v.shape[1]), axis=0)


def pad_rows(scratch, ref, length):
    for j in range(ref.shape[0]):
        scratch[j, 0:length, :] = ref[j].astype(scratch.dtype)


def zero_tail(scratch, length):
    images, rows, columns = scratch.shape
    low = (length // 16) * 16
    scratch[:, low:rows, :] = jnp.zeros((images, rows - low, columns), scratch.dtype)


def split_pair(v):
    first = lax.broadcasted_iota(jnp.int32, v.shape, 1) < HEAD_DIM
    zero = jnp.zeros_like(v)
    return jnp.concatenate([jnp.where(first, v, zero), jnp.where(first, zero, v)], axis=0)


def join_pair(v):
    rows = v.shape[0] // 2
    first = lax.broadcasted_iota(jnp.int32, (rows, PAIR), 1) < HEAD_DIM
    return jnp.where(first, v[:rows], v[rows:])


def join_pieces(full, own, near, far, index):
    block = own.shape[0]
    half = block // 2
    x, core = index[0], index[1]
    other = (1 - x) * block
    full[pl.ds(pl.multiple_of(x * block, 16), block), :] = own[...]
    full[pl.ds(pl.multiple_of(other + core * half, 16), half), :] = near[0:half, :]
    full[pl.ds(pl.multiple_of(other + (1 - core) * half, 16), half), :] = far[0:half, :]


def quarters(index, keep, send, x_first=False):
    x, core = index[0], index[1]
    yield keep, 0, x, core
    yield (keep if x_first else send), int(x_first), x, 1 - core
    yield (send if x_first else keep), int(not x_first), 1 - x, core
    yield send, 1, 1 - x, 1 - core


def pack_first_kernel(index, *refs):
    vectors, lift_bias, weight, packed = refs[:8], *refs[8:]
    half = weight.shape[0] // 2
    shard, width = vectors[0].shape[0], weight.shape[1] // 3
    packed[0:half, :] = weight[pl.ds(pl.multiple_of(index[1] * half, 16), half), :]
    packed[half:, :] = jnp.zeros((8, 3 * width), BF16)
    for i, ref in enumerate(vectors):
        row = ref[...].astype(F32).reshape(1, shard)
        packed[half + i : half + i + 1, 0:shard] = row.astype(BF16)
    bias = lift_bias[...].astype(F32).reshape(1, lift_bias.shape[0]).astype(BF16)
    for k in range(lift_bias.shape[0] // width):
        packed[half + k : half + k + 1, width : 2 * width] = bias[:, k * width : (k + 1) * width]


def pack_rest_kernel(index, *refs):
    for weight, half_out in zip(refs[:3], refs[3:]):
        half = half_out.shape[0]
        half_out[...] = weight[pl.ds(pl.multiple_of(index[1] * half, 16), half), :]


def join_vectors(vec_ref, own, other, index):
    width = vec_ref.shape[1]
    half = width // 2
    mine, theirs = own[-8:, :].astype(F32), other[-8:, :].astype(F32)
    first = index[0] == 0
    low, high = jnp.where(first, mine, theirs), jnp.where(first, theirs, mine)
    vec_ref[0:8, :] = jnp.concatenate([low[:, :half], high[:, :half]], axis=1)
    blocks = vec_ref.shape[0] // 2 - 4
    vec_ref[8 : 8 + blocks, :] = low[:blocks, width : 2 * width]
    vec_ref[8 + blocks :, :] = high[:blocks, width : 2 * width]


def attend_kernel(
    length,
    index,
    tok_ref,
    packed,
    own,
    near,
    far,
    normed_ref,
    proj_ref,
    mixed_ref,
    w_ref,
    vec_ref,
    n_s,
):
    images, rows, width = n_s.shape

    @pl.when(pl.program_id(0) == 0)
    def _():
        zero_tail(n_s, length)
        join_pieces(w_ref, own, near, far, index)
        join_vectors(vec_ref, packed, near, index)

    gain, shift = vec_ref[0:1, :], vec_ref[1:2, :]
    bias = jnp.concatenate([vec_ref[2:3, :], jnp.zeros((1, width), F32), vec_ref[3:4, :]], axis=1)
    for j in range(images):
        normal, _ = normalise(tok_ref[j].astype(F32))
        n_s[j, 0:length, :] = (normal * gain + shift).astype(BF16)
    normed_ref[...] = n_s[...]
    flat = n_s[...].reshape(images * rows, width)
    proj_ref[...] = (nn(flat, w_ref[...]) + bias).astype(BF16).reshape(images, rows, 3 * width)
    live = lax.broadcasted_iota(jnp.int32, (2 * rows, rows), 1) < length
    ones = jnp.ones((rows, PAIR), BF16)
    for j in range(images):
        for c in range(0, width, PAIR):
            query = split_pair(proj_ref[j, :, c : c + PAIR] * jnp.asarray(SCALE, BF16))
            key = proj_ref[j, :, width + c : width + c + PAIR]
            value = proj_ref[j, :, 2 * width + c : 2 * width + c + PAIR]
            scores = jnp.where(live, nt(query, key), -1e30)
            top = jnp.max(scores, axis=-1, keepdims=True)
            weights = jnp.exp(scores - top).astype(BF16)
            both = nn(weights, jnp.concatenate([value, ones], axis=1))
            mixed_ref[j, :, c : c + PAIR] = join_pair(both[:, :PAIR] / both[:, PAIR:]).astype(BF16)


def join_mlp(index, turn, w_lift, w_drop, lift_bias, vec_ref, lift, drop):
    own, near, far = lift
    block = own.shape[0]
    half = block // 2
    width = w_lift.shape[0]
    x, core = index[0], index[1]
    other = (1 - x) * block
    for k in range(2):
        source = slice((2 * k + turn) * width, (2 * k + turn + 1) * width)
        part = slice(k * width, (k + 1) * width)
        w_lift[pl.ds(pl.multiple_of(x * block, 16), block), part] = own[:, source]
        w_lift[pl.ds(pl.multiple_of(other + core * half, 16), half), part] = near[:, source]
        w_lift[pl.ds(pl.multiple_of(other + (1 - core) * half, 16), half), part] = far[:, source]
        lift_bias[:, part] = vec_ref[8 + 2 * k + turn : 9 + 2 * k + turn, :]
    own, near, far = drop
    w_drop[pl.ds(pl.multiple_of(x * width, 16), width), :] = own[turn * width : (turn + 1) * width, :]
    rest = jnp.where(core == turn, near[...], far[...])
    w_drop[pl.ds(pl.multiple_of((1 - x) * width, 16), width), :] = rest


def mlp_turn(normed, dz, w_lift, w_drop, lift_bias, a_drop, a_lift, a_bias, result, d_normed):
    chunk = 256
    for c in range(0, w_drop.shape[0], chunk):
        part = slice(c, c + chunk)
        hidden = nn(normed, w_lift[:, part]) + lift_bias[:, part]
        cdf = 0.5 + 0.5 * lax.erf(hidden * ROOT_HALF)
        bell = jnp.exp(hidden * hidden * -0.5) * GAUSS
        active = (hidden * cdf).astype(BF16)
        d_active = nt(dz, w_drop[part, :])
        d_hidden = (d_active * (cdf + hidden * bell)).astype(BF16)
        result = result + nn(active, w_drop[part, :])
        d_normed = d_normed + nt(d_hidden, w_lift[:, part])
        a_drop[part, :] += tn(active, dz)
        a_lift[:, part] += tn(normed, d_hidden)
        a_bias[:, part] += fold(d_hidden.astype(F32))
    return result, d_normed


def emit_turn(index, here, there, a_drop, a_lift, a_bias, vector_rows, a_out=None):
    width = a_lift.shape[0]
    columns = jnp.sum(a_bias[...], axis=0, keepdims=True)
    rows = [columns[:, :width], columns[:, width:], *vector_rows]
    count = sum(r.shape[0] for r in rows)
    rows.append(jnp.zeros((VEC_ROWS - count, width), F32))
    vectors = jnp.concatenate(rows, axis=0).astype(BF16)
    deep, tall = width // 2, width // 4
    for dest, slot, half, core in quarters(index, here, there, x_first=a_out is None):
        first = pl.multiple_of((2 * half + core) * deep, 8)
        rows_of = pl.ds(pl.multiple_of((2 * half + core) * tall, 8), tall)
        dest[slot, 0:deep, :] = a_drop[pl.ds(first, deep), :].astype(BF16)
        for k in range(2):
            dest[slot, deep + k * tall : deep + (k + 1) * tall, :] = a_lift[
                rows_of, k * width : (k + 1) * width
            ].astype(BF16)
        dest[slot, 2 * deep : 2 * deep + VEC_ROWS, :] = vectors
        if a_out is not None:
            dest[slot, 2 * deep + VEC_ROWS :, :] = a_out[rows_of, :].astype(BF16)


def mlp_first_kernel(
    length,
    index,
    tok_ref,
    cot_ref,
    mixed_ref,
    vec_ref,
    out_own,
    out_near,
    out_far,
    lift_own,
    lift_near,
    lift_far,
    drop_own,
    drop_near,
    drop_far,
    middle_ref,
    result_ref,
    d_normed_ref,
    here,
    there,
    x_s,
    z_s,
    w_out_ref,
    w_lift_ref,
    w_drop_ref,
    lift_bias_ref,
    a_drop,
    a_lift,
    a_bias,
):
    images, rows, width = x_s.shape
    total = images * rows

    @pl.when(pl.program_id(0) == 0)
    def _():
        zero_tail(x_s, length)
        zero_tail(z_s, length)
        join_pieces(w_out_ref, out_own, out_near, out_far, index)
        join_mlp(
            index,
            0,
            w_lift_ref,
            w_drop_ref,
            lift_bias_ref,
            vec_ref,
            (lift_own, lift_near, lift_far),
            (drop_own, drop_near, drop_far),
        )
        for acc in (a_drop, a_lift, a_bias):
            acc[...] = jnp.zeros_like(acc)

    pad_rows(x_s, tok_ref, length)
    pad_rows(z_s, cot_ref, length)
    out_bias, gain, shift, drop_bias = (vec_ref[i : i + 1, :] for i in range(4, 8))
    mixed = mixed_ref[...].reshape(total, width)
    dz = z_s[...].reshape(total, width)
    middle = x_s[...].reshape(total, width).astype(F32) + nn(mixed, w_out_ref[...]) + out_bias
    middle_ref[...] = middle.reshape(images, rows, width)
    normal, _ = normalise(middle)
    normed = (normal * gain + shift).astype(BF16)
    result, d_normed = mlp_turn(
        normed,
        dz,
        w_lift_ref,
        w_drop_ref,
        lift_bias_ref,
        a_drop,
        a_lift,
        a_bias,
        middle + drop_bias,
        jnp.zeros((total, width), F32),
    )
    result_ref[...] = result.reshape(images, rows, width)
    d_normed_ref[...] = d_normed.reshape(images, rows, width)

    @pl.when(pl.program_id(0) == pl.num_programs(0) - 1)
    def _():
        emit_turn(index, here, there, a_drop, a_lift, a_bias, [])


def mlp_second_kernel(
    length,
    index,
    cot_ref,
    mixed_ref,
    middle_ref,
    result_ref,
    d_normed_ref,
    vec_ref,
    out_own,
    out_near,
    out_far,
    lift_own,
    lift_near,
    lift_far,
    drop_own,
    drop_near,
    drop_far,
    out_ref,
    d_middle_ref,
    d_mixed_ref,
    here,
    there,
    z_s,
    w_out_ref,
    w_lift_ref,
    w_drop_ref,
    lift_bias_ref,
    a_drop,
    a_lift,
    a_out,
    a_vec,
    a_bias,
):
    images, rows, width = z_s.shape
    total = images * rows

    @pl.when(pl.program_id(0) == 0)
    def _():
        zero_tail(z_s, length)
        join_pieces(w_out_ref, out_own, out_near, out_far, index)
        join_mlp(
            index,
            1,
            w_lift_ref,
            w_drop_ref,
            lift_bias_ref,
            vec_ref,
            (lift_own, lift_near, lift_far),
            (drop_own, drop_near, drop_far),
        )
        for acc in (a_drop, a_lift, a_out, a_vec, a_bias):
            acc[...] = jnp.zeros_like(acc)

    pad_rows(z_s, cot_ref, length)
    gain, shift = vec_ref[5:6, :], vec_ref[6:7, :]
    mixed = mixed_ref[...].reshape(total, width)
    dz = z_s[...].reshape(total, width)
    dz_f = dz.astype(F32)
    normal, inverse = normalise(middle_ref[...].reshape(total, width))
    normed = (normal * gain + shift).astype(BF16)
    result, d_normed = mlp_turn(
        normed,
        dz,
        w_lift_ref,
        w_drop_ref,
        lift_bias_ref,
        a_drop,
        a_lift,
        a_bias,
        result_ref[...].reshape(total, width),
        d_normed_ref[...].reshape(total, width),
    )
    out = result.astype(BF16)
    for j in range(images):
        out_ref[j] = out[j * rows : j * rows + length]
    d_middle = dz_f + norm_back(d_normed, normal, inverse, gain)
    d_middle_ref[...] = d_middle.reshape(images, rows, width)
    d_attended = d_middle.astype(BF16)
    d_mixed_ref[...] = nt(d_attended, w_out_ref[...]).astype(BF16).reshape(images, rows, width)
    a_out[...] += tn(mixed, d_attended)
    a_vec[0] += fold(d_attended.astype(F32))
    a_vec[1] += fold(d_normed * normal)
    a_vec[2] += fold(d_normed)
    a_vec[3] += fold(dz_f)

    @pl.when(pl.program_id(0) == pl.num_programs(0) - 1)
    def _():
        vectors = jnp.sum(a_vec[...], axis=1)
        emit_turn(index, here, there, a_drop, a_lift, a_bias, [vectors], a_out)


def back_kernel(length, first, index, proj_ref, normed_ref, d_mixed_ref, *refs):
    if first:
        d_proj_ref, a_qkv, a_proj = refs
    else:
        old_qkv, old_proj, _, d_proj_ref, here, there, a_qkv, a_proj = refs
    images, rows, wide = d_proj_ref.shape
    width = wide // 3
    total = images * rows

    @pl.when(pl.program_id(0) == 0)
    def _():
        a_qkv[...] = jnp.zeros_like(a_qkv) if first else old_qkv[...]
        a_proj[...] = jnp.zeros_like(a_proj) if first else old_proj[...]

    live = lax.broadcasted_iota(jnp.int32, (rows, 2 * rows), 0) < length
    for j in range(images):
        for c in range(0, width, PAIR):
            query = split_pair(proj_ref[j, :, c : c + PAIR] * jnp.asarray(SCALE, BF16))
            key = proj_ref[j, :, width + c : width + c + PAIR]
            value = proj_ref[j, :, 2 * width + c : 2 * width + c + PAIR]
            d_mixed = split_pair(d_mixed_ref[j, :, c : c + PAIR])
            scores = jnp.where(live, nt(key, query), -1e30)
            top = jnp.max(scores, axis=0, keepdims=True)
            weights = jnp.exp(scores - top)
            probs = weights * (1.0 / jnp.sum(weights, axis=0, keepdims=True))
            d_probs = nt(value, d_mixed)
            delta = jnp.sum(probs * d_probs, axis=0, keepdims=True)
            d_scores = (probs * (d_probs - delta)).astype(BF16)
            d_value = nn(probs.astype(BF16), d_mixed)
            d_key = nn(d_scores, query)
            d_query = join_pair(tn(d_scores, key)) * SCALE
            d_proj_ref[j, :, c : c + PAIR] = d_query.astype(BF16)
            d_proj_ref[j, :, width + c : width + c + PAIR] = d_key.astype(BF16)
            d_proj_ref[j, :, 2 * width + c : 2 * width + c + PAIR] = d_value.astype(BF16)
    d_proj = d_proj_ref[...].reshape(total, wide)
    a_qkv[...] += tn(normed_ref[...].reshape(total, width), d_proj)
    a_proj[...] += fold(d_proj.astype(F32))
    if first:
        return

    @pl.when(pl.program_id(0) == pl.num_programs(0) - 1)
    def _():
        columns = jnp.sum(a_proj[...], axis=0, keepdims=True)
        vectors = jnp.concatenate(
            [columns[:, :width], columns[:, 2 * width :], jnp.zeros((VEC_ROWS - 2, width), F32)], axis=0
        ).astype(BF16)
        tall = width // 4
        for dest, slot, half, core in quarters(index, here, there):
            rows_of = pl.ds(pl.multiple_of((2 * half + core) * tall, 8), tall)
            for k in range(3):
                dest[slot, k * tall : (k + 1) * tall, :] = a_qkv[
                    rows_of, k * width : (k + 1) * width
                ].astype(BF16)
            dest[slot, 3 * tall : 3 * tall + VEC_ROWS, :] = vectors


def input_kernel(length, tok_ref, d_proj_ref, d_middle_ref, w_ref, vec_ref, in_grad_ref, g_vec_ref):
    images, rows, wide = d_proj_ref.shape

    @pl.when(pl.program_id(0) == 0)
    def _():
        g_vec_ref[...] = jnp.zeros_like(g_vec_ref)

    d_normed = nt(d_proj_ref[...].reshape(images * rows, wide), w_ref[...])
    gain = vec_ref[0:1, :]
    for j in range(images):
        normal, inverse = normalise(tok_ref[j].astype(F32))
        grad = d_normed[j * rows : j * rows + length]
        in_grad_ref[j] = (
            d_middle_ref[j, 0:length, :] + norm_back(grad, normal, inverse, gain)
        ).astype(BF16)
        g_vec_ref[0:1, :] += jnp.sum(grad * normal, axis=0, keepdims=True)
        g_vec_ref[1:2, :] += jnp.sum(grad, axis=0, keepdims=True)


def placed(full, index, pieces):
    half = pieces[0].shape[0]
    core, y = index[1], index[2]
    spots = ((core, y), (core, 1 - y), (1 - core, y), (1 - core, 1 - y))
    for (where, side), piece in zip(spots, pieces):
        full[where, pl.ds(pl.multiple_of(side * half, 8), half), :] = piece[...].astype(F32)


def own_half(index, row):
    half = row.shape[-1] // 2
    return jnp.where(index[0] == 0, row[:, :half], row[:, half:])[0]


def unpack_outer_kernel(index, *refs):
    g_drop, g_lift, g_out, g_out_bias, g_gain, g_shift, g_drop_bias, g_lift_bias, a_s, b_s = refs[8:]
    width = g_out.shape[1]
    deep, tall = width // 2, width // 4
    for turn, (full, pieces) in enumerate(((a_s, refs[0:4]), (b_s, refs[4:8]))):
        placed(full, index, pieces)
        for core in range(2):
            first = turn * width + core * deep
            g_drop[first : first + deep, :] = full[core, 0:deep, :]
            for k in range(2):
                block = 2 * k + turn
                g_lift[core * tall : (core + 1) * tall, block * width : (block + 1) * width] = full[
                    core, deep + k * tall : deep + (k + 1) * tall, :
                ]
        low, high = full[0, 2 * deep : 2 * deep + 1, :], full[0, 2 * deep + 1 : 2 * deep + 2, :]
        g_lift_bias[turn * width : (turn + 1) * width] = jnp.where(index[0] == 0, low, high)[0]
    for core in range(2):
        g_out[core * tall : (core + 1) * tall, :] = b_s[core, 2 * deep + VEC_ROWS :, :]
    vectors = b_s[0, 2 * deep : 2 * deep + VEC_ROWS, :]
    for i, ref in enumerate((g_out_bias, g_gain, g_shift, g_drop_bias)):
        ref[...] = own_half(index, vectors[2 + i : 3 + i, :])


def unpack_inner_kernel(index, *refs):
    pieces, late = refs[0:4], refs[4]
    g_qkv, g_query, g_value, g_gain, g_shift, c_s = refs[5:]
    placed(c_s, index, pieces)
    width = late.shape[1]
    tall = g_qkv.shape[0] // 2
    for core in range(2):
        for k in range(3):
            g_qkv[core * tall : (core + 1) * tall, k * width : (k + 1) * width] = c_s[
                core, k * tall : (k + 1) * tall, :
            ]
    vectors = c_s[0, 3 * tall : 3 * tall + VEC_ROWS, :]
    g_query[...] = own_half(index, vectors[0:1, :])
    g_value[...] = own_half(index, vectors[1:2, :])
    g_gain[...] = own_half(index, late[0:1, :])
    g_shift[...] = own_half(index, late[1:2, :])


VEC_ROWS = 16


VMEM_LIMIT = 60 * 1024 * 1024
PARAMS = pltpu.CompilerParams(vmem_limit_bytes=VMEM_LIMIT)
SCALARS = pl.BlockSpec(memory_space=pltpu.SMEM)


def whole(*shape):
    return pl.BlockSpec(shape, lambda i: (0,) * len(shape))


def whole_like(arrays):
    return [whole(*a.shape) for a in arrays]


def per_step(*shape):
    return pl.BlockSpec(shape, lambda i: (i,) + (0,) * (len(shape) - 1))


def shape_of(dtype, *shape):
    return jax.ShapeDtypeStruct(shape, dtype)


def cost(microseconds):
    return pl.CostEstimate(flops=int(microseconds * 1e3), bytes_accessed=1, transcendentals=0)


def pack_first(index, vectors, lift_bias, weight):
    rows, columns = weight.shape
    return pl.pallas_call(
        pack_first_kernel,
        grid=(1,),
        in_specs=[SCALARS, *whole_like((*vectors, lift_bias, weight))],
        out_specs=whole(rows // 2 + 8, columns),
        out_shape=shape_of(BF16, rows // 2 + 8, columns),
        compiler_params=PARAMS,
        cost_estimate=cost(1),
        name="pack_first",
    )(index, *vectors, lift_bias, weight)


def pack_rest(index, weights):
    return pl.pallas_call(
        pack_rest_kernel,
        grid=(1,),
        in_specs=[SCALARS, *whole_like(weights)],
        out_specs=[whole(w.shape[0] // 2, w.shape[1]) for w in weights],
        out_shape=[shape_of(BF16, w.shape[0] // 2, w.shape[1]) for w in weights],
        compiler_params=PARAMS,
        cost_estimate=cost(1),
        name="pack_rest",
    )(index, *weights)


def forward_attention(index, tokens, ff, packed, pieces):
    images, length, width = tokens.shape
    rows = -(-length // 16) * 16
    group = 4 if images % 4 == 0 else 1
    return pl.pallas_call(
        functools.partial(attend_kernel, length),
        grid=(images // group,),
        in_specs=[SCALARS, per_step(group, length, width), *whole_like((packed, *pieces))],
        out_specs=[
            per_step(group, rows, width),
            per_step(group, rows, 3 * width),
            per_step(group, rows, width),
            whole(width, 3 * width),
            whole(8 + ff // width, width),
        ],
        out_shape=[
            shape_of(BF16, images, rows, width),
            shape_of(BF16, images, rows, 3 * width),
            shape_of(BF16, images, rows, width),
            shape_of(BF16, width, 3 * width),
            shape_of(F32, 8 + ff // width, width),
        ],
        scratch_shapes=[pltpu.VMEM((group, rows, width), BF16)],
        compiler_params=PARAMS,
        cost_estimate=cost(1),
        name="attend",
    )(index, tokens, packed, *pieces)


def mlp_first(index, tokens, cotangent, mixed, vectors, ff, pieces):
    images, length, width = tokens.shape
    rows = mixed.shape[1]
    group = 2 if images % 2 == 0 else 1
    quarter = width + VEC_ROWS
    return pl.pallas_call(
        functools.partial(mlp_first_kernel, length),
        grid=(images // group,),
        in_specs=[
            SCALARS,
            per_step(group, length, width),
            per_step(group, length, width),
            per_step(group, rows, width),
            *whole_like((vectors, *pieces)),
        ],
        out_specs=[per_step(group, rows, width)] * 3 + [whole(2, quarter, width)] * 2,
        out_shape=[shape_of(F32, images, rows, width)] * 3 + [shape_of(BF16, 2, quarter, width)] * 2,
        scratch_shapes=[
            pltpu.VMEM((group, rows, width), BF16),
            pltpu.VMEM((group, rows, width), BF16),
            pltpu.VMEM((width, width), BF16),
            pltpu.VMEM((width, ff // 2), BF16),
            pltpu.VMEM((ff // 2, width), BF16),
            pltpu.VMEM((1, ff // 2), F32),
            pltpu.VMEM((ff // 2, width), F32),
            pltpu.VMEM((width, ff // 2), F32),
            pltpu.VMEM((8, ff // 2), F32),
        ],
        compiler_params=PARAMS,
        cost_estimate=cost(1),
        name="mlp_first",
    )(index, tokens, cotangent, mixed, vectors, *pieces)


def mlp_second(index, cotangent, mixed, middle, result, d_normed, vectors, ff, pieces):
    images, length, width = cotangent.shape
    rows = mixed.shape[1]
    group = 2 if images % 2 == 0 else 1
    quarter = width + VEC_ROWS + width // 4
    return pl.pallas_call(
        functools.partial(mlp_second_kernel, length),
        grid=(images // group,),
        in_specs=[
            SCALARS,
            per_step(group, length, width),
            *[per_step(group, rows, width)] * 4,
            *whole_like((vectors, *pieces)),
        ],
        out_specs=[
            per_step(group, length, width),
            per_step(group, rows, width),
            per_step(group, rows, width),
            whole(2, quarter, width),
            whole(2, quarter, width),
        ],
        out_shape=[
            shape_of(BF16, images, length, width),
            shape_of(F32, images, rows, width),
            shape_of(BF16, images, rows, width),
            shape_of(BF16, 2, quarter, width),
            shape_of(BF16, 2, quarter, width),
        ],
        scratch_shapes=[
            pltpu.VMEM((group, rows, width), BF16),
            pltpu.VMEM((width, width), BF16),
            pltpu.VMEM((width, ff // 2), BF16),
            pltpu.VMEM((ff // 2, width), BF16),
            pltpu.VMEM((1, ff // 2), F32),
            pltpu.VMEM((ff // 2, width), F32),
            pltpu.VMEM((width, ff // 2), F32),
            pltpu.VMEM((width, width), F32),
            pltpu.VMEM((4, 8, width), F32),
            pltpu.VMEM((8, ff // 2), F32),
        ],
        compiler_params=PARAMS,
        cost_estimate=cost(1),
        name="mlp_second",
    )(index, cotangent, mixed, middle, result, d_normed, vectors, *pieces)


def attention_backward(index, projected, normed, d_mixed, length, start, count, earlier=None):
    images, rows, wide = projected.shape
    width = wide // 3
    group = 2 if images % 2 == 0 else 1
    offset = start // group
    first = earlier is None
    c_rows = 3 * width // 4 + VEC_ROWS

    def at(*shape):
        return pl.BlockSpec(shape, lambda i: (i + offset if offset else i, 0, 0))

    sums = [(width, wide), (8, wide)]
    more = () if first else earlier
    return pl.pallas_call(
        functools.partial(back_kernel, length, first),
        grid=(count // group,),
        in_specs=[SCALARS, at(group, rows, wide), at(group, rows, width), at(group, rows, width)]
        + ([] if first else [whole(*d) for d in sums] + [pl.BlockSpec(memory_space=pl.ANY)]),
        out_specs=[at(group, rows, wide)]
        + ([whole(*d) for d in sums] if first else [whole(2, c_rows, width)] * 2),
        out_shape=[shape_of(BF16, images, rows, wide)]
        + ([shape_of(F32, *d) for d in sums] if first else [shape_of(BF16, 2, c_rows, width)] * 2),
        scratch_shapes=[] if first else [pltpu.VMEM(d, F32) for d in sums],
        input_output_aliases={} if first else {6: 0},
        compiler_params=PARAMS,
        cost_estimate=cost(1),
        name="back",
    )(index, projected, normed, d_mixed, *more)


def input_gradient(tokens, d_proj, d_middle, w_qkv, vectors):
    images, length, width = tokens.shape
    rows = d_proj.shape[1]
    group = 2 if images % 2 == 0 else 1
    return pl.pallas_call(
        functools.partial(input_kernel, length),
        grid=(images // group,),
        in_specs=[
            per_step(group, length, width),
            per_step(group, rows, 3 * width),
            per_step(group, rows, width),
            *whole_like((w_qkv, vectors)),
        ],
        out_specs=[per_step(group, length, width), whole(8, width)],
        out_shape=[shape_of(BF16, images, length, width), shape_of(F32, 8, width)],
        compiler_params=PARAMS,
        cost_estimate=cost(1),
        name="input_gradient",
    )(tokens, d_proj, d_middle, w_qkv, vectors)


def unpack_outer(index, a_pieces, b_pieces, width, ff):
    half = width // 2
    return pl.pallas_call(
        unpack_outer_kernel,
        grid=(1,),
        in_specs=[SCALARS, *whole_like((*a_pieces, *b_pieces))],
        out_specs=[
            whole(ff // 2, width),
            whole(half, ff),
            whole(half, width),
            *[whole(half)] * 4,
            whole(ff // 2),
        ],
        out_shape=[
            shape_of(F32, ff // 2, width),
            shape_of(F32, half, ff),
            shape_of(F32, half, width),
            *[shape_of(F32, half)] * 4,
            shape_of(F32, ff // 2),
        ],
        scratch_shapes=[
            pltpu.VMEM((2, 2 * a_pieces[0].shape[0], width), F32),
            pltpu.VMEM((2, 2 * b_pieces[0].shape[0], width), F32),
        ],
        compiler_params=PARAMS,
        cost_estimate=cost(3),
        name="unpack_outer",
    )(index, *a_pieces, *b_pieces)


def unpack_inner(index, pieces, late):
    width = late.shape[1]
    half = width // 2
    return pl.pallas_call(
        unpack_inner_kernel,
        grid=(1,),
        in_specs=[SCALARS, *whole_like((*pieces, late))],
        out_specs=[whole(half, 3 * width), *[whole(half)] * 4],
        out_shape=[shape_of(F32, half, 3 * width), *[shape_of(F32, half)] * 4],
        scratch_shapes=[pltpu.VMEM((2, 2 * pieces[0].shape[0], width), F32)],
        compiler_params=PARAMS,
        cost_estimate=cost(2),
        name="unpack_inner",
    )(index, *pieces, late)


AXES = ("rep", "fsdp")


class Butterfly:
    def __init__(self):
        rep, x = lax.axis_index("rep"), lax.axis_index("fsdp")
        self.x, self.core, self.y = x, rep & 1, (rep >> 1) & 1
        self.index = jnp.stack([self.x, self.core, self.y]).astype(jnp.int32)

    def swap(self, v, rep_mask, x_mask=0):
        pairs = [
            (rep * 2 + x, (rep ^ rep_mask) * 2 + (x ^ x_mask)) for rep in range(16) for x in range(2)
        ]
        return lax.ppermute(v, AXES, pairs)

    def over_x(self, v):
        return self.swap(v, 0, 1)

    def over_core(self, v):
        return self.swap(v, 1)

    def over_y(self, v):
        return self.swap(v, 2)

    def over_z(self, v, mask):
        return self.swap(v, 4 * mask)

    def half_of(self, v, which):
        rows = v.shape[-2] // 2
        return lax.dynamic_slice_in_dim(v, which * rows, rows, v.ndim - 2)

    def to_send(self, v):
        return self.half_of(v, 1 - self.y)

    def to_keep(self, v):
        return self.half_of(v, self.y)


class Collective:
    def __init__(self):
        self.index = jnp.zeros((3,), jnp.int32)

    def gather_weight(self, own):
        full = lax.all_gather(own, "fsdp", axis=0, tiled=True)
        quarter = full.shape[0] // 4
        return full[: 2 * quarter], full[2 * quarter : 3 * quarter], full[3 * quarter :]

    def gather_vectors(self, vectors, lift_bias):
        whole_vectors = [lax.all_gather(v, "fsdp", axis=0, tiled=True) for v in vectors]
        whole_bias = lax.all_gather(lift_bias, "fsdp", axis=0, tiled=True)
        width = whole_vectors[0].shape[0]
        table = jnp.stack(whole_vectors).reshape(8, 2, width // 2)
        bias = whole_bias.reshape(2, -1, width)
        return (
            jnp.zeros((2, 8, 3 * width), BF16)
            .at[:, :, : width // 2]
            .set(table.transpose(1, 0, 2))
            .at[:, : bias.shape[1], width : 2 * width]
            .set(bias)
        )

    def reduce(self, v):
        owned = lax.psum_scatter(v.astype(BF16), "fsdp", scatter_dimension=0, tiled=True)
        return lax.psum(owned, "rep").astype(F32)


def after(*arrays):
    return lax.optimization_barrier(arrays)


def assembled(here, there, first, tall, blocks=1, x_first=False):
    middle = (here[1], there[0]) if x_first else (there[0], here[1])
    order = (here[0], *middle, there[1])
    return [
        jnp.concatenate(
            [q[first + k * tall : first + (k + 1) * tall] for k in range(blocks)], axis=1
        )
        for q in order
    ]


def per_device(
    tokens,
    gain_one,
    shift_one,
    qkv_weight,
    query_bias,
    value_bias,
    out_weight,
    out_bias,
    gain_two,
    shift_two,
    lift_weight,
    lift_bias,
    drop_weight,
    drop_bias,
    cotangent,
    swaps,
):
    length, width = tokens.shape[1:]
    plan = Butterfly() if swaps else Collective()
    index = plan.index
    small = (
        gain_one,
        shift_one,
        query_bias,
        value_bias,
        out_bias,
        gain_two,
        shift_two,
        drop_bias,
    )
    ff = lift_weight.shape[1]
    rest = (out_weight, lift_weight, drop_weight)
    if swaps:
        packed = pack_first(index, small, lift_bias, qkv_weight)
        near = plan.over_x(packed)
        qkv = (qkv_weight, near, plan.over_core(near))
        rest_then, packed = after(rest, packed)
        nears = [plan.over_x(half) for half in pack_rest(index, rest_then)]
    else:
        packed, theirs = plan.gather_vectors(small, lift_bias)
        own, near, far = plan.gather_weight(qkv_weight)
        qkv = (own, jnp.concatenate([near, theirs]), far)
    normed, projected, mixed, full_qkv, vectors = forward_attention(
        index, tokens, ff, packed, qkv
    )
    if swaps:
        mixed, nears = after(mixed, nears)
        outer = [
            piece for w, near in zip(rest, nears) for piece in (w, near, plan.over_core(near))
        ]
    else:
        outer = [piece for w in rest for piece in plan.gather_weight(w)]
    middle, result, d_normed, here_a, there_a = mlp_first(
        index, tokens, cotangent, mixed, vectors, ff, outer
    )
    second = functools.partial(
        mlp_second, index, cotangent, mixed, middle, result, d_normed, vectors, ff, outer
    )
    backward = functools.partial(attention_backward, index, projected, normed)
    images = tokens.shape[0]
    some = images // 4 * 2 if images % 4 == 0 else images // 2
    if swaps:
        over_a = plan.over_x(there_a)
        output, d_middle, d_mixed, here_b, there_b = second()
        over_a, here_b, there_b, d_mixed = after(over_a, here_b, there_b, d_mixed)
        sum_a, send_a = here_a[0] + over_a[0], here_a[1] + over_a[1]
        send_a, d_mixed = after(send_a, d_mixed)
        got_a = plan.over_core(send_a)
        got_b = plan.over_core(there_b)
        earlier = backward(d_mixed, length, 0, some)
        earlier, got_a, got_b = after(earlier, got_a, got_b)
        mine_a, other_b = sum_a + got_a, here_b[1] + got_b[1]
        earlier, other_a, mine_a, other_b = after(earlier, plan.to_send(mine_a), mine_a, other_b)
        over_a, over_b = plan.over_y(other_a), plan.over_x(other_b)
        d_proj, here_c, there_c = backward(
            d_mixed, length, some, images - some, (earlier[1], earlier[2], earlier[0])
        )
        here_c, there_c, over_a = after(here_c, there_c, over_a)
        got_c = plan.over_core(there_c)
        part_a = plan.to_keep(mine_a) + over_a
        part_a, over_b, got_c = after(part_a, over_b, got_c)
        other_c = here_c[1] + got_c[1]
        mine_b = here_b[0] + got_b[0] + over_b
        d_proj, part_a, other_b, mine_b, other_c = after(
            d_proj, part_a, plan.to_send(mine_b), mine_b, other_c
        )
        over_c, over_a, over_b = plan.over_x(other_c), plan.over_z(part_a, 1), plan.over_y(other_b)
        input_grad, late = input_gradient(tokens, d_proj, d_middle, full_qkv, vectors)
        late, over_c, over_a, over_b = after(late, over_c, over_a, over_b)
        mine_c = here_c[0] + got_c[0] + over_c
        other_c, mine_c, late = after(plan.to_send(mine_c), mine_c, late)
        over_c, more = plan.over_y(other_c), plan.over_core(late)
        part_a, part_b = part_a + over_a, plan.to_keep(mine_b) + over_b
        over_c, more, part_a, part_b = after(over_c, more, part_a, part_b)
        over_a = plan.over_z(part_a, 2)
        part_c, late = plan.to_keep(mine_c) + over_c, late + more
        part_c, late = after(part_c, late)
        over_c, more, over_b = plan.over_z(part_c, 1), plan.over_x(late), plan.over_z(part_b, 1)
        over_c, more, over_a = after(over_c, more, over_a)
        part_c, late, part_a = part_c + over_c, late + more, part_a + over_a
        part_c, late, part_a = after(part_c, late, part_a)
        over_c, more = plan.over_z(part_c, 2), plan.over_y(late)
        across_a, beside_a = plan.over_y(part_a), plan.over_core(part_a)
        part_b = part_b + over_b
        over_c, more, part_b = after(over_c, more, part_b)
        over_b = plan.over_z(part_b, 2)
        part_c, late = part_c + over_c, late + more
        part_c, late, across_a = after(part_c, late, across_a)
        across_c, beside_c, more = plan.over_y(part_c), plan.over_core(part_c), plan.over_z(late, 1)
        a_pieces = (part_a, across_a, beside_a, plan.over_core(across_a))
        across_c, more, over_b = after(across_c, more, over_b)
        part_b, late = part_b + over_b, late + more
        part_b, late, across_c = after(part_b, late, across_c)
        across_b, beside_b, more = plan.over_y(part_b), plan.over_core(part_b), plan.over_z(late, 2)
        c_pieces = (part_c, across_c, beside_c, plan.over_core(across_c))
        late = late + more
        g_qkv, g_query, g_value, g_gain_one, g_shift_one = unpack_inner(index, c_pieces, late)
        across_b, g_qkv = after(across_b, g_qkv)
        b_pieces = (part_b, across_b, beside_b, plan.over_core(across_b))
        g_drop, g_lift, g_out, g_out_bias, g_gain_two, g_shift_two, g_drop_bias, g_lift_bias = (
            unpack_outer(index, a_pieces, b_pieces, width, ff)
        )
    else:
        output, d_middle, d_mixed, here_b, there_b = second()
        earlier = backward(d_mixed, length, 0, some)
        d_proj, here_c, there_c = backward(
            d_mixed, length, some, images - some, (earlier[1], earlier[2], earlier[0])
        )
        input_grad, late = input_gradient(tokens, d_proj, d_middle, full_qkv, vectors)
        deep, tall = width // 2, width // 4
        drop_a, drop_b = assembled(here_a, there_a, 0, deep, 1, True), assembled(here_b, there_b, 0, deep)
        g_drop = plan.reduce(
            jnp.concatenate([*drop_a[:2], *drop_b[:2], *drop_a[2:], *drop_b[2:]])
        )
        lift_a = jnp.concatenate(assembled(here_a, there_a, deep, tall, 2, True))
        lift_b = jnp.concatenate(assembled(here_b, there_b, deep, tall, 2))
        g_lift = plan.reduce(
            jnp.stack(
                [lift_a.reshape(width, 2, width), lift_b.reshape(width, 2, width)], axis=2
            ).reshape(width, ff)
        )
        g_out = plan.reduce(jnp.concatenate(assembled(here_b, there_b, width + VEC_ROWS, tall)))
        g_qkv = plan.reduce(jnp.concatenate(assembled(here_c, there_c, 0, tall, 3)))
        rows_a, rows_b, rows_c = here_a[0, width:], here_b[0, width:], here_c[0, 3 * tall :]
        g_out_bias, g_gain_two, g_shift_two, g_drop_bias = (
            plan.reduce(rows_b[2 + i]) for i in range(4)
        )
        g_lift_bias = plan.reduce(jnp.concatenate([rows_a[0], rows_b[0], rows_a[1], rows_b[1]]))
        g_query, g_value = plan.reduce(rows_c[0]), plan.reduce(rows_c[1])
        g_gain_one, g_shift_one = plan.reduce(late[0]), plan.reduce(late[1])
    return (
        output,
        input_grad,
        g_gain_one,
        g_shift_one,
        g_qkv,
        g_query,
        g_value,
        g_out,
        g_out_bias,
        g_gain_two,
        g_shift_two,
        g_lift,
        g_lift_bias,
        g_drop,
        g_drop_bias,
    )


def solution(mesh):
    spread = P(("rep", "fsdp"), None, None)
    vector, matrix = P("fsdp"), P("fsdp", None)
    in_specs = (
        spread,
        vector,
        vector,
        matrix,
        vector,
        vector,
        matrix,
        vector,
        vector,
        vector,
        matrix,
        vector,
        matrix,
        vector,
        spread,
    )
    out_specs = (
        spread,
        spread,
        vector,
        vector,
        matrix,
        vector,
        vector,
        matrix,
        vector,
        vector,
        vector,
        matrix,
        vector,
        matrix,
        vector,
    )
    swaps = mesh.shape["rep"] == 16 and mesh.shape["fsdp"] == 2
    return jax.shard_map(
        functools.partial(per_device, swaps=swaps),
        mesh=mesh,
        in_specs=in_specs,
        out_specs=out_specs,
        check_vma=False,
    )
```

```python
import functools

import jax
import jax.numpy as jnp
from jax import lax
from jax.experimental import pallas as pl
from jax.experimental.pallas import tpu as pltpu
from jax.sharding import PartitionSpec as P

HEADS = 6
HEAD_DIM = 64
PAIR = 2 * HEAD_DIM
LANE = 128
EPS = 1e-06
ROOT_HALF = 0.7071067811865476
GAUSS = 0.3989422804014327
LOG2E = 1.4426950408889634
SCALE = HEAD_DIM ** (-0.5)
F32 = jnp.float32
BF16 = jnp.bfloat16


def nn(a, b):
    return lax.dot_general(a, b, (((1,), (0,)), ((), ())), preferred_element_type=F32)


def nt(a, b):
    return lax.dot_general(a, b, (((1,), (1,)), ((), ())), preferred_element_type=F32)


def tn(a, b):
    return lax.dot_general(a, b, (((0,), (0,)), ((), ())), preferred_element_type=F32)


def normalise(v):
    mean = jnp.mean(v, axis=-1, keepdims=True)
    centred = v - mean
    var = jnp.mean(centred * centred, axis=-1, keepdims=True)
    inverse = lax.rsqrt(var + EPS)
    return centred * inverse, inverse


def norm_back(grad, normal, inverse, gain):
    scaled = grad * gain
    return inverse * (
        scaled
        - jnp.mean(scaled, axis=-1, keepdims=True)
        - normal * jnp.mean(scaled * normal, axis=-1, keepdims=True)
    )


def fold(v):
    return jnp.sum(v.reshape(v.shape[0] // 8, 8, v.shape[1]), axis=0)


def pad_rows(scratch, ref, length):
    for j in range(ref.shape[0]):
        scratch[j, 0:length, :] = ref[j].astype(scratch.dtype)


def zero_tail(scratch, length):
    images, rows, columns = scratch.shape
    low = (length // 16) * 16
    scratch[:, low:rows, :] = jnp.zeros((images, rows - low, columns), scratch.dtype)


def split_pair(v):
    first = lax.broadcasted_iota(jnp.int32, v.shape, 1) < HEAD_DIM
    zero = jnp.zeros_like(v)
    return jnp.concatenate([jnp.where(first, v, zero), jnp.where(first, zero, v)], axis=0)


def join_pair(v):
    rows = v.shape[0] // 2
    first = lax.broadcasted_iota(jnp.int32, (rows, PAIR), 1) < HEAD_DIM
    return jnp.where(first, v[:rows], v[rows:])


def join_pieces(full, own, near, far, index):
    block = own.shape[0]
    half = block // 2
    x, core = index[0], index[1]
    other = (1 - x) * block
    full[pl.ds(pl.multiple_of(x * block, 16), block), :] = own[...]
    full[pl.ds(pl.multiple_of(other + core * half, 16), half), :] = near[0:half, :]
    full[pl.ds(pl.multiple_of(other + (1 - core) * half, 16), half), :] = far[0:half, :]


def quarters(index, keep, send):
    x, core, y = index[0], index[1], index[2]
    for dest, owner in ((keep, core), (send, 1 - core)):
        for slot, half in ((0, x), (1, 1 - x)):
            for side in range(2):
                yield dest.at[slot, jnp.where(y == side, 0, 1)], half, owner, side


def pack_first_kernel(index, *refs):
    vectors, lift_bias, weight, packed = refs[:8], *refs[8:]
    half = weight.shape[0] // 2
    shard, width = vectors[0].shape[0], weight.shape[1] // 3
    packed[0:half, :] = weight[pl.ds(pl.multiple_of(index[1] * half, 16), half), :]
    packed[half:, :] = jnp.zeros((8, 3 * width), BF16)
    for i, ref in enumerate(vectors):
        row = ref[...].astype(F32).reshape(1, shard)
        packed[half + i : half + i + 1, 0:shard] = row.astype(BF16)
    bias = lift_bias[...].astype(F32).reshape(1, lift_bias.shape[0]).astype(BF16)
    for k in range(lift_bias.shape[0] // width):
        packed[half + k : half + k + 1, width : 2 * width] = bias[:, k * width : (k + 1) * width]


def pack_rest_kernel(index, *refs):
    for weight, half_out in zip(refs[:3], refs[3:]):
        half = half_out.shape[0]
        half_out[...] = weight[pl.ds(pl.multiple_of(index[1] * half, 16), half), :]


def join_vectors(vec_ref, own, other, index):
    width = vec_ref.shape[1]
    half = width // 2
    mine, theirs = own[-8:, :].astype(F32), other[-8:, :].astype(F32)
    first = index[0] == 0
    low, high = jnp.where(first, mine, theirs), jnp.where(first, theirs, mine)
    vec_ref[0:8, :] = jnp.concatenate([low[:, :half], high[:, :half]], axis=1)
    blocks = vec_ref.shape[0] // 2 - 4
    vec_ref[8 : 8 + blocks, :] = low[:blocks, width : 2 * width]
    vec_ref[8 + blocks :, :] = high[:blocks, width : 2 * width]


def attend_kernel(
    length,
    index,
    tok_ref,
    packed,
    own,
    near,
    far,
    normed_ref,
    proj_ref,
    mixed_ref,
    w_ref,
    vec_ref,
    n_s,
):
    images, rows, width = n_s.shape

    @pl.when(pl.program_id(0) == 0)
    def _():
        zero_tail(n_s, length)
        join_pieces(w_ref, own, near, far, index)
        join_vectors(vec_ref, packed, near, index)

    gain, shift = vec_ref[0:1, :], vec_ref[1:2, :]
    bias = jnp.concatenate([vec_ref[2:3, :], jnp.zeros((1, width), F32), vec_ref[3:4, :]], axis=1)
    for j in range(images):
        normal, _ = normalise(tok_ref[j].astype(F32))
        n_s[j, 0:length, :] = (normal * gain + shift).astype(BF16)
    normed_ref[...] = n_s[...]
    flat = n_s[...].reshape(images * rows, width)
    proj_ref[...] = (nn(flat, w_ref[...]) + bias).astype(BF16).reshape(images, rows, 3 * width)
    live = lax.broadcasted_iota(jnp.int32, (2 * rows, rows), 1) < length
    ones = jnp.ones((rows, PAIR), BF16)
    for j in range(images):
        for c in range(0, width, PAIR):
            query = split_pair(proj_ref[j, :, c : c + PAIR] * jnp.asarray(SCALE, BF16))
            key = proj_ref[j, :, width + c : width + c + PAIR]
            value = proj_ref[j, :, 2 * width + c : 2 * width + c + PAIR]
            scores = jnp.where(live, nt(query, key), -1e30)
            top = jnp.max(scores, axis=-1, keepdims=True)
            weights = jnp.exp(scores - top).astype(BF16)
            both = nn(weights, jnp.concatenate([value, ones], axis=1))
            mixed_ref[j, :, c : c + PAIR] = join_pair(both[:, :PAIR] / both[:, PAIR:]).astype(BF16)


def mlp_kernel(
    length,
    chunk,
    index,
    tok_ref,
    cot_ref,
    mixed_ref,
    vec_ref,
    out_own,
    out_near,
    out_far,
    lift_own,
    lift_near,
    lift_far,
    drop_own,
    drop_near,
    drop_far,
    out_ref,
    d_middle_ref,
    d_mixed_ref,
    keep,
    send,
    x_s,
    z_s,
    w_out_ref,
    w_lift_ref,
    w_drop_ref,
    lift_bias_ref,
    a_drop,
    a_lift,
    a_out,
    a_vec,
    a_bias,
):
    step = pl.program_id(0)
    images, rows, width = x_s.shape
    total = images * rows
    hidden_width = w_lift_ref.shape[1]

    @pl.when(step == 0)
    def _():
        zero_tail(x_s, length)
        zero_tail(z_s, length)
        join_pieces(w_out_ref, out_own, out_near, out_far, index)
        join_pieces(w_lift_ref, lift_own, lift_near, lift_far, index)
        join_pieces(w_drop_ref, drop_own, drop_near, drop_far, index)
        for k in range(hidden_width // width):
            lift_bias_ref[:, k * width : (k + 1) * width] = vec_ref[8 + k : 9 + k, :]
        for acc in (a_drop, a_lift, a_out, a_vec, a_bias):
            acc[...] = jnp.zeros_like(acc)

    pad_rows(x_s, tok_ref, length)
    pad_rows(z_s, cot_ref, length)
    out_bias, gain, shift, drop_bias = (vec_ref[i : i + 1, :] for i in range(4, 8))
    mixed = mixed_ref[...].reshape(total, width)
    dz = z_s[...].reshape(total, width)
    dz_f = dz.astype(F32)
    middle = x_s[...].reshape(total, width).astype(F32) + nn(mixed, w_out_ref[...]) + out_bias
    normal, inverse = normalise(middle)
    normed = (normal * gain + shift).astype(BF16)
    result = middle + drop_bias
    d_normed = jnp.zeros((total, width), F32)
    for c in range(0, hidden_width, chunk):
        part = slice(c, c + chunk)
        hidden = nn(normed, w_lift_ref[:, part]) + lift_bias_ref[:, part]
        cdf = 0.5 + 0.5 * lax.erf(hidden * ROOT_HALF)
        bell = jnp.exp(hidden * hidden * -0.5) * GAUSS
        active = (hidden * cdf).astype(BF16)
        d_active = nt(dz, w_drop_ref[part, :])
        d_hidden_f = d_active * (cdf + hidden * bell)
        d_hidden = d_hidden_f.astype(BF16)
        result = result + nn(active, w_drop_ref[part, :])
        d_normed = d_normed + nt(d_hidden, w_lift_ref[:, part])
        a_drop[part, :] += tn(active, dz)
        a_lift[:, part] += tn(normed, d_hidden)
        a_bias[:, part] += fold(d_hidden.astype(F32))
    out = result.astype(BF16)
    for j in range(images):
        out_ref[j] = out[j * rows : j * rows + length]
    d_middle = dz_f + norm_back(d_normed, normal, inverse, gain)
    d_middle_ref[...] = d_middle.reshape(images, rows, width)
    d_attended = d_middle.astype(BF16)
    d_mixed_ref[...] = nt(d_attended, w_out_ref[...]).astype(BF16).reshape(images, rows, width)
    a_out[...] += tn(mixed, d_attended)
    a_vec[0] += fold(d_attended.astype(F32))
    a_vec[1] += fold(d_normed * normal)
    a_vec[2] += fold(d_normed)
    a_vec[3] += fold(dz_f)

    @pl.when(step == pl.num_programs(0) - 1)
    def _():
        columns = jnp.sum(a_bias[...], axis=0, keepdims=True)
        vectors = jnp.concatenate(
            [jnp.sum(a_vec[...], axis=1)]
            + [columns[:, c : c + width] for c in range(0, hidden_width, width)],
            axis=0,
        ).astype(BF16)
        deep, tall, small = hidden_width // 4, width // 4, width // 8
        for place, half, core, side in quarters(index, keep, send):
            quarter = 2 * half + core
            if side == 0:
                first = pl.multiple_of(quarter * deep, 8)
                place[0:deep, :] = a_drop[pl.ds(first, deep), :].astype(BF16)
                place[deep + small :, :] = vectors
            else:
                rows_of = pl.ds(pl.multiple_of(quarter * tall, 8), tall)
                for k in range(hidden_width // width):
                    place[k * tall : (k + 1) * tall, :] = a_lift[
                        rows_of, k * width : (k + 1) * width
                    ].astype(BF16)
                place[deep + small :, :] = jnp.zeros((8, width), BF16)
            first = pl.multiple_of(quarter * tall + side * small, 8)
            place[deep : deep + small, :] = a_out[pl.ds(first, small), :].astype(BF16)


def back_kernel(
    length, first, last, index, tok_ref, proj_ref, normed_ref, d_mixed_ref, d_middle_ref, w_ref, vec_ref, *refs
):
    if not first:
        old, refs = refs[:3], refs[4:]
    in_grad_ref = refs[0]
    if last:
        keep, send = refs[1:3]
        sums, d_s = refs[3:6], refs[6]
    else:
        sums, d_s = refs[1:4], refs[4]
    a_qkv, a_proj, a_vec = sums
    images, rows, wide = d_s.shape
    width = wide // 3
    total = images * rows

    @pl.when(pl.program_id(0) == 0)
    def _():
        for i, acc in enumerate(sums):
            acc[...] = jnp.zeros_like(acc) if first else old[i][...]

    live = lax.broadcasted_iota(jnp.int32, (rows, 2 * rows), 0) < length
    for j in range(images):
        for c in range(0, width, PAIR):
            query = split_pair(proj_ref[j, :, c : c + PAIR] * jnp.asarray(SCALE, BF16))
            key = proj_ref[j, :, width + c : width + c + PAIR]
            value = proj_ref[j, :, 2 * width + c : 2 * width + c + PAIR]
            d_mixed = split_pair(d_mixed_ref[j, :, c : c + PAIR])
            scores = jnp.where(live, nt(key, query), -1e30)
            top = jnp.max(scores, axis=0, keepdims=True)
            weights = jnp.exp(scores - top)
            probs = weights * (1.0 / jnp.sum(weights, axis=0, keepdims=True))
            d_probs = nt(value, d_mixed)
            delta = jnp.sum(probs * d_probs, axis=0, keepdims=True)
            d_scores = (probs * (d_probs - delta)).astype(BF16)
            d_value = nn(probs.astype(BF16), d_mixed)
            d_key = nn(d_scores, query)
            d_query = join_pair(tn(d_scores, key)) * SCALE
            d_s[j, :, c : c + PAIR] = d_query.astype(BF16)
            d_s[j, :, width + c : width + c + PAIR] = d_key.astype(BF16)
            d_s[j, :, 2 * width + c : 2 * width + c + PAIR] = d_value.astype(BF16)
    d_proj = d_s[...].reshape(total, wide)
    a_qkv[...] += tn(normed_ref[...].reshape(total, width), d_proj)
    a_proj[...] += fold(d_proj.astype(F32))
    d_normed = nt(d_proj, w_ref[...])
    gain = vec_ref[0:1, :]
    for j in range(images):
        normal, inverse = normalise(tok_ref[j].astype(F32))
        grad = d_normed[j * rows : j * rows + length]
        in_grad_ref[j] = (
            d_middle_ref[j, 0:length, :] + norm_back(grad, normal, inverse, gain)
        ).astype(BF16)
        a_vec[0:1, :] += jnp.sum(grad * normal, axis=0, keepdims=True)
        a_vec[1:2, :] += jnp.sum(grad, axis=0, keepdims=True)
    if not last:
        return

    @pl.when(pl.program_id(0) == pl.num_programs(0) - 1)
    def _():
        columns = jnp.sum(a_proj[...], axis=0, keepdims=True)
        vectors = jnp.concatenate(
            [columns[:, :width], columns[:, 2 * width :], a_vec[...], jnp.zeros((4, width), F32)],
            axis=0,
        ).astype(BF16)
        small = width // 8
        for place, half, core, side in quarters(index, keep, send):
            first_row = pl.multiple_of((2 * half + core) * 2 * small + side * small, 8)
            for k in range(3):
                place[k * small : (k + 1) * small, :] = a_qkv[
                    pl.ds(first_row, small), k * width : (k + 1) * width
                ].astype(BF16)
            place[3 * small :, :] = vectors


def placed(full, index, pieces):
    core, y = index[1], index[2]
    spots = ((core, y), (core, 1 - y), (1 - core, y), (1 - core, 1 - y))
    for (owner, side), piece in zip(spots, pieces):
        full[owner, side] = piece[...].astype(F32)


def own_half(index, row):
    half = row.shape[-1] // 2
    return jnp.where(index[0] == 0, row[:, :half], row[:, half:])[0]


def unpack_outer_kernel(index, *refs):
    g_drop, g_lift, g_out, g_out_bias, g_gain, g_shift, g_drop_bias, g_lift_bias, full = refs[4:]
    placed(full, index, refs[0:4])
    width = g_out.shape[1]
    deep, tall, small = g_drop.shape[0] // 2, width // 4, width // 8
    blocks = g_lift.shape[1] // width
    for core in range(2):
        g_drop[core * deep : (core + 1) * deep, :] = full[core, 0, 0:deep, :]
        for k in range(blocks):
            g_lift[core * tall : (core + 1) * tall, k * width : (k + 1) * width] = full[
                core, 1, k * tall : (k + 1) * tall, :
            ]
        for side in range(2):
            first = core * tall + side * small
            g_out[first : first + small, :] = full[core, side, deep : deep + small, :]
    vectors = full[0, 0, deep + small :, :]
    for i, ref in enumerate((g_out_bias, g_gain, g_shift, g_drop_bias)):
        ref[...] = own_half(index, vectors[i : i + 1, :])
    for k in range(blocks // 2):
        row = jnp.where(
            index[0] == 0,
            vectors[4 + k : 5 + k, :],
            vectors[4 + blocks // 2 + k : 5 + blocks // 2 + k, :],
        )
        g_lift_bias[k * width : (k + 1) * width] = row[0]


def unpack_inner_kernel(index, *refs):
    g_qkv, g_query, g_value, g_gain, g_shift, full = refs[4:]
    placed(full, index, refs[0:4])
    width = full.shape[3]
    small = width // 8
    for core in range(2):
        for side in range(2):
            first = (2 * core + side) * small
            for k in range(3):
                g_qkv[first : first + small, k * width : (k + 1) * width] = full[
                    core, side, k * small : (k + 1) * small, :
                ]
    vectors = full[0, 0, 3 * small :, :]
    for i, ref in enumerate((g_query, g_value, g_gain, g_shift)):
        ref[...] = own_half(index, vectors[i : i + 1, :])


VMEM_LIMIT = 60 * 1024 * 1024
PARAMS = pltpu.CompilerParams(vmem_limit_bytes=VMEM_LIMIT)
SCALARS = pl.BlockSpec(memory_space=pltpu.SMEM)


def whole(*shape):
    return pl.BlockSpec(shape, lambda i: (0,) * len(shape))


def whole_like(arrays):
    return [whole(*a.shape) for a in arrays]


def per_step(*shape):
    return pl.BlockSpec(shape, lambda i: (i,) + (0,) * (len(shape) - 1))


def shape_of(dtype, *shape):
    return jax.ShapeDtypeStruct(shape, dtype)


def cost(microseconds):
    return pl.CostEstimate(flops=int(microseconds * 1e3), bytes_accessed=1, transcendentals=0)


def pack_first(index, vectors, lift_bias, weight):
    rows, columns = weight.shape
    return pl.pallas_call(
        pack_first_kernel,
        grid=(1,),
        in_specs=[SCALARS, *whole_like((*vectors, lift_bias, weight))],
        out_specs=whole(rows // 2 + 8, columns),
        out_shape=shape_of(BF16, rows // 2 + 8, columns),
        compiler_params=PARAMS,
        cost_estimate=cost(1),
        name="pack_first",
    )(index, *vectors, lift_bias, weight)


def pack_rest(index, weights):
    return pl.pallas_call(
        pack_rest_kernel,
        grid=(1,),
        in_specs=[SCALARS, *whole_like(weights)],
        out_specs=[whole(w.shape[0] // 2, w.shape[1]) for w in weights],
        out_shape=[shape_of(BF16, w.shape[0] // 2, w.shape[1]) for w in weights],
        compiler_params=PARAMS,
        cost_estimate=cost(1),
        name="pack_rest",
    )(index, *weights)


def forward_attention(index, tokens, ff, packed, pieces):
    images, length, width = tokens.shape
    rows = -(-length // 16) * 16
    group = 4 if images % 4 == 0 else 1
    return pl.pallas_call(
        functools.partial(attend_kernel, length),
        grid=(images // group,),
        in_specs=[SCALARS, per_step(group, length, width), *whole_like((packed, *pieces))],
        out_specs=[
            per_step(group, rows, width),
            per_step(group, rows, 3 * width),
            per_step(group, rows, width),
            whole(width, 3 * width),
            whole(8 + ff // width, width),
        ],
        out_shape=[
            shape_of(BF16, images, rows, width),
            shape_of(BF16, images, rows, 3 * width),
            shape_of(BF16, images, rows, width),
            shape_of(BF16, width, 3 * width),
            shape_of(F32, 8 + ff // width, width),
        ],
        scratch_shapes=[pltpu.VMEM((group, rows, width), BF16)],
        compiler_params=PARAMS,
        cost_estimate=cost(1),
        name="attend",
    )(index, tokens, packed, *pieces)


def mlp_both_ways(index, tokens, cotangent, mixed, vectors, ff, pieces):
    images, length, width = tokens.shape
    rows = mixed.shape[1]
    group = 2 if images % 2 == 0 else 1
    eighth = (2, 2, ff // 4 + width // 8 + 8, width)
    return pl.pallas_call(
        functools.partial(mlp_kernel, length, 512),
        grid=(images // group,),
        in_specs=[
            SCALARS,
            per_step(group, length, width),
            per_step(group, length, width),
            per_step(group, rows, width),
            *whole_like((vectors, *pieces)),
        ],
        out_specs=[
            per_step(group, length, width),
            per_step(group, rows, width),
            per_step(group, rows, width),
            whole(*eighth),
            whole(*eighth),
        ],
        out_shape=[
            shape_of(BF16, images, length, width),
            shape_of(F32, images, rows, width),
            shape_of(BF16, images, rows, width),
            shape_of(BF16, *eighth),
            shape_of(BF16, *eighth),
        ],
        scratch_shapes=[
            pltpu.VMEM((group, rows, width), BF16),
            pltpu.VMEM((group, rows, width), BF16),
            pltpu.VMEM((width, width), BF16),
            pltpu.VMEM((width, ff), BF16),
            pltpu.VMEM((ff, width), BF16),
            pltpu.VMEM((1, ff), F32),
            pltpu.VMEM((ff, width), F32),
            pltpu.VMEM((width, ff), F32),
            pltpu.VMEM((width, width), F32),
            pltpu.VMEM((4, 8, width), F32),
            pltpu.VMEM((8, ff), F32),
        ],
        compiler_params=PARAMS,
        cost_estimate=cost(1),
        name="mlp",
    )(index, tokens, cotangent, mixed, vectors, *pieces)


def attention_backward(
    index, tokens, projected, normed, w_qkv, vectors, d_mixed, d_middle, start, stop, earlier=()
):
    images, length, width = tokens.shape
    rows = normed.shape[1]
    wide = 3 * width
    group = 2 if images % 2 == 0 else 1
    offset = start // group
    first, last = not earlier, stop == images
    chunk = (2, 2, 3 * width // 8 + 8, width)
    sums = [(width, wide), (8, wide), (2, width)]

    def at(*shape):
        return pl.BlockSpec((group,) + shape, lambda i: (i + offset if offset else i, 0, 0))

    return pl.pallas_call(
        functools.partial(back_kernel, length, first, last),
        grid=((stop - start) // group,),
        in_specs=[
            SCALARS,
            at(length, width),
            at(rows, wide),
            at(rows, width),
            at(rows, width),
            at(rows, width),
            *whole_like((w_qkv, vectors)),
        ]
        + ([] if first else [whole(*d) for d in sums] + [pl.BlockSpec(memory_space=pl.ANY)]),
        out_specs=[at(length, width)]
        + ([whole(*chunk)] * 2 if last else [whole(*d) for d in sums]),
        out_shape=[shape_of(BF16, images, length, width)]
        + ([shape_of(BF16, *chunk)] * 2 if last else [shape_of(F32, *d) for d in sums]),
        scratch_shapes=([pltpu.VMEM(d, F32) for d in sums] if last else [])
        + [pltpu.VMEM((group, rows, wide), BF16)],
        input_output_aliases={} if first else {11: 0},
        compiler_params=PARAMS,
        cost_estimate=cost(1),
        name="back",
    )(index, tokens, projected, normed, d_mixed, d_middle, w_qkv, vectors, *earlier)


def unpack(kernel, index, pieces, shapes, name):
    return pl.pallas_call(
        kernel,
        grid=(1,),
        in_specs=[SCALARS, *whole_like(pieces)],
        out_specs=[whole(*d) for d in shapes],
        out_shape=[shape_of(F32, *d) for d in shapes],
        scratch_shapes=[pltpu.VMEM((2, 2) + pieces[0].shape, F32)],
        compiler_params=PARAMS,
        cost_estimate=cost(1),
        name=name,
    )(index, *pieces)


AXES = ("rep", "fsdp")


class Butterfly:
    def __init__(self):
        rep, x = lax.axis_index("rep"), lax.axis_index("fsdp")
        self.x, self.core, self.y = x, rep & 1, (rep >> 1) & 1
        self.index = jnp.stack([self.x, self.core, self.y]).astype(jnp.int32)

    def swap(self, v, rep_mask, x_mask=0):
        pairs = [
            (rep * 2 + x, (rep ^ rep_mask) * 2 + (x ^ x_mask)) for rep in range(16) for x in range(2)
        ]
        return lax.ppermute(v, AXES, pairs)

    def over_x(self, v):
        return self.swap(v, 0, 1)

    def over_core(self, v):
        return self.swap(v, 1)

    def over_y(self, v):
        return self.swap(v, 2)

    def over_z(self, v, mask):
        return self.swap(v, 4 * mask)

    def over_corner(self, v):
        return self.swap(v, 2, 1)

    def over_y_and_core(self, v):
        return self.swap(v, 3)

    def scatter(self, keep, got):
        total = [[keep[i, j] + got[i, j] for j in range(2)] for i in range(2)]
        return (total[1][0], total[0][1], total[1][1]), total[0][0]

    def send(self, parts):
        return self.over_x(parts[0]), self.over_y(parts[1]), self.over_corner(parts[2])


class Collective:
    def __init__(self):
        self.index = jnp.zeros((3,), jnp.int32)

    def gather_weight(self, own):
        full = lax.all_gather(own, "fsdp", axis=0, tiled=True)
        quarter = full.shape[0] // 4
        return full[: 2 * quarter], full[2 * quarter : 3 * quarter], full[3 * quarter :]

    def gather_vectors(self, vectors, lift_bias):
        whole_vectors = [lax.all_gather(v, "fsdp", axis=0, tiled=True) for v in vectors]
        whole_bias = lax.all_gather(lift_bias, "fsdp", axis=0, tiled=True)
        width = whole_vectors[0].shape[0]
        table = jnp.stack(whole_vectors).reshape(8, 2, width // 2)
        bias = whole_bias.reshape(2, -1, width)
        return (
            jnp.zeros((2, 8, 3 * width), BF16)
            .at[:, :, : width // 2]
            .set(table.transpose(1, 0, 2))
            .at[:, : bias.shape[1], width : 2 * width]
            .set(bias)
        )

    def reduce(self, v):
        owned = lax.psum_scatter(v.astype(BF16), "fsdp", scatter_dimension=0, tiled=True)
        return lax.psum(owned, "rep").astype(F32)


def after(*arrays):
    return lax.optimization_barrier(arrays)


def in_order(keep, send):
    return [(q[0], q[1]) for q in (keep[0], send[0], keep[1], send[1])]


def per_device(
    tokens,
    gain_one,
    shift_one,
    qkv_weight,
    query_bias,
    value_bias,
    out_weight,
    out_bias,
    gain_two,
    shift_two,
    lift_weight,
    lift_bias,
    drop_weight,
    drop_bias,
    cotangent,
    swaps,
):
    length, width = tokens.shape[1:]
    plan = Butterfly() if swaps else Collective()
    index = plan.index
    small = (
        gain_one,
        shift_one,
        query_bias,
        value_bias,
        out_bias,
        gain_two,
        shift_two,
        drop_bias,
    )
    ff = lift_weight.shape[1]
    rest = (out_weight, lift_weight, drop_weight)
    if swaps:
        packed = pack_first(index, small, lift_bias, qkv_weight)
        near = plan.over_x(packed)
        qkv = (qkv_weight, near, plan.over_core(near))
        rest_then, packed = after(rest, packed)
        nears = [plan.over_x(half) for half in pack_rest(index, rest_then)]
    else:
        packed, theirs = plan.gather_vectors(small, lift_bias)
        own, near, far = plan.gather_weight(qkv_weight)
        qkv = (own, jnp.concatenate([near, theirs]), far)
    normed, projected, mixed, full_qkv, vectors = forward_attention(
        index, tokens, ff, packed, qkv
    )
    if swaps:
        mixed, nears = after(mixed, nears)
        outer = [
            piece for w, near in zip(rest, nears) for piece in (w, near, plan.over_core(near))
        ]
    else:
        outer = [piece for w in rest for piece in plan.gather_weight(w)]
    output, d_middle, d_mixed, keep_a, send_a = mlp_both_ways(
        index, tokens, cotangent, mixed, vectors, ff, outer
    )
    backward = functools.partial(
        attention_backward, index, tokens, projected, normed, full_qkv, vectors
    )
    images, half = tokens.shape[0], width // 2
    if swaps:
        got_a = plan.over_core(send_a)
        input_grad, *sums = backward(d_mixed, d_middle, 0, 2)
        sums, got_a = after(sums, got_a)
        parts_a, stay_a = plan.scatter(keep_a, got_a)
        sums, parts_a = after(sums, parts_a)
        more_a = plan.send(parts_a)
        input_grad, keep_c, send_c = backward(
            d_mixed, d_middle, 2, images, (*sums, input_grad)
        )
        send_c, more_a = after(send_c, more_a)
        got_c = plan.over_core(send_c)
        sum_a = stay_a + more_a[0] + more_a[1] + more_a[2]
        over_a = plan.over_z(sum_a, 1)
        got_c, sum_a = after(got_c, sum_a)
        parts_c, stay_c = plan.scatter(keep_c, got_c)
        parts_c = after(*parts_c)
        more_c = plan.send(parts_c)
        more_c, over_a = after(more_c, over_a)
        sum_c = stay_c + more_c[0] + more_c[1] + more_c[2]
        sum_a = sum_a + over_a
        sum_c, sum_a = after(sum_c, sum_a)
        over_c, over_a = plan.over_z(sum_c, 1), plan.over_z(sum_a, 2)
        sum_c = sum_c + over_c
        over_c = plan.over_z(sum_c, 2)
        over_c, over_a = after(over_c, over_a)
        sum_c, sum_a = sum_c + over_c, sum_a + over_a
        sum_c, sum_a = after(sum_c, sum_a)
        pieces_c = (sum_c, plan.over_y(sum_c), plan.over_core(sum_c), plan.over_y_and_core(sum_c))
        across_a, beside_a = plan.over_y(sum_a), plan.over_core(sum_a)
        pieces_c, beside_a = after(pieces_c, beside_a)
    else:
        input_grad, *sums = backward(d_mixed, d_middle, 0, images - 2)
        input_grad, keep_c, send_c = backward(
            d_mixed, d_middle, images - 2, images, (*sums, input_grad)
        )
        deep, tall, small = ff // 4, width // 4, width // 8
        eighths = in_order(keep_a, send_a)
        g_drop = plan.reduce(jnp.concatenate([q[0][:deep] for q in eighths]))
        g_lift = plan.reduce(
            jnp.concatenate(
                [
                    jnp.concatenate(
                        [q[1][k * tall : (k + 1) * tall] for k in range(ff // width)], axis=1
                    )
                    for q in eighths
                ]
            )
        )
        g_out = plan.reduce(
            jnp.concatenate([side[deep : deep + small] for q in eighths for side in q])
        )
        rows = eighths[0][0][deep + small :]
        g_out_bias, g_gain_two, g_shift_two, g_drop_bias = (plan.reduce(rows[i]) for i in range(4))
        g_lift_bias = plan.reduce(rows[4:].reshape(-1))
        eighths = in_order(keep_c, send_c)
        g_qkv = plan.reduce(
            jnp.concatenate(
                [
                    jnp.concatenate([side[k * small : (k + 1) * small] for k in range(3)], axis=1)
                    for q in eighths
                    for side in q
                ]
            )
        )
        rows = eighths[0][0][3 * small :]
        g_query, g_value, g_gain_one, g_shift_one = (plan.reduce(rows[i]) for i in range(4))
    if swaps:
        g_qkv, g_query, g_value, g_gain_one, g_shift_one = unpack(
            unpack_inner_kernel,
            index,
            pieces_c,
            [(half, 3 * width)] + [(half,)] * 4,
            "unpack_inner",
        )
        across_a, g_qkv = after(across_a, g_qkv)
        pieces_a = (sum_a, across_a, beside_a, plan.over_core(across_a))
        g_drop, g_lift, g_out, g_out_bias, g_gain_two, g_shift_two, g_drop_bias, g_lift_bias = (
            unpack(
                unpack_outer_kernel,
                index,
                pieces_a,
                [(ff // 2, width), (half, ff), (half, width)] + [(half,)] * 4 + [(ff // 2,)],
                "unpack_outer",
            )
        )
    return (
        output,
        input_grad,
        g_gain_one,
        g_shift_one,
        g_qkv,
        g_query,
        g_value,
        g_out,
        g_out_bias,
        g_gain_two,
        g_shift_two,
        g_lift,
        g_lift_bias,
        g_drop,
        g_drop_bias,
    )


def solution(mesh):
    spread = P(("rep", "fsdp"), None, None)
    vector, matrix = P("fsdp"), P("fsdp", None)
    in_specs = (
        spread,
        vector,
        vector,
        matrix,
        vector,
        vector,
        matrix,
        vector,
        vector,
        vector,
        matrix,
        vector,
        matrix,
        vector,
        spread,
    )
    out_specs = (
        spread,
        spread,
        vector,
        vector,
        matrix,
        vector,
        vector,
        matrix,
        vector,
        vector,
        vector,
        matrix,
        vector,
        matrix,
        vector,
    )
    swaps = mesh.shape["rep"] == 16 and mesh.shape["fsdp"] == 2
    return jax.shard_map(
        functools.partial(per_device, swaps=swaps),
        mesh=mesh,
        in_specs=in_specs,
        out_specs=out_specs,
        check_vma=False,
    )
```

```python
import functools

import jax
import jax.numpy as jnp
from jax import lax
from jax.experimental import pallas as pl
from jax.experimental.layout import Layout, with_layout_constraint
from jax.experimental.pallas import tpu as pltpu
from jax.sharding import PartitionSpec as P

HEADS = 6
HEAD_DIM = 64
PAIR = 2 * HEAD_DIM
LANE = 128
EPS = 1e-06
ROOT_HALF = 0.7071067811865476
GAUSS = 0.3989422804014327
LOG2E = 1.4426950408889634
SCALE = HEAD_DIM ** (-0.5)
F32 = jnp.float32
BF16 = jnp.bfloat16


def nn(a, b):
    return lax.dot_general(a, b, (((1,), (0,)), ((), ())), preferred_element_type=F32)


def nt(a, b):
    return lax.dot_general(a, b, (((1,), (1,)), ((), ())), preferred_element_type=F32)


def tn(a, b):
    return lax.dot_general(a, b, (((0,), (0,)), ((), ())), preferred_element_type=F32)


def normalise(v):
    mean = jnp.mean(v, axis=-1, keepdims=True)
    centred = v - mean
    var = jnp.mean(centred * centred, axis=-1, keepdims=True)
    inverse = lax.rsqrt(var + EPS)
    return centred * inverse, inverse


def norm_back(grad, normal, inverse, gain):
    scaled = grad * gain
    return inverse * (
        scaled
        - jnp.mean(scaled, axis=-1, keepdims=True)
        - normal * jnp.mean(scaled * normal, axis=-1, keepdims=True)
    )


def fold(v):
    return jnp.sum(v.reshape(v.shape[0] // 8, 8, v.shape[1]), axis=0)


def pad_rows(scratch, ref, length):
    for j in range(ref.shape[0]):
        scratch[j, 0:length, :] = ref[j].astype(scratch.dtype)


def zero_tail(scratch, length):
    images, rows, columns = scratch.shape
    low = (length // 16) * 16
    scratch[:, low:rows, :] = jnp.zeros((images, rows - low, columns), scratch.dtype)


def split_pair(v):
    first = lax.broadcasted_iota(jnp.int32, v.shape, 1) < HEAD_DIM
    zero = jnp.zeros_like(v)
    return jnp.concatenate([jnp.where(first, v, zero), jnp.where(first, zero, v)], axis=0)


def join_pair(v):
    rows = v.shape[0] // 2
    first = lax.broadcasted_iota(jnp.int32, (rows, PAIR), 1) < HEAD_DIM
    return jnp.where(first, v[:rows], v[rows:])


def join_pieces(full, own, near, far, index):
    block = own.shape[0]
    half = block // 2
    x, core = index[0], index[1]
    other = (1 - x) * block
    full[pl.ds(pl.multiple_of(x * block, 16), block), :] = own[...]
    full[pl.ds(pl.multiple_of(other + core * half, 16), half), :] = near[0:half, :]
    full[pl.ds(pl.multiple_of(other + (1 - core) * half, 16), half), :] = far[0:half, :]


def quarters(index, keep, send):
    x, core, y = index[0], index[1], index[2]
    for dest, owner in ((keep, core), (send, 1 - core)):
        for slot, half in ((0, x), (1, 1 - x)):
            for side in range(2):
                yield dest.at[slot, jnp.where(y == side, 0, 1)], half, owner, side


def pack_first_kernel(index, *refs):
    vectors, lift_bias, weight, packed = refs[:8], *refs[8:]
    half = weight.shape[0] // 2
    shard, width = vectors[0].shape[0], weight.shape[1] // 3
    packed[0:half, :] = weight[pl.ds(pl.multiple_of(index[1] * half, 16), half), :]
    packed[half:, :] = jnp.zeros((8, 3 * width), BF16)
    for i, ref in enumerate(vectors):
        row = ref[...].astype(F32).reshape(1, shard)
        packed[half + i : half + i + 1, 0:shard] = row.astype(BF16)
    bias = lift_bias[...].astype(F32).reshape(1, lift_bias.shape[0]).astype(BF16)
    for k in range(lift_bias.shape[0] // width):
        packed[half + k : half + k + 1, width : 2 * width] = bias[:, k * width : (k + 1) * width]


def pack_rest_kernel(index, *refs):
    for weight, half_out in zip(refs[:3], refs[3:]):
        half = half_out.shape[0]
        half_out[...] = weight[pl.ds(pl.multiple_of(index[1] * half, 16), half), :]


def join_vectors(vec_ref, own, other, index):
    width = vec_ref.shape[1]
    half = width // 2
    mine, theirs = own[-8:, :].astype(F32), other[-8:, :].astype(F32)
    first = index[0] == 0
    low, high = jnp.where(first, mine, theirs), jnp.where(first, theirs, mine)
    vec_ref[0:8, :] = jnp.concatenate([low[:, :half], high[:, :half]], axis=1)
    blocks = vec_ref.shape[0] // 2 - 4
    vec_ref[8 : 8 + blocks, :] = low[:blocks, width : 2 * width]
    vec_ref[8 + blocks :, :] = high[:blocks, width : 2 * width]


def attend_kernel(
    length,
    index,
    tok_ref,
    packed,
    own,
    near,
    far,
    normed_ref,
    proj_ref,
    mixed_ref,
    w_ref,
    vec_ref,
    n_s,
):
    images, rows, width = n_s.shape

    @pl.when(pl.program_id(0) == 0)
    def _():
        zero_tail(n_s, length)
        join_pieces(w_ref, own, near, far, index)
        join_vectors(vec_ref, packed, near, index)

    gain, shift = vec_ref[0:1, :], vec_ref[1:2, :]
    bias = jnp.concatenate([vec_ref[2:3, :], jnp.zeros((1, width), F32), vec_ref[3:4, :]], axis=1)
    for j in range(images):
        normal, _ = normalise(tok_ref[j].astype(F32))
        n_s[j, 0:length, :] = (normal * gain + shift).astype(BF16)
    normed_ref[...] = n_s[...]
    flat = n_s[...].reshape(images * rows, width)
    proj_ref[...] = (nn(flat, w_ref[...]) + bias).astype(BF16).reshape(images, rows, 3 * width)
    live = lax.broadcasted_iota(jnp.int32, (2 * rows, rows), 1) < length
    ones = jnp.ones((rows, PAIR), BF16)
    for j in range(images):
        for c in range(0, width, PAIR):
            query = split_pair(proj_ref[j, :, c : c + PAIR] * jnp.asarray(SCALE, BF16))
            key = proj_ref[j, :, width + c : width + c + PAIR]
            value = proj_ref[j, :, 2 * width + c : 2 * width + c + PAIR]
            scores = jnp.where(live, nt(query, key), -1e30)
            top = jnp.max(scores, axis=-1, keepdims=True)
            weights = jnp.exp(scores - top).astype(BF16)
            both = nn(weights, jnp.concatenate([value, ones], axis=1))
            mixed_ref[j, :, c : c + PAIR] = join_pair(both[:, :PAIR] / both[:, PAIR:]).astype(BF16)


def mlp_kernel(
    length,
    chunk,
    index,
    tok_ref,
    cot_ref,
    mixed_ref,
    vec_ref,
    out_own,
    out_near,
    out_far,
    lift_own,
    lift_near,
    lift_far,
    drop_own,
    drop_near,
    drop_far,
    out_ref,
    d_middle_ref,
    d_mixed_ref,
    keep,
    send,
    x_s,
    z_s,
    w_out_ref,
    w_lift_ref,
    w_drop_ref,
    lift_bias_ref,
    a_drop,
    a_lift,
    a_out,
    a_vec,
    a_bias,
):
    step = pl.program_id(0)
    images, rows, width = x_s.shape
    total = images * rows
    hidden_width = w_lift_ref.shape[1]

    @pl.when(step == 0)
    def _():
        zero_tail(x_s, length)
        zero_tail(z_s, length)
        join_pieces(w_out_ref, out_own, out_near, out_far, index)
        join_pieces(w_lift_ref, lift_own, lift_near, lift_far, index)
        join_pieces(w_drop_ref, drop_own, drop_near, drop_far, index)
        for k in range(hidden_width // width):
            lift_bias_ref[:, k * width : (k + 1) * width] = vec_ref[8 + k : 9 + k, :]
        for acc in (a_drop, a_lift, a_out, a_vec, a_bias):
            acc[...] = jnp.zeros_like(acc)

    pad_rows(x_s, tok_ref, length)
    pad_rows(z_s, cot_ref, length)
    out_bias, gain, shift, drop_bias = (vec_ref[i : i + 1, :] for i in range(4, 8))
    mixed = mixed_ref[...].reshape(total, width)
    dz = z_s[...].reshape(total, width)
    dz_f = dz.astype(F32)
    middle = x_s[...].reshape(total, width).astype(F32) + nn(mixed, w_out_ref[...]) + out_bias
    normal, inverse = normalise(middle)
    normed = (normal * gain + shift).astype(BF16)
    result = middle + drop_bias
    d_normed = jnp.zeros((total, width), F32)
    for c in range(0, hidden_width, chunk):
        part = slice(c, c + chunk)
        hidden = nn(normed, w_lift_ref[:, part]) + lift_bias_ref[:, part]
        cdf = 0.5 + 0.5 * lax.erf(hidden * ROOT_HALF)
        bell = jnp.exp(hidden * hidden * -0.5) * GAUSS
        active = (hidden * cdf).astype(BF16)
        d_active = nt(dz, w_drop_ref[part, :])
        d_hidden_f = d_active * (cdf + hidden * bell)
        d_hidden = d_hidden_f.astype(BF16)
        result = result + nn(active, w_drop_ref[part, :])
        d_normed = d_normed + nt(d_hidden, w_lift_ref[:, part])
        a_drop[part, :] += tn(active, dz)
        a_lift[:, part] += tn(normed, d_hidden)
        a_bias[:, part] += fold(d_hidden.astype(F32))
    out = result.astype(BF16)
    for j in range(images):
        out_ref[j] = out[j * rows : j * rows + length]
    d_middle = dz_f + norm_back(d_normed, normal, inverse, gain)
    d_middle_ref[...] = d_middle.reshape(images, rows, width)
    d_attended = d_middle.astype(BF16)
    d_mixed_ref[...] = nt(d_attended, w_out_ref[...]).astype(BF16).reshape(images, rows, width)
    a_out[...] += tn(mixed, d_attended)
    a_vec[0] += fold(d_attended.astype(F32))
    a_vec[1] += fold(d_normed * normal)
    a_vec[2] += fold(d_normed)
    a_vec[3] += fold(dz_f)

    @pl.when(step == pl.num_programs(0) - 1)
    def _():
        columns = jnp.sum(a_bias[...], axis=0, keepdims=True)
        vectors = jnp.concatenate(
            [jnp.sum(a_vec[...], axis=1)]
            + [columns[:, c : c + width] for c in range(0, hidden_width, width)],
            axis=0,
        ).astype(BF16)
        deep, tall, small = hidden_width // 4, width // 4, width // 8
        for place, half, core, side in quarters(index, keep, send):
            quarter = 2 * half + core
            if side == 0:
                first = pl.multiple_of(quarter * deep, 8)
                place[0:deep, :] = a_drop[pl.ds(first, deep), :].astype(BF16)
                place[deep + small : deep + small + 8, :] = vectors
                place[deep + small + 8 :, :] = jnp.zeros((8, width), BF16)
            else:
                rows_of = pl.ds(pl.multiple_of(quarter * tall, 8), tall)
                for k in range(hidden_width // width):
                    place[k * tall : (k + 1) * tall, :] = a_lift[
                        rows_of, k * width : (k + 1) * width
                    ].astype(BF16)
                place[deep + small :, :] = jnp.zeros((16, width), BF16)
            first = pl.multiple_of(quarter * tall + side * small, 8)
            place[deep : deep + small, :] = a_out[pl.ds(first, small), :].astype(BF16)


def back_kernel(
    length, first, last, index, tok_ref, proj_ref, normed_ref, d_mixed_ref, d_middle_ref, w_ref, vec_ref, *refs
):
    if not first:
        old, refs = refs[:3], refs[4:]
    in_grad_ref = refs[0]
    if last:
        keep, send = refs[1:3]
        sums, d_s = refs[3:6], refs[6]
    else:
        sums, d_s = refs[1:4], refs[4]
    a_qkv, a_proj, a_vec = sums
    images, rows, wide = d_s.shape
    width = wide // 3
    total = images * rows

    @pl.when(pl.program_id(0) == 0)
    def _():
        for i, acc in enumerate(sums):
            acc[...] = jnp.zeros_like(acc) if first else old[i][...]

    live = lax.broadcasted_iota(jnp.int32, (rows, 2 * rows), 0) < length
    for j in range(images):
        for c in range(0, width, PAIR):
            query = split_pair(proj_ref[j, :, c : c + PAIR] * jnp.asarray(SCALE, BF16))
            key = proj_ref[j, :, width + c : width + c + PAIR]
            value = proj_ref[j, :, 2 * width + c : 2 * width + c + PAIR]
            d_mixed = split_pair(d_mixed_ref[j, :, c : c + PAIR])
            scores = jnp.where(live, nt(key, query), -1e30)
            top = jnp.max(scores, axis=0, keepdims=True)
            weights = jnp.exp(scores - top)
            probs = weights * (1.0 / jnp.sum(weights, axis=0, keepdims=True))
            d_probs = nt(value, d_mixed)
            delta = jnp.sum(probs * d_probs, axis=0, keepdims=True)
            d_scores = (probs * (d_probs - delta)).astype(BF16)
            d_value = nn(probs.astype(BF16), d_mixed)
            d_key = nn(d_scores, query)
            d_query = join_pair(tn(d_scores, key)) * SCALE
            d_s[j, :, c : c + PAIR] = d_query.astype(BF16)
            d_s[j, :, width + c : width + c + PAIR] = d_key.astype(BF16)
            d_s[j, :, 2 * width + c : 2 * width + c + PAIR] = d_value.astype(BF16)
    d_proj = d_s[...].reshape(total, wide)
    a_qkv[...] += tn(normed_ref[...].reshape(total, width), d_proj)
    a_proj[...] += fold(d_proj.astype(F32))
    d_normed = nt(d_proj, w_ref[...])
    gain = vec_ref[0:1, :]
    for j in range(images):
        normal, inverse = normalise(tok_ref[j].astype(F32))
        grad = d_normed[j * rows : j * rows + length]
        in_grad_ref[j] = (
            d_middle_ref[j, 0:length, :] + norm_back(grad, normal, inverse, gain)
        ).astype(BF16)
        a_vec[0:1, :] += jnp.sum(grad * normal, axis=0, keepdims=True)
        a_vec[1:2, :] += jnp.sum(grad, axis=0, keepdims=True)
    if not last:
        return

    @pl.when(pl.program_id(0) == pl.num_programs(0) - 1)
    def _():
        columns = jnp.sum(a_proj[...], axis=0, keepdims=True)
        vectors = jnp.concatenate(
            [columns[:, :width], columns[:, 2 * width :], a_vec[...], jnp.zeros((4, width), F32)],
            axis=0,
        ).astype(BF16)
        small = width // 8
        for place, half, core, side in quarters(index, keep, send):
            first_row = pl.multiple_of((2 * half + core) * 2 * small + side * small, 8)
            for k in range(3):
                place[k * small : (k + 1) * small, :] = a_qkv[
                    pl.ds(first_row, small), k * width : (k + 1) * width
                ].astype(BF16)
            place[3 * small :, :] = vectors


def placed(full, index, pieces, by_z=False):
    core, y = index[1], index[2]
    spots = ((core, y), (core, 1 - y), (1 - core, y), (1 - core, 1 - y))
    rows = pieces[0].shape[0]
    for (owner, side), piece in zip(spots, pieces):
        if by_z:
            half = rows // 2
            for k, z in ((0, index[3]), (1, 1 - index[3])):
                full[owner, side, pl.ds(pl.multiple_of(z * half, 8), half), :] = piece[
                    k * half : (k + 1) * half, :
                ].astype(F32)
        else:
            full[owner, side] = piece[...].astype(F32)


def own_half(index, row):
    half = row.shape[-1] // 2
    return jnp.where(index[0] == 0, row[:, :half], row[:, half:])[0]


def unpack_kernel(index, *refs):
    unpack_outer(index, refs[0:4], refs[8:16], refs[21])
    unpack_inner(index, refs[4:8], refs[16:21], refs[22])


def unpack_outer(index, pieces, outs, full):
    g_drop, g_lift, g_out, g_out_bias, g_gain, g_shift, g_drop_bias, g_lift_bias = outs
    placed(full, index, pieces, by_z=True)
    width = g_out.shape[1]
    deep, tall, small = g_drop.shape[0] // 2, width // 4, width // 8
    blocks = g_lift.shape[1] // width
    for core in range(2):
        g_drop[core * deep : (core + 1) * deep, :] = full[core, 0, 0:deep, :]
        for k in range(blocks):
            g_lift[core * tall : (core + 1) * tall, k * width : (k + 1) * width] = full[
                core, 1, k * tall : (k + 1) * tall, :
            ]
        for side in range(2):
            first = core * tall + side * small
            g_out[first : first + small, :] = full[core, side, deep : deep + small, :]
    vectors = full[0, 0, deep + small :, :]
    for i, ref in enumerate((g_out_bias, g_gain, g_shift, g_drop_bias)):
        ref[...] = own_half(index, vectors[i : i + 1, :])
    for k in range(blocks // 2):
        row = jnp.where(
            index[0] == 0,
            vectors[4 + k : 5 + k, :],
            vectors[4 + blocks // 2 + k : 5 + blocks // 2 + k, :],
        )
        g_lift_bias[k * width : (k + 1) * width] = row[0]


def unpack_inner(index, pieces, outs, full):
    g_qkv, g_query, g_value, g_gain, g_shift = outs
    placed(full, index, pieces)
    width = full.shape[3]
    small = width // 8
    for core in range(2):
        for side in range(2):
            first = (2 * core + side) * small
            for k in range(3):
                g_qkv[first : first + small, k * width : (k + 1) * width] = full[
                    core, side, k * small : (k + 1) * small, :
                ]
    vectors = full[0, 0, 3 * small :, :]
    for i, ref in enumerate((g_query, g_value, g_gain, g_shift)):
        ref[...] = own_half(index, vectors[i : i + 1, :])


VMEM_LIMIT = 60 * 1024 * 1024
PARAMS = pltpu.CompilerParams(vmem_limit_bytes=VMEM_LIMIT)
SCALARS = pl.BlockSpec(memory_space=pltpu.SMEM)


def whole(*shape):
    return pl.BlockSpec(shape, lambda i: (0,) * len(shape))


def whole_like(arrays):
    return [whole(*a.shape) for a in arrays]


def per_step(*shape):
    return pl.BlockSpec(shape, lambda i: (i,) + (0,) * (len(shape) - 1))


def shape_of(dtype, *shape):
    return jax.ShapeDtypeStruct(shape, dtype)


def cost(microseconds):
    return pl.CostEstimate(flops=int(microseconds * 1e3), bytes_accessed=1, transcendentals=0)


def pack_first(index, vectors, lift_bias, weight):
    rows, columns = weight.shape
    return pl.pallas_call(
        pack_first_kernel,
        grid=(1,),
        in_specs=[SCALARS, *whole_like((*vectors, lift_bias, weight))],
        out_specs=whole(rows // 2 + 8, columns),
        out_shape=shape_of(BF16, rows // 2 + 8, columns),
        compiler_params=PARAMS,
        cost_estimate=cost(1),
        name="pack_first",
    )(index, *vectors, lift_bias, weight)


def pack_rest(index, weights):
    return pl.pallas_call(
        pack_rest_kernel,
        grid=(1,),
        in_specs=[SCALARS, *whole_like(weights)],
        out_specs=[whole(w.shape[0] // 2, w.shape[1]) for w in weights],
        out_shape=[shape_of(BF16, w.shape[0] // 2, w.shape[1]) for w in weights],
        compiler_params=PARAMS,
        cost_estimate=cost(1),
        name="pack_rest",
    )(index, *weights)


def forward_attention(index, tokens, ff, packed, pieces):
    images, length, width = tokens.shape
    rows = -(-length // 16) * 16
    group = 4 if images % 4 == 0 else 1
    return pl.pallas_call(
        functools.partial(attend_kernel, length),
        grid=(images // group,),
        in_specs=[SCALARS, per_step(group, length, width), *whole_like((packed, *pieces))],
        out_specs=[
            per_step(group, rows, width),
            per_step(group, rows, 3 * width),
            per_step(group, rows, width),
            whole(width, 3 * width),
            whole(8 + ff // width, width),
        ],
        out_shape=[
            shape_of(BF16, images, rows, width),
            shape_of(BF16, images, rows, 3 * width),
            shape_of(BF16, images, rows, width),
            shape_of(BF16, width, 3 * width),
            shape_of(F32, 8 + ff // width, width),
        ],
        scratch_shapes=[pltpu.VMEM((group, rows, width), BF16)],
        compiler_params=PARAMS,
        cost_estimate=cost(1),
        name="attend",
    )(index, tokens, packed, *pieces)


def mlp_both_ways(index, tokens, cotangent, mixed, vectors, ff, pieces):
    images, length, width = tokens.shape
    rows = mixed.shape[1]
    group = 2 if images % 2 == 0 else 1
    eighth = (2, 2, ff // 4 + width // 8 + 16, width)
    return pl.pallas_call(
        functools.partial(mlp_kernel, length, 512),
        grid=(images // group,),
        in_specs=[
            SCALARS,
            per_step(group, length, width),
            per_step(group, length, width),
            per_step(group, rows, width),
            *whole_like((vectors, *pieces)),
        ],
        out_specs=[
            per_step(group, length, width),
            per_step(group, rows, width),
            per_step(group, rows, width),
            whole(*eighth),
            whole(*eighth),
        ],
        out_shape=[
            shape_of(BF16, images, length, width),
            shape_of(F32, images, rows, width),
            shape_of(BF16, images, rows, width),
            shape_of(BF16, *eighth),
            shape_of(BF16, *eighth),
        ],
        scratch_shapes=[
            pltpu.VMEM((group, rows, width), BF16),
            pltpu.VMEM((group, rows, width), BF16),
            pltpu.VMEM((width, width), BF16),
            pltpu.VMEM((width, ff), BF16),
            pltpu.VMEM((ff, width), BF16),
            pltpu.VMEM((1, ff), F32),
            pltpu.VMEM((ff, width), F32),
            pltpu.VMEM((width, ff), F32),
            pltpu.VMEM((width, width), F32),
            pltpu.VMEM((4, 8, width), F32),
            pltpu.VMEM((8, ff), F32),
        ],
        compiler_params=PARAMS,
        cost_estimate=cost(1),
        name="mlp",
    )(index, tokens, cotangent, mixed, vectors, *pieces)


def attention_backward(
    index, tokens, projected, normed, w_qkv, vectors, d_mixed, d_middle, start, stop, earlier=()
):
    images, length, width = tokens.shape
    rows = normed.shape[1]
    wide = 3 * width
    group = 2 if images % 2 == 0 else 1
    offset = start // group
    first, last = not earlier, stop == images
    chunk = (2, 2, 3 * width // 8 + 8, width)
    sums = [(width, wide), (8, wide), (2, width)]

    def at(*shape):
        return pl.BlockSpec((group,) + shape, lambda i: (i + offset if offset else i, 0, 0))

    return pl.pallas_call(
        functools.partial(back_kernel, length, first, last),
        grid=((stop - start) // group,),
        in_specs=[
            SCALARS,
            at(length, width),
            at(rows, wide),
            at(rows, width),
            at(rows, width),
            at(rows, width),
            *whole_like((w_qkv, vectors)),
        ]
        + ([] if first else [whole(*d) for d in sums] + [pl.BlockSpec(memory_space=pl.ANY)]),
        out_specs=[at(length, width)]
        + ([whole(*chunk)] * 2 if last else [whole(*d) for d in sums]),
        out_shape=[shape_of(BF16, images, length, width)]
        + ([shape_of(BF16, *chunk)] * 2 if last else [shape_of(F32, *d) for d in sums]),
        scratch_shapes=([pltpu.VMEM(d, F32) for d in sums] if last else [])
        + [pltpu.VMEM((group, rows, wide), BF16)],
        input_output_aliases={} if first else {11: 0},
        compiler_params=PARAMS,
        cost_estimate=cost(1),
        name="back",
    )(index, tokens, projected, normed, d_mixed, d_middle, w_qkv, vectors, *earlier)


def unpack(index, outer, inner, shapes):
    return pl.pallas_call(
        unpack_kernel,
        grid=(1,),
        in_specs=[SCALARS, *whole_like((*outer, *inner))],
        out_specs=[whole(*d) for d in shapes],
        out_shape=[shape_of(F32, *d) for d in shapes],
        scratch_shapes=[
            pltpu.VMEM((2, 2) + outer[0].shape, F32),
            pltpu.VMEM((2, 2) + inner[0].shape, F32),
        ],
        compiler_params=PARAMS,
        cost_estimate=cost(1),
        name="unpack",
    )(index, *outer, *inner)


AXES = ("rep", "fsdp")


class Butterfly:
    def __init__(self):
        rep, x = lax.axis_index("rep"), lax.axis_index("fsdp")
        self.z = (rep >> 2) & 1
        self.index = jnp.stack([x, rep & 1, (rep >> 1) & 1, self.z]).astype(jnp.int32)

    def swap(self, v, rep_mask, x_mask=0):
        pairs = [
            (rep * 2 + x, (rep ^ rep_mask) * 2 + (x ^ x_mask)) for rep in range(16) for x in range(2)
        ]
        return lax.ppermute(v, AXES, pairs)

    def over_x(self, v):
        return self.swap(v, 0, 1)

    def over_core(self, v):
        return self.swap(v, 1)

    def over_y(self, v):
        return self.swap(v, 2)

    def over_z(self, v, mask):
        return self.swap(v, 4 * mask)

    def over_corner(self, v):
        return self.swap(v, 2, 1)

    def over_y_and_core(self, v):
        return self.swap(v, 3)

    def half(self, v, which):
        rows = v.shape[0] // 2
        return lax.dynamic_slice_in_dim(v, which * rows, rows, 0)

    def scatter(self, keep, got):
        total = [[keep[i, j] + got[i, j] for j in range(2)] for i in range(2)]
        return (total[1][0], total[0][1], total[1][1]), total[0][0]

    def send(self, parts):
        return self.over_x(parts[0]), self.over_y(parts[1]), self.over_corner(parts[2])


class Collective:
    def __init__(self):
        self.index = jnp.zeros((4,), jnp.int32)

    def gather_weight(self, own):
        full = lax.all_gather(own, "fsdp", axis=0, tiled=True)
        quarter = full.shape[0] // 4
        return full[: 2 * quarter], full[2 * quarter : 3 * quarter], full[3 * quarter :]

    def gather_vectors(self, vectors, lift_bias):
        whole_vectors = [lax.all_gather(v, "fsdp", axis=0, tiled=True) for v in vectors]
        whole_bias = lax.all_gather(lift_bias, "fsdp", axis=0, tiled=True)
        width = whole_vectors[0].shape[0]
        table = jnp.stack(whole_vectors).reshape(8, 2, width // 2)
        bias = whole_bias.reshape(2, -1, width)
        return (
            jnp.zeros((2, 8, 3 * width), BF16)
            .at[:, :, : width // 2]
            .set(table.transpose(1, 0, 2))
            .at[:, : bias.shape[1], width : 2 * width]
            .set(bias)
        )

    def reduce(self, v):
        owned = lax.psum_scatter(v.astype(BF16), "fsdp", scatter_dimension=0, tiled=True)
        return lax.psum(owned, "rep").astype(F32)


def after(*arrays):
    return lax.optimization_barrier(arrays)


def behind(arrays, *others):
    return lax.optimization_barrier((arrays, others))[0]


def settled(v):
    return with_layout_constraint(v.transpose(1, 0, 2), Layout(major_to_minor=(0, 1, 2)))


def in_order(keep, send):
    return [(q[0], q[1]) for q in (keep[0], send[0], keep[1], send[1])]


def per_device(
    tokens,
    gain_one,
    shift_one,
    qkv_weight,
    query_bias,
    value_bias,
    out_weight,
    out_bias,
    gain_two,
    shift_two,
    lift_weight,
    lift_bias,
    drop_weight,
    drop_bias,
    cotangent,
    swaps,
):
    length, width = tokens.shape[1:]
    plan = Butterfly() if swaps else Collective()
    index = plan.index
    small = (
        gain_one,
        shift_one,
        query_bias,
        value_bias,
        out_bias,
        gain_two,
        shift_two,
        drop_bias,
    )
    ff = lift_weight.shape[1]
    rest = (out_weight, lift_weight, drop_weight)
    if swaps:
        packed = pack_first(index, small, lift_bias, qkv_weight)
        near = plan.over_x(packed)
        qkv = (qkv_weight, near, plan.over_core(near))
        rest_then, packed = after(rest, packed)
        nears = [plan.over_x(half) for half in pack_rest(index, rest_then)]
    else:
        packed, theirs = plan.gather_vectors(small, lift_bias)
        own, near, far = plan.gather_weight(qkv_weight)
        qkv = (own, jnp.concatenate([near, theirs]), far)
    normed, projected, mixed, full_qkv, vectors = forward_attention(
        index, tokens, ff, packed, qkv
    )
    if swaps:
        mixed, nears = after(mixed, nears)
        outer = [
            piece for w, near in zip(rest, nears) for piece in (w, near, plan.over_core(near))
        ]
    else:
        outer = [piece for w in rest for piece in plan.gather_weight(w)]
    output, d_middle, d_mixed, keep_a, send_a = mlp_both_ways(
        index, tokens, cotangent, mixed, vectors, ff, outer
    )
    backward = functools.partial(
        attention_backward, index, tokens, projected, normed, full_qkv, vectors
    )
    images, half = tokens.shape[0], width // 2
    if swaps:
        got_a = plan.over_core(send_a)
        input_grad, *sums = backward(d_mixed, d_middle, 0, 2)
        sums, got_a = after(sums, got_a)
        parts_a, stay_a = plan.scatter(keep_a, got_a)
        sums, parts_a = after(sums, parts_a)
        more_a = plan.send(parts_a)
        input_grad, keep_c, send_c = backward(
            d_mixed, d_middle, 2, images, (*sums, input_grad)
        )
        send_c, more_a = after(send_c, more_a)
        got_c = plan.over_core(send_c)
        sum_a = stay_a + more_a[0] + more_a[1] + more_a[2]
        low_a, high_a = plan.half(sum_a, plan.z), plan.half(sum_a, 1 - plan.z)
        over_a = plan.over_z(high_a, 1)
        got_c = behind(got_c, low_a, high_a)
        parts_c, stay_c = plan.scatter(keep_c, got_c)
        over_a = behind(over_a, parts_c)
        more_c = plan.send(parts_c)
        low_a = low_a + over_a
        over_a = plan.over_z(low_a, 2)
        more_c = behind(more_c, low_a)
        sum_c = stay_c + more_c[0] + more_c[1] + more_c[2]
        over_a = behind(over_a, sum_c)
        over_c = plan.over_z(sum_c, 1)
        low_a = low_a + over_a
        over_a = plan.over_z(low_a, 1)
        over_c = behind(over_c, low_a)
        sum_c = sum_c + over_c
        over_a = behind(over_a, sum_c)
        over_c = plan.over_z(sum_c, 2)
        sum_a = jnp.concatenate([low_a, over_a])
        across_a, beside_a = plan.over_y(sum_a), plan.over_core(sum_a)
        output, input_grad = settled(output), settled(input_grad)
        over_c, output, input_grad = behind((over_c, output, input_grad), sum_a)
        output, input_grad = output.transpose(1, 0, 2), input_grad.transpose(1, 0, 2)
        sum_c = sum_c + over_c
        across_a = behind(across_a, sum_c)
        pieces_c = (sum_c, plan.over_y(sum_c), plan.over_core(sum_c), plan.over_y_and_core(sum_c))
        pieces_a = (sum_a, across_a, beside_a, plan.over_core(across_a))
        (
            g_drop,
            g_lift,
            g_out,
            g_out_bias,
            g_gain_two,
            g_shift_two,
            g_drop_bias,
            g_lift_bias,
            g_qkv,
            g_query,
            g_value,
            g_gain_one,
            g_shift_one,
        ) = unpack(
            index,
            pieces_a,
            pieces_c,
            [(ff // 2, width), (half, ff), (half, width)]
            + [(half,)] * 4
            + [(ff // 2,), (half, 3 * width)]
            + [(half,)] * 4,
        )
    else:
        input_grad, *sums = backward(d_mixed, d_middle, 0, images - 2)
        input_grad, keep_c, send_c = backward(
            d_mixed, d_middle, images - 2, images, (*sums, input_grad)
        )
        deep, tall, small = ff // 4, width // 4, width // 8
        eighths = in_order(keep_a, send_a)
        g_drop = plan.reduce(jnp.concatenate([q[0][:deep] for q in eighths]))
        g_lift = plan.reduce(
            jnp.concatenate(
                [
                    jnp.concatenate(
                        [q[1][k * tall : (k + 1) * tall] for k in range(ff // width)], axis=1
                    )
                    for q in eighths
                ]
            )
        )
        g_out = plan.reduce(
            jnp.concatenate([side[deep : deep + small] for q in eighths for side in q])
        )
        rows = eighths[0][0][deep + small : deep + small + 8]
        g_out_bias, g_gain_two, g_shift_two, g_drop_bias = (plan.reduce(rows[i]) for i in range(4))
        g_lift_bias = plan.reduce(rows[4:].reshape(-1))
        eighths = in_order(keep_c, send_c)
        g_qkv = plan.reduce(
            jnp.concatenate(
                [
                    jnp.concatenate([side[k * small : (k + 1) * small] for k in range(3)], axis=1)
                    for q in eighths
                    for side in q
                ]
            )
        )
        rows = eighths[0][0][3 * small :]
        g_query, g_value, g_gain_one, g_shift_one = (plan.reduce(rows[i]) for i in range(4))
    return (
        output,
        input_grad,
        g_gain_one,
        g_shift_one,
        g_qkv,
        g_query,
        g_value,
        g_out,
        g_out_bias,
        g_gain_two,
        g_shift_two,
        g_lift,
        g_lift_bias,
        g_drop,
        g_drop_bias,
    )


def solution(mesh):
    spread = P(("rep", "fsdp"), None, None)
    vector, matrix = P("fsdp"), P("fsdp", None)
    in_specs = (
        spread,
        vector,
        vector,
        matrix,
        vector,
        vector,
        matrix,
        vector,
        vector,
        vector,
        matrix,
        vector,
        matrix,
        vector,
        spread,
    )
    out_specs = (
        spread,
        spread,
        vector,
        vector,
        matrix,
        vector,
        vector,
        matrix,
        vector,
        vector,
        vector,
        matrix,
        vector,
        matrix,
        vector,
    )
    swaps = mesh.shape["rep"] == 16 and mesh.shape["fsdp"] == 2
    return jax.shard_map(
        functools.partial(per_device, swaps=swaps),
        mesh=mesh,
        in_specs=in_specs,
        out_specs=out_specs,
        check_vma=False,
    )
```

```python
import functools

import jax
import jax.numpy as jnp
from jax import lax
from jax.experimental import pallas as pl
from jax.experimental.layout import Layout, with_layout_constraint
from jax.experimental.pallas import tpu as pltpu
from jax.sharding import PartitionSpec as P

HEADS = 6
HEAD_DIM = 64
PAIR = 2 * HEAD_DIM
LANE = 128
EPS = 1e-06
ROOT_HALF = 0.7071067811865476
GAUSS = 0.3989422804014327
LOG2E = 1.4426950408889634
SCALE = HEAD_DIM ** (-0.5)
F32 = jnp.float32
BF16 = jnp.bfloat16


def nn(a, b):
    return lax.dot_general(a, b, (((1,), (0,)), ((), ())), preferred_element_type=F32)


def nt(a, b):
    return lax.dot_general(a, b, (((1,), (1,)), ((), ())), preferred_element_type=F32)


def tn(a, b):
    return lax.dot_general(a, b, (((0,), (0,)), ((), ())), preferred_element_type=F32)


def normalise(v):
    mean = jnp.mean(v, axis=-1, keepdims=True)
    centred = v - mean
    var = jnp.mean(centred * centred, axis=-1, keepdims=True)
    inverse = lax.rsqrt(var + EPS)
    return centred * inverse, inverse


def norm_back(grad, normal, inverse, gain):
    scaled = grad * gain
    return inverse * (
        scaled
        - jnp.mean(scaled, axis=-1, keepdims=True)
        - normal * jnp.mean(scaled * normal, axis=-1, keepdims=True)
    )


def fold(v):
    return jnp.sum(v.reshape(v.shape[0] // 8, 8, v.shape[1]), axis=0)


def pad_rows(scratch, ref, length):
    for j in range(ref.shape[0]):
        scratch[j, 0:length, :] = ref[j].astype(scratch.dtype)


def zero_tail(scratch, length):
    images, rows, columns = scratch.shape
    low = (length // 16) * 16
    scratch[:, low:rows, :] = jnp.zeros((images, rows - low, columns), scratch.dtype)


def split_pair(v):
    first = lax.broadcasted_iota(jnp.int32, v.shape, 1) < HEAD_DIM
    zero = jnp.zeros_like(v)
    return jnp.concatenate([jnp.where(first, v, zero), jnp.where(first, zero, v)], axis=0)


def join_pair(v):
    rows = v.shape[0] // 2
    first = lax.broadcasted_iota(jnp.int32, (rows, PAIR), 1) < HEAD_DIM
    return jnp.where(first, v[:rows], v[rows:])


def join_pieces(full, own, near, far, index, first=0):
    block = own.shape[0]
    half = block // 2
    x, core = index[0], index[1]
    other = (1 - x) * block
    full[pl.ds(pl.multiple_of(x * block, 16), block), :] = own[...]
    full[pl.ds(pl.multiple_of(other + core * half, 16), half), :] = near[first : first + half, :]
    full[pl.ds(pl.multiple_of(other + (1 - core) * half, 16), half), :] = far[first : first + half, :]


def quarters(index, keep, send):
    x, core, y = index[0], index[1], index[2]
    for dest, owner in ((keep, core), (send, 1 - core)):
        for slot, half in ((0, x), (1, 1 - x)):
            for side in range(2):
                yield dest.at[slot, jnp.where(y == side, 0, 1)], half, owner, side


def pack_first_kernel(index, *refs):
    vectors, lift_bias, weight, packed = refs[:8], *refs[8:]
    half = weight.shape[0] // 2
    shard, width = vectors[0].shape[0], weight.shape[1] // 3
    packed[0:half, :] = weight[pl.ds(pl.multiple_of(index[1] * half, 16), half), :]
    packed[half:, :] = jnp.zeros((8, 3 * width), BF16)
    for i, ref in enumerate(vectors):
        row = ref[...].astype(F32).reshape(1, shard)
        packed[half + i : half + i + 1, 0:shard] = row.astype(BF16)
    bias = lift_bias[...].astype(F32).reshape(1, lift_bias.shape[0]).astype(BF16)
    for k in range(lift_bias.shape[0] // width):
        packed[half + k : half + k + 1, width : 2 * width] = bias[:, k * width : (k + 1) * width]


def pack_rest_kernel(index, out_own, lift_own, drop_own, lift_half, both_half):
    tall, deep = lift_half.shape[0], drop_own.shape[0] // 2
    rows_of = pl.ds(pl.multiple_of(index[1] * tall, 16), tall)
    lift_half[...] = lift_own[rows_of, :]
    both_half[0:deep, :] = drop_own[pl.ds(pl.multiple_of(index[1] * deep, 16), deep), :]
    both_half[deep:, :] = out_own[rows_of, :]


def join_vectors(vec_ref, own, other, index):
    width = vec_ref.shape[1]
    half = width // 2
    mine, theirs = own[-8:, :].astype(F32), other[-8:, :].astype(F32)
    first = index[0] == 0
    low, high = jnp.where(first, mine, theirs), jnp.where(first, theirs, mine)
    vec_ref[0:8, :] = jnp.concatenate([low[:, :half], high[:, :half]], axis=1)
    blocks = vec_ref.shape[0] // 2 - 4
    vec_ref[8 : 8 + blocks, :] = low[:blocks, width : 2 * width]
    vec_ref[8 + blocks :, :] = high[:blocks, width : 2 * width]


def attend_kernel(
    length,
    index,
    tok_ref,
    packed,
    own,
    near,
    far,
    normed_ref,
    proj_ref,
    mixed_ref,
    w_ref,
    vec_ref,
    n_s,
):
    images, rows, width = n_s.shape

    @pl.when(pl.program_id(0) == 0)
    def _():
        zero_tail(n_s, length)
        join_pieces(w_ref, own, near, far, index)
        join_vectors(vec_ref, packed, near, index)

    gain, shift = vec_ref[0:1, :], vec_ref[1:2, :]
    bias = jnp.concatenate([vec_ref[2:3, :], jnp.zeros((1, width), F32), vec_ref[3:4, :]], axis=1)
    for j in range(images):
        normal, _ = normalise(tok_ref[j].astype(F32))
        n_s[j, 0:length, :] = (normal * gain + shift).astype(BF16)
    normed_ref[...] = n_s[...]
    flat = n_s[...].reshape(images * rows, width)
    proj_ref[...] = (nn(flat, w_ref[...]) + bias).astype(BF16).reshape(images, rows, 3 * width)
    live = lax.broadcasted_iota(jnp.int32, (2 * rows, rows), 1) < length
    ones = jnp.ones((rows, PAIR), BF16)
    for j in range(images):
        for c in range(0, width, PAIR):
            query = split_pair(proj_ref[j, :, c : c + PAIR] * jnp.asarray(SCALE, BF16))
            key = proj_ref[j, :, width + c : width + c + PAIR]
            value = proj_ref[j, :, 2 * width + c : 2 * width + c + PAIR]
            scores = jnp.where(live, nt(query, key), -1e30)
            top = jnp.max(scores, axis=-1, keepdims=True)
            weights = jnp.exp(scores - top).astype(BF16)
            both = nn(weights, jnp.concatenate([value, ones], axis=1))
            mixed_ref[j, :, c : c + PAIR] = join_pair(both[:, :PAIR] / both[:, PAIR:]).astype(BF16)


def mlp_kernel(
    length,
    chunk,
    index,
    tok_ref,
    cot_ref,
    mixed_ref,
    vec_ref,
    out_own,
    lift_own,
    drop_own,
    lift_near,
    lift_far,
    both_near,
    both_far,
    out_ref,
    d_middle_ref,
    d_mixed_ref,
    keep,
    send,
    x_s,
    z_s,
    w_out_ref,
    w_lift_ref,
    w_drop_ref,
    lift_bias_ref,
    a_drop,
    a_lift,
    a_out,
    a_vec,
    a_bias,
):
    step = pl.program_id(0)
    images, rows, width = x_s.shape
    total = images * rows
    hidden_width = w_lift_ref.shape[1]

    @pl.when(step == 0)
    def _():
        zero_tail(x_s, length)
        zero_tail(z_s, length)
        deep = drop_own.shape[0] // 2
        join_pieces(w_out_ref, out_own, both_near, both_far, index, deep)
        join_pieces(w_lift_ref, lift_own, lift_near, lift_far, index)
        join_pieces(w_drop_ref, drop_own, both_near, both_far, index)
        for k in range(hidden_width // width):
            lift_bias_ref[:, k * width : (k + 1) * width] = vec_ref[8 + k : 9 + k, :]
        for acc in (a_drop, a_lift, a_out, a_vec, a_bias):
            acc[...] = jnp.zeros_like(acc)

    pad_rows(x_s, tok_ref, length)
    pad_rows(z_s, cot_ref, length)
    out_bias, gain, shift, drop_bias = (vec_ref[i : i + 1, :] for i in range(4, 8))
    mixed = mixed_ref[...].reshape(total, width)
    dz = z_s[...].reshape(total, width)
    dz_f = dz.astype(F32)
    middle = x_s[...].reshape(total, width).astype(F32) + nn(mixed, w_out_ref[...]) + out_bias
    normal, inverse = normalise(middle)
    normed = (normal * gain + shift).astype(BF16)
    result = middle + drop_bias
    d_normed = jnp.zeros((total, width), F32)
    for c in range(0, hidden_width, chunk):
        part = slice(c, c + chunk)
        hidden = nn(normed, w_lift_ref[:, part]) + lift_bias_ref[:, part]
        cdf = 0.5 + 0.5 * lax.erf(hidden * ROOT_HALF)
        bell = jnp.exp(hidden * hidden * -0.5) * GAUSS
        active = (hidden * cdf).astype(BF16)
        d_active = nt(dz, w_drop_ref[part, :])
        d_hidden_f = d_active * (cdf + hidden * bell)
        d_hidden = d_hidden_f.astype(BF16)
        result = result + nn(active, w_drop_ref[part, :])
        d_normed = d_normed + nt(d_hidden, w_lift_ref[:, part])
        a_drop[part, :] += tn(active, dz)
        a_lift[:, part] += tn(normed, d_hidden)
        a_bias[:, part] += fold(d_hidden.astype(F32))
    out = result.astype(BF16)
    for j in range(images):
        out_ref[j] = out[j * rows : j * rows + length]
    d_middle = dz_f + norm_back(d_normed, normal, inverse, gain)
    d_middle_ref[...] = d_middle.reshape(images, rows, width)
    d_attended = d_middle.astype(BF16)
    d_mixed_ref[...] = nt(d_attended, w_out_ref[...]).astype(BF16).reshape(images, rows, width)
    a_out[...] += tn(mixed, d_attended)
    a_vec[0] += fold(d_attended.astype(F32))
    a_vec[1] += fold(d_normed * normal)
    a_vec[2] += fold(d_normed)
    a_vec[3] += fold(dz_f)

    @pl.when(step == pl.num_programs(0) - 1)
    def _():
        columns = jnp.sum(a_bias[...], axis=0, keepdims=True)
        vectors = jnp.concatenate(
            [jnp.sum(a_vec[...], axis=1)]
            + [columns[:, c : c + width] for c in range(0, hidden_width, width)],
            axis=0,
        ).astype(BF16)
        deep, tall, small = hidden_width // 4, width // 4, width // 8
        for place, half, core, side in quarters(index, keep, send):
            quarter = 2 * half + core
            if side == 0:
                first = pl.multiple_of(quarter * deep, 8)
                place[0:deep, :] = a_drop[pl.ds(first, deep), :].astype(BF16)
                place[deep + small : deep + small + 8, :] = vectors
                place[deep + small + 8 :, :] = jnp.zeros((8, width), BF16)
            else:
                rows_of = pl.ds(pl.multiple_of(quarter * tall, 8), tall)
                for k in range(hidden_width // width):
                    place[k * tall : (k + 1) * tall, :] = a_lift[
                        rows_of, k * width : (k + 1) * width
                    ].astype(BF16)
                place[deep + small :, :] = jnp.zeros((16, width), BF16)
            first = pl.multiple_of(quarter * tall + side * small, 8)
            place[deep : deep + small, :] = a_out[pl.ds(first, small), :].astype(BF16)


def back_kernel(
    length, first, last, index, tok_ref, proj_ref, normed_ref, d_mixed_ref, d_middle_ref, w_ref, vec_ref, *refs
):
    if not first:
        old, refs = refs[:3], refs[4:]
    in_grad_ref = refs[0]
    if last:
        keep, send = refs[1:3]
        sums, d_s = refs[3:6], refs[6]
    else:
        sums, d_s = refs[1:4], refs[4]
    a_qkv, a_proj, a_vec = sums
    images, rows, wide = d_s.shape
    width = wide // 3
    total = images * rows

    @pl.when(pl.program_id(0) == 0)
    def _():
        for i, acc in enumerate(sums):
            acc[...] = jnp.zeros_like(acc) if first else old[i][...]

    live = lax.broadcasted_iota(jnp.int32, (rows, 2 * rows), 0) < length
    for j in range(images):
        for c in range(0, width, PAIR):
            query = split_pair(proj_ref[j, :, c : c + PAIR] * jnp.asarray(SCALE, BF16))
            key = proj_ref[j, :, width + c : width + c + PAIR]
            value = proj_ref[j, :, 2 * width + c : 2 * width + c + PAIR]
            d_mixed = split_pair(d_mixed_ref[j, :, c : c + PAIR])
            scores = jnp.where(live, nt(key, query), -1e30)
            top = jnp.max(scores, axis=0, keepdims=True)
            weights = jnp.exp(scores - top)
            probs = weights * (1.0 / jnp.sum(weights, axis=0, keepdims=True))
            d_probs = nt(value, d_mixed)
            delta = jnp.sum(probs * d_probs, axis=0, keepdims=True)
            d_scores = (probs * (d_probs - delta)).astype(BF16)
            d_value = nn(probs.astype(BF16), d_mixed)
            d_key = nn(d_scores, query)
            d_query = join_pair(tn(d_scores, key)) * SCALE
            d_s[j, :, c : c + PAIR] = d_query.astype(BF16)
            d_s[j, :, width + c : width + c + PAIR] = d_key.astype(BF16)
            d_s[j, :, 2 * width + c : 2 * width + c + PAIR] = d_value.astype(BF16)
    d_proj = d_s[...].reshape(total, wide)
    a_qkv[...] += tn(normed_ref[...].reshape(total, width), d_proj)
    a_proj[...] += fold(d_proj.astype(F32))
    d_normed = nt(d_proj, w_ref[...])
    gain = vec_ref[0:1, :]
    for j in range(images):
        normal, inverse = normalise(tok_ref[j].astype(F32))
        grad = d_normed[j * rows : j * rows + length]
        in_grad_ref[j] = (
            d_middle_ref[j, 0:length, :] + norm_back(grad, normal, inverse, gain)
        ).astype(BF16)
        a_vec[0:1, :] += jnp.sum(grad * normal, axis=0, keepdims=True)
        a_vec[1:2, :] += jnp.sum(grad, axis=0, keepdims=True)
    if not last:
        return

    @pl.when(pl.program_id(0) == pl.num_programs(0) - 1)
    def _():
        columns = jnp.sum(a_proj[...], axis=0, keepdims=True)
        vectors = jnp.concatenate(
            [columns[:, :width], columns[:, 2 * width :], a_vec[...], jnp.zeros((4, width), F32)],
            axis=0,
        ).astype(BF16)
        small = width // 8
        for place, half, core, side in quarters(index, keep, send):
            first_row = pl.multiple_of((2 * half + core) * 2 * small + side * small, 8)
            for k in range(3):
                place[k * small : (k + 1) * small, :] = a_qkv[
                    pl.ds(first_row, small), k * width : (k + 1) * width
                ].astype(BF16)
            place[3 * small :, :] = vectors


def placed(full, index, pieces, by_z=False):
    core, y = index[1], index[2]
    spots = ((core, y), (core, 1 - y), (1 - core, y), (1 - core, 1 - y))
    rows = pieces[0].shape[0]
    for (owner, side), piece in zip(spots, pieces):
        if by_z:
            half = rows // 2
            for k, z in ((0, index[3]), (1, 1 - index[3])):
                full[owner, side, pl.ds(pl.multiple_of(z * half, 8), half), :] = piece[
                    k * half : (k + 1) * half, :
                ].astype(F32)
        else:
            full[owner, side] = piece[...].astype(F32)


def own_half(index, row):
    half = row.shape[-1] // 2
    return jnp.where(index[0] == 0, row[:, :half], row[:, half:])[0]


def unpack_outer_kernel(index, *refs):
    g_drop, g_lift, g_out, g_out_bias, g_gain, g_shift, g_drop_bias, g_lift_bias, full = refs[4:]
    placed(full, index, refs[:4], by_z=True)
    width = g_out.shape[1]
    deep, tall, small = g_drop.shape[0] // 2, width // 4, width // 8
    blocks = g_lift.shape[1] // width
    for core in range(2):
        g_drop[core * deep : (core + 1) * deep, :] = full[core, 0, 0:deep, :]
        for k in range(blocks):
            g_lift[core * tall : (core + 1) * tall, k * width : (k + 1) * width] = full[
                core, 1, k * tall : (k + 1) * tall, :
            ]
        for side in range(2):
            first = core * tall + side * small
            g_out[first : first + small, :] = full[core, side, deep : deep + small, :]
    vectors = full[0, 0, deep + small :, :]
    for i, ref in enumerate((g_out_bias, g_gain, g_shift, g_drop_bias)):
        ref[...] = own_half(index, vectors[i : i + 1, :])
    for k in range(blocks // 2):
        row = jnp.where(
            index[0] == 0,
            vectors[4 + k : 5 + k, :],
            vectors[4 + blocks // 2 + k : 5 + blocks // 2 + k, :],
        )
        g_lift_bias[k * width : (k + 1) * width] = row[0]


def unpack_inner_kernel(index, *refs):
    g_qkv, g_query, g_value, g_gain, g_shift, full = refs[4:]
    placed(full, index, refs[:4])
    width = full.shape[3]
    small = width // 8
    for core in range(2):
        for side in range(2):
            first = (2 * core + side) * small
            for k in range(3):
                g_qkv[first : first + small, k * width : (k + 1) * width] = full[
                    core, side, k * small : (k + 1) * small, :
                ]
    vectors = full[0, 0, 3 * small :, :]
    for i, ref in enumerate((g_query, g_value, g_gain, g_shift)):
        ref[...] = own_half(index, vectors[i : i + 1, :])


VMEM_LIMIT = 60 * 1024 * 1024
PARAMS = pltpu.CompilerParams(vmem_limit_bytes=VMEM_LIMIT)
SCALARS = pl.BlockSpec(memory_space=pltpu.SMEM)


def whole(*shape):
    return pl.BlockSpec(shape, lambda i: (0,) * len(shape))


def whole_like(arrays):
    return [whole(*a.shape) for a in arrays]


def per_step(*shape):
    return pl.BlockSpec(shape, lambda i: (i,) + (0,) * (len(shape) - 1))


def shape_of(dtype, *shape):
    return jax.ShapeDtypeStruct(shape, dtype)


def cost(microseconds):
    return pl.CostEstimate(flops=int(microseconds * 1e3), bytes_accessed=1, transcendentals=0)


def pack_first(index, vectors, lift_bias, weight):
    rows, columns = weight.shape
    return pl.pallas_call(
        pack_first_kernel,
        grid=(1,),
        in_specs=[SCALARS, *whole_like((*vectors, lift_bias, weight))],
        out_specs=whole(rows // 2 + 8, columns),
        out_shape=shape_of(BF16, rows // 2 + 8, columns),
        compiler_params=PARAMS,
        cost_estimate=cost(1),
        name="pack_first",
    )(index, *vectors, lift_bias, weight)


def pack_rest(index, weights):
    out_weight, lift_weight, drop_weight = weights
    tall, width = out_weight.shape[0] // 2, out_weight.shape[1]
    shapes = [(tall, lift_weight.shape[1]), (drop_weight.shape[0] // 2 + tall, width)]
    return pl.pallas_call(
        pack_rest_kernel,
        grid=(1,),
        in_specs=[SCALARS, *whole_like(weights)],
        out_specs=[whole(*d) for d in shapes],
        out_shape=[shape_of(BF16, *d) for d in shapes],
        compiler_params=PARAMS,
        cost_estimate=cost(1),
        name="pack_rest",
    )(index, *weights)


def forward_attention(index, tokens, ff, packed, pieces):
    images, length, width = tokens.shape
    rows = -(-length // 16) * 16
    group = 4 if images % 4 == 0 else 1
    return pl.pallas_call(
        functools.partial(attend_kernel, length),
        grid=(images // group,),
        in_specs=[SCALARS, per_step(group, length, width), *whole_like((packed, *pieces))],
        out_specs=[
            per_step(group, rows, width),
            per_step(group, rows, 3 * width),
            per_step(group, rows, width),
            whole(width, 3 * width),
            whole(8 + ff // width, width),
        ],
        out_shape=[
            shape_of(BF16, images, rows, width),
            shape_of(BF16, images, rows, 3 * width),
            shape_of(BF16, images, rows, width),
            shape_of(BF16, width, 3 * width),
            shape_of(F32, 8 + ff // width, width),
        ],
        scratch_shapes=[pltpu.VMEM((group, rows, width), BF16)],
        compiler_params=PARAMS,
        cost_estimate=cost(1),
        name="attend",
    )(index, tokens, packed, *pieces)


def mlp_both_ways(index, tokens, cotangent, mixed, vectors, ff, pieces):
    images, length, width = tokens.shape
    rows = mixed.shape[1]
    group = 2 if images % 2 == 0 else 1
    eighth = (2, 2, ff // 4 + width // 8 + 16, width)
    return pl.pallas_call(
        functools.partial(mlp_kernel, length, 512),
        grid=(images // group,),
        in_specs=[
            SCALARS,
            per_step(group, length, width),
            per_step(group, length, width),
            per_step(group, rows, width),
            *whole_like((vectors, *pieces)),
        ],
        out_specs=[
            per_step(group, length, width),
            per_step(group, rows, width),
            per_step(group, rows, width),
            whole(*eighth),
            whole(*eighth),
        ],
        out_shape=[
            shape_of(BF16, images, length, width),
            shape_of(F32, images, rows, width),
            shape_of(BF16, images, rows, width),
            shape_of(BF16, *eighth),
            shape_of(BF16, *eighth),
        ],
        scratch_shapes=[
            pltpu.VMEM((group, rows, width), BF16),
            pltpu.VMEM((group, rows, width), BF16),
            pltpu.VMEM((width, width), BF16),
            pltpu.VMEM((width, ff), BF16),
            pltpu.VMEM((ff, width), BF16),
            pltpu.VMEM((1, ff), F32),
            pltpu.VMEM((ff, width), F32),
            pltpu.VMEM((width, ff), F32),
            pltpu.VMEM((width, width), F32),
            pltpu.VMEM((4, 8, width), F32),
            pltpu.VMEM((8, ff), F32),
        ],
        compiler_params=PARAMS,
        cost_estimate=cost(1),
        name="mlp",
    )(index, tokens, cotangent, mixed, vectors, *pieces)


def attention_backward(
    index, tokens, projected, normed, w_qkv, vectors, d_mixed, d_middle, start, stop, earlier=()
):
    images, length, width = tokens.shape
    rows = normed.shape[1]
    wide = 3 * width
    group = 2 if images % 2 == 0 else 1
    offset = start // group
    first, last = not earlier, stop == images
    chunk = (2, 2, 3 * width // 8 + 8, width)
    sums = [(width, wide), (8, wide), (2, width)]

    def at(*shape):
        return pl.BlockSpec((group,) + shape, lambda i: (i + offset if offset else i, 0, 0))

    return pl.pallas_call(
        functools.partial(back_kernel, length, first, last),
        grid=((stop - start) // group,),
        in_specs=[
            SCALARS,
            at(length, width),
            at(rows, wide),
            at(rows, width),
            at(rows, width),
            at(rows, width),
            *whole_like((w_qkv, vectors)),
        ]
        + ([] if first else [whole(*d) for d in sums] + [pl.BlockSpec(memory_space=pl.ANY)]),
        out_specs=[at(length, width)]
        + ([whole(*chunk)] * 2 if last else [whole(*d) for d in sums]),
        out_shape=[shape_of(BF16, images, length, width)]
        + ([shape_of(BF16, *chunk)] * 2 if last else [shape_of(F32, *d) for d in sums]),
        scratch_shapes=([pltpu.VMEM(d, F32) for d in sums] if last else [])
        + [pltpu.VMEM((group, rows, wide), BF16)],
        input_output_aliases={} if first else {11: 0},
        compiler_params=PARAMS,
        cost_estimate=cost(1),
        name="back",
    )(index, tokens, projected, normed, d_mixed, d_middle, w_qkv, vectors, *earlier)


def unpack(kernel, name, index, pieces, shapes):
    return pl.pallas_call(
        kernel,
        grid=(1,),
        in_specs=[SCALARS, *whole_like(pieces)],
        out_specs=[whole(*d) for d in shapes],
        out_shape=[shape_of(F32, *d) for d in shapes],
        scratch_shapes=[pltpu.VMEM((2, 2) + pieces[0].shape, F32)],
        compiler_params=PARAMS,
        cost_estimate=cost(1),
        name=name,
    )(index, *pieces)


AXES = ("rep", "fsdp")


class Butterfly:
    def __init__(self):
        rep, x = lax.axis_index("rep"), lax.axis_index("fsdp")
        self.z = (rep >> 2) & 1
        self.index = jnp.stack([x, rep & 1, (rep >> 1) & 1, self.z]).astype(jnp.int32)

    def swap(self, v, rep_mask, x_mask=0):
        pairs = [
            (rep * 2 + x, (rep ^ rep_mask) * 2 + (x ^ x_mask)) for rep in range(16) for x in range(2)
        ]
        return lax.ppermute(v, AXES, pairs)

    def over_x(self, v):
        return self.swap(v, 0, 1)

    def over_core(self, v):
        return self.swap(v, 1)

    def over_y(self, v):
        return self.swap(v, 2)

    def over_z(self, v, mask):
        return self.swap(v, 4 * mask)

    def over_corner(self, v):
        return self.swap(v, 2, 1)

    def over_y_and_core(self, v):
        return self.swap(v, 3)

    def half(self, v, which):
        rows = v.shape[0] // 2
        return lax.dynamic_slice_in_dim(v, which * rows, rows, 0)

    def scatter(self, keep, got):
        total = [[keep[i, j] + got[i, j] for j in range(2)] for i in range(2)]
        return (total[1][0], total[0][1], total[1][1]), total[0][0]

    def send(self, parts):
        return self.over_x(parts[0]), self.over_y(parts[1]), self.over_corner(parts[2])


class Collective:
    def __init__(self):
        self.index = jnp.zeros((4,), jnp.int32)

    def gather_weight(self, own):
        full = lax.all_gather(own, "fsdp", axis=0, tiled=True)
        quarter = full.shape[0] // 4
        return full[: 2 * quarter], full[2 * quarter : 3 * quarter], full[3 * quarter :]

    def gather_vectors(self, vectors, lift_bias):
        whole_vectors = [lax.all_gather(v, "fsdp", axis=0, tiled=True) for v in vectors]
        whole_bias = lax.all_gather(lift_bias, "fsdp", axis=0, tiled=True)
        width = whole_vectors[0].shape[0]
        table = jnp.stack(whole_vectors).reshape(8, 2, width // 2)
        bias = whole_bias.reshape(2, -1, width)
        return (
            jnp.zeros((2, 8, 3 * width), BF16)
            .at[:, :, : width // 2]
            .set(table.transpose(1, 0, 2))
            .at[:, : bias.shape[1], width : 2 * width]
            .set(bias)
        )

    def reduce(self, v):
        owned = lax.psum_scatter(v.astype(BF16), "fsdp", scatter_dimension=0, tiled=True)
        return lax.psum(owned, "rep").astype(F32)


def after(*arrays):
    return lax.optimization_barrier(arrays)


def behind(arrays, *others):
    return lax.optimization_barrier((arrays, others))[0]


def settled(v):
    return with_layout_constraint(v.transpose(1, 0, 2), Layout(major_to_minor=(0, 1, 2)))


def in_order(keep, send):
    return [(q[0], q[1]) for q in (keep[0], send[0], keep[1], send[1])]


def per_device(
    tokens,
    gain_one,
    shift_one,
    qkv_weight,
    query_bias,
    value_bias,
    out_weight,
    out_bias,
    gain_two,
    shift_two,
    lift_weight,
    lift_bias,
    drop_weight,
    drop_bias,
    cotangent,
    swaps,
):
    length, width = tokens.shape[1:]
    plan = Butterfly() if swaps else Collective()
    index = plan.index
    small = (
        gain_one,
        shift_one,
        query_bias,
        value_bias,
        out_bias,
        gain_two,
        shift_two,
        drop_bias,
    )
    ff = lift_weight.shape[1]
    rest = (out_weight, lift_weight, drop_weight)
    if swaps:
        packed = pack_first(index, small, lift_bias, qkv_weight)
        near = plan.over_x(packed)
        qkv = (qkv_weight, near, plan.over_core(near))
        rest_then, packed = after(rest, packed)
        nears = [plan.over_x(half) for half in pack_rest(index, rest_then)]
    else:
        packed, theirs = plan.gather_vectors(small, lift_bias)
        own, near, far = plan.gather_weight(qkv_weight)
        qkv = (own, jnp.concatenate([near, theirs]), far)
    normed, projected, mixed, full_qkv, vectors = forward_attention(
        index, tokens, ff, packed, qkv
    )
    if swaps:
        mixed, nears = after(mixed, nears)
        pieces = [piece for near in nears for piece in (near, plan.over_core(near))]
    else:
        (out_own, *outs), (lift_own, *lifts), (drop_own, *drops) = map(plan.gather_weight, rest)
        rest = (out_own, lift_own, drop_own)
        pieces = [*lifts, *(jnp.concatenate(both) for both in zip(drops, outs))]
    outer = (*rest, *pieces)
    output, d_middle, d_mixed, keep_a, send_a = mlp_both_ways(
        index, tokens, cotangent, mixed, vectors, ff, outer
    )
    backward = functools.partial(
        attention_backward, index, tokens, projected, normed, full_qkv, vectors
    )
    images, half = tokens.shape[0], width // 2
    if swaps:
        got_a = plan.over_core(send_a)
        input_grad, *sums = backward(d_mixed, d_middle, 0, 2)
        sums, got_a = after(sums, got_a)
        parts_a, stay_a = plan.scatter(keep_a, got_a)
        sums, parts_a = after(sums, parts_a)
        more_a = plan.send(parts_a)
        input_grad, keep_c, send_c = backward(
            d_mixed, d_middle, 2, images, (*sums, input_grad)
        )
        send_c, more_a = after(send_c, more_a)
        got_c = plan.over_core(send_c)
        sum_a = stay_a + more_a[0] + more_a[1] + more_a[2]
        low_a, high_a = plan.half(sum_a, plan.z), plan.half(sum_a, 1 - plan.z)
        over_a = plan.over_z(high_a, 1)
        got_c = behind(got_c, low_a, high_a)
        parts_c, stay_c = plan.scatter(keep_c, got_c)
        over_a = behind(over_a, parts_c)
        more_c = plan.send(parts_c)
        low_a = low_a + over_a
        over_a = plan.over_z(low_a, 2)
        more_c = behind(more_c, low_a)
        sum_c = stay_c + more_c[0] + more_c[1] + more_c[2]
        over_a = behind(over_a, sum_c)
        over_c = plan.over_z(sum_c, 1)
        low_a = low_a + over_a
        over_a = plan.over_z(low_a, 1)
        over_c = behind(over_c, low_a)
        sum_c = sum_c + over_c
        over_a = behind(over_a, sum_c)
        over_c = plan.over_z(sum_c, 2)
        sum_a = jnp.concatenate([low_a, over_a])
        across_a, beside_a = plan.over_y(sum_a), plan.over_core(sum_a)
        output, input_grad = settled(output), settled(input_grad)
        over_c, output, input_grad = behind((over_c, output, input_grad), sum_a)
        output, input_grad = output.transpose(1, 0, 2), input_grad.transpose(1, 0, 2)
        sum_c = sum_c + over_c
        across_a = behind(across_a, sum_c)
        pieces_c = (sum_c, plan.over_y(sum_c), plan.over_core(sum_c), plan.over_y_and_core(sum_c))
        pieces_a = (sum_a, across_a, beside_a, plan.over_core(across_a))
        outer_grads = unpack(
            unpack_outer_kernel,
            "unpack_outer",
            index,
            pieces_a,
            [(ff // 2, width), (half, ff), (half, width)] + [(half,)] * 4 + [(ff // 2,)],
        )
        g_drop, g_lift, g_out, g_out_bias, g_gain_two, g_shift_two, g_drop_bias, g_lift_bias = (
            outer_grads
        )
        pieces_c = behind(pieces_c, g_drop)
        g_qkv, g_query, g_value, g_gain_one, g_shift_one = unpack(
            unpack_inner_kernel,
            "unpack_inner",
            index,
            pieces_c,
            [(half, 3 * width)] + [(half,)] * 4,
        )
    else:
        input_grad, *sums = backward(d_mixed, d_middle, 0, images - 2)
        input_grad, keep_c, send_c = backward(
            d_mixed, d_middle, images - 2, images, (*sums, input_grad)
        )
        deep, tall, small = ff // 4, width // 4, width // 8
        eighths = in_order(keep_a, send_a)
        g_drop = plan.reduce(jnp.concatenate([q[0][:deep] for q in eighths]))
        g_lift = plan.reduce(
            jnp.concatenate(
                [
                    jnp.concatenate(
                        [q[1][k * tall : (k + 1) * tall] for k in range(ff // width)], axis=1
                    )
                    for q in eighths
                ]
            )
        )
        g_out = plan.reduce(
            jnp.concatenate([side[deep : deep + small] for q in eighths for side in q])
        )
        rows = eighths[0][0][deep + small : deep + small + 8]
        g_out_bias, g_gain_two, g_shift_two, g_drop_bias = (plan.reduce(rows[i]) for i in range(4))
        g_lift_bias = plan.reduce(rows[4:].reshape(-1))
        eighths = in_order(keep_c, send_c)
        g_qkv = plan.reduce(
            jnp.concatenate(
                [
                    jnp.concatenate([side[k * small : (k + 1) * small] for k in range(3)], axis=1)
                    for q in eighths
                    for side in q
                ]
            )
        )
        rows = eighths[0][0][3 * small :]
        g_query, g_value, g_gain_one, g_shift_one = (plan.reduce(rows[i]) for i in range(4))
    return (
        output,
        input_grad,
        g_gain_one,
        g_shift_one,
        g_qkv,
        g_query,
        g_value,
        g_out,
        g_out_bias,
        g_gain_two,
        g_shift_two,
        g_lift,
        g_lift_bias,
        g_drop,
        g_drop_bias,
    )


def solution(mesh):
    spread = P(("rep", "fsdp"), None, None)
    vector, matrix = P("fsdp"), P("fsdp", None)
    in_specs = (
        spread,
        vector,
        vector,
        matrix,
        vector,
        vector,
        matrix,
        vector,
        vector,
        vector,
        matrix,
        vector,
        matrix,
        vector,
        spread,
    )
    out_specs = (
        spread,
        spread,
        vector,
        vector,
        matrix,
        vector,
        vector,
        matrix,
        vector,
        vector,
        vector,
        matrix,
        vector,
        matrix,
        vector,
    )
    swaps = mesh.shape["rep"] == 16 and mesh.shape["fsdp"] == 2
    return jax.shard_map(
        functools.partial(per_device, swaps=swaps),
        mesh=mesh,
        in_specs=in_specs,
        out_specs=out_specs,
        check_vma=False,
    )
```

```python
import functools

import jax
import jax.numpy as jnp
from jax import lax
from jax.experimental import pallas as pl
from jax.experimental.layout import Layout, with_layout_constraint
from jax.experimental.pallas import tpu as pltpu
from jax.sharding import PartitionSpec as P

HEADS = 6
HEAD_DIM = 64
PAIR = 2 * HEAD_DIM
LANE = 128
EPS = 1e-06
ROOT_HALF = 0.7071067811865476
GAUSS = 0.3989422804014327
LOG2E = 1.4426950408889634
SCALE = HEAD_DIM ** (-0.5)
F32 = jnp.float32
BF16 = jnp.bfloat16


def nn(a, b):
    return lax.dot_general(a, b, (((1,), (0,)), ((), ())), preferred_element_type=F32)


def nt(a, b):
    return lax.dot_general(a, b, (((1,), (1,)), ((), ())), preferred_element_type=F32)


def tn(a, b):
    return lax.dot_general(a, b, (((0,), (0,)), ((), ())), preferred_element_type=F32)


def normalise(v):
    mean = jnp.mean(v, axis=-1, keepdims=True)
    centred = v - mean
    var = jnp.mean(centred * centred, axis=-1, keepdims=True)
    inverse = lax.rsqrt(var + EPS)
    return centred * inverse, inverse


def norm_back(grad, normal, inverse, gain):
    scaled = grad * gain
    return inverse * (
        scaled
        - jnp.mean(scaled, axis=-1, keepdims=True)
        - normal * jnp.mean(scaled * normal, axis=-1, keepdims=True)
    )


def fold(v):
    return jnp.sum(v.reshape(v.shape[0] // 8, 8, v.shape[1]), axis=0)


def pad_rows(scratch, ref, length):
    for j in range(ref.shape[0]):
        scratch[j, 0:length, :] = ref[j].astype(scratch.dtype)


def zero_tail(scratch, length):
    images, rows, columns = scratch.shape
    low = (length // 16) * 16
    scratch[:, low:rows, :] = jnp.zeros((images, rows - low, columns), scratch.dtype)


def split_pair(v):
    first = lax.broadcasted_iota(jnp.int32, v.shape, 1) < HEAD_DIM
    zero = jnp.zeros_like(v)
    return jnp.concatenate([jnp.where(first, v, zero), jnp.where(first, zero, v)], axis=0)


def join_pair(v):
    rows = v.shape[0] // 2
    first = lax.broadcasted_iota(jnp.int32, (rows, PAIR), 1) < HEAD_DIM
    return jnp.where(first, v[:rows], v[rows:])


def join_pieces(full, own, near, far, index, first=0):
    block = own.shape[0]
    half = block // 2
    x, core = index[0], index[1]
    other = (1 - x) * block
    full[pl.ds(pl.multiple_of(x * block, 16), block), :] = own[...]
    full[pl.ds(pl.multiple_of(other + core * half, 16), half), :] = near[first : first + half, :]
    full[pl.ds(pl.multiple_of(other + (1 - core) * half, 16), half), :] = far[first : first + half, :]


def quarters(index, keep, send):
    x, core, y = index[0], index[1], index[2]
    for dest, owner in ((keep, core), (send, 1 - core)):
        for slot, half in ((0, x), (1, 1 - x)):
            for side in range(2):
                yield dest.at[slot, jnp.where(y == side, 0, 1)], half, owner, side


def pack_first_kernel(index, *refs):
    vectors, lift_bias, weight, packed = refs[:8], *refs[8:]
    half = weight.shape[0] // 2
    shard, width = vectors[0].shape[0], weight.shape[1] // 3
    packed[0:half, :] = weight[pl.ds(pl.multiple_of(index[1] * half, 16), half), :]
    packed[half:, :] = jnp.zeros((8, 3 * width), BF16)
    for i, ref in enumerate(vectors):
        row = ref[...].astype(F32).reshape(1, shard)
        packed[half + i : half + i + 1, 0:shard] = row.astype(BF16)
    bias = lift_bias[...].astype(F32).reshape(1, lift_bias.shape[0]).astype(BF16)
    for k in range(lift_bias.shape[0] // width):
        packed[half + k : half + k + 1, width : 2 * width] = bias[:, k * width : (k + 1) * width]


def pack_rest_kernel(index, out_own, lift_own, drop_own, lift_half, both_half):
    tall, deep = lift_half.shape[0], drop_own.shape[0] // 2
    rows_of = pl.ds(pl.multiple_of(index[1] * tall, 16), tall)
    lift_half[...] = lift_own[rows_of, :]
    both_half[0:deep, :] = drop_own[pl.ds(pl.multiple_of(index[1] * deep, 16), deep), :]
    both_half[deep:, :] = out_own[rows_of, :]


def join_vectors(vec_ref, own, other, index):
    width = vec_ref.shape[1]
    half = width // 2
    mine, theirs = own[-8:, :].astype(F32), other[-8:, :].astype(F32)
    first = index[0] == 0
    low, high = jnp.where(first, mine, theirs), jnp.where(first, theirs, mine)
    vec_ref[0:8, :] = jnp.concatenate([low[:, :half], high[:, :half]], axis=1)
    blocks = vec_ref.shape[0] // 2 - 4
    vec_ref[8 : 8 + blocks, :] = low[:blocks, width : 2 * width]
    vec_ref[8 + blocks :, :] = high[:blocks, width : 2 * width]


def attend_kernel(
    length,
    index,
    tok_ref,
    packed,
    own,
    near,
    far,
    normed_ref,
    proj_ref,
    mixed_ref,
    w_ref,
    vec_ref,
    n_s,
):
    images, rows, width = n_s.shape

    @pl.when(pl.program_id(0) == 0)
    def _():
        zero_tail(n_s, length)
        join_pieces(w_ref, own, near, far, index)
        join_vectors(vec_ref, packed, near, index)

    gain, shift = vec_ref[0:1, :], vec_ref[1:2, :]
    bias = jnp.concatenate([vec_ref[2:3, :], jnp.zeros((1, width), F32), vec_ref[3:4, :]], axis=1)
    for j in range(images):
        normal, _ = normalise(tok_ref[j].astype(F32))
        n_s[j, 0:length, :] = (normal * gain + shift).astype(BF16)
    normed_ref[...] = n_s[...]
    flat = n_s[...].reshape(images * rows, width)
    proj_ref[...] = (nn(flat, w_ref[...]) + bias).astype(BF16).reshape(images, rows, 3 * width)
    live = lax.broadcasted_iota(jnp.int32, (2 * rows, rows), 1) < length
    ones = jnp.ones((rows, PAIR), BF16)
    for j in range(images):
        for c in range(0, width, PAIR):
            query = split_pair(proj_ref[j, :, c : c + PAIR] * jnp.asarray(SCALE, BF16))
            key = proj_ref[j, :, width + c : width + c + PAIR]
            value = proj_ref[j, :, 2 * width + c : 2 * width + c + PAIR]
            scores = jnp.where(live, nt(query, key), -1e30)
            top = jnp.max(scores, axis=-1, keepdims=True)
            weights = jnp.exp(scores - top).astype(BF16)
            both = nn(weights, jnp.concatenate([value, ones], axis=1))
            mixed_ref[j, :, c : c + PAIR] = join_pair(both[:, :PAIR] / both[:, PAIR:]).astype(BF16)


def mlp_kernel(
    length,
    chunk,
    index,
    tok_ref,
    cot_ref,
    mixed_ref,
    vec_ref,
    out_own,
    lift_own,
    drop_own,
    lift_near,
    lift_far,
    both_near,
    both_far,
    out_ref,
    d_middle_ref,
    d_mixed_ref,
    keep,
    send,
    x_s,
    z_s,
    w_out_ref,
    w_lift_ref,
    w_drop_ref,
    lift_bias_ref,
    a_drop,
    a_lift,
    a_out,
    a_vec,
    a_bias,
):
    step = pl.program_id(0)
    images, rows, width = x_s.shape
    total = images * rows
    hidden_width = w_lift_ref.shape[1]

    @pl.when(step == 0)
    def _():
        zero_tail(x_s, length)
        zero_tail(z_s, length)
        deep = drop_own.shape[0] // 2
        join_pieces(w_out_ref, out_own, both_near, both_far, index, deep)
        join_pieces(w_lift_ref, lift_own, lift_near, lift_far, index)
        join_pieces(w_drop_ref, drop_own, both_near, both_far, index)
        for k in range(hidden_width // width):
            lift_bias_ref[:, k * width : (k + 1) * width] = vec_ref[8 + k : 9 + k, :]
        for acc in (a_drop, a_lift, a_out, a_vec, a_bias):
            acc[...] = jnp.zeros_like(acc)

    pad_rows(x_s, tok_ref, length)
    pad_rows(z_s, cot_ref, length)
    out_bias, gain, shift, drop_bias = (vec_ref[i : i + 1, :] for i in range(4, 8))
    mixed = mixed_ref[...].reshape(total, width)
    dz = z_s[...].reshape(total, width)
    dz_f = dz.astype(F32)
    middle = x_s[...].reshape(total, width).astype(F32) + nn(mixed, w_out_ref[...]) + out_bias
    normal, inverse = normalise(middle)
    normed = (normal * gain + shift).astype(BF16)
    result = middle + drop_bias
    d_normed = jnp.zeros((total, width), F32)
    for c in range(0, hidden_width, chunk):
        part = slice(c, c + chunk)
        hidden = nn(normed, w_lift_ref[:, part]) + lift_bias_ref[:, part]
        cdf = 0.5 + 0.5 * lax.erf(hidden * ROOT_HALF)
        bell = jnp.exp(hidden * hidden * -0.5) * GAUSS
        active = (hidden * cdf).astype(BF16)
        d_active = nt(dz, w_drop_ref[part, :])
        d_hidden_f = d_active * (cdf + hidden * bell)
        d_hidden = d_hidden_f.astype(BF16)
        result = result + nn(active, w_drop_ref[part, :])
        d_normed = d_normed + nt(d_hidden, w_lift_ref[:, part])
        a_drop[part, :] += tn(active, dz)
        a_lift[:, part] += tn(normed, d_hidden)
        a_bias[:, part] += fold(d_hidden.astype(F32))
    out = result.astype(BF16)
    for j in range(images):
        out_ref[j] = out[j * rows : j * rows + length]
    d_middle = dz_f + norm_back(d_normed, normal, inverse, gain)
    d_middle_ref[...] = d_middle.reshape(images, rows, width)
    d_attended = d_middle.astype(BF16)
    d_mixed_ref[...] = nt(d_attended, w_out_ref[...]).astype(BF16).reshape(images, rows, width)
    a_out[...] += tn(mixed, d_attended)
    a_vec[0] += fold(d_attended.astype(F32))
    a_vec[1] += fold(d_normed * normal)
    a_vec[2] += fold(d_normed)
    a_vec[3] += fold(dz_f)

    @pl.when(step == pl.num_programs(0) - 1)
    def _():
        columns = jnp.sum(a_bias[...], axis=0, keepdims=True)
        vectors = jnp.concatenate(
            [jnp.sum(a_vec[...], axis=1)]
            + [columns[:, c : c + width] for c in range(0, hidden_width, width)],
            axis=0,
        ).astype(BF16)
        deep, tall, small = hidden_width // 4, width // 4, width // 8
        for place, half, core, side in quarters(index, keep, send):
            quarter = 2 * half + core
            if side == 0:
                first = pl.multiple_of(quarter * deep, 8)
                place[0:deep, :] = a_drop[pl.ds(first, deep), :].astype(BF16)
                place[deep + small : deep + small + 8, :] = vectors
                place[deep + small + 8 :, :] = jnp.zeros((8, width), BF16)
            else:
                rows_of = pl.ds(pl.multiple_of(quarter * tall, 8), tall)
                for k in range(hidden_width // width):
                    place[k * tall : (k + 1) * tall, :] = a_lift[
                        rows_of, k * width : (k + 1) * width
                    ].astype(BF16)
                place[deep + small :, :] = jnp.zeros((16, width), BF16)
            first = pl.multiple_of(quarter * tall + side * small, 8)
            place[deep : deep + small, :] = a_out[pl.ds(first, small), :].astype(BF16)


def attention_back(length, proj_ref, d_mixed_ref, d_s):
    images, rows, wide = d_s.shape
    width = wide // 3
    live = lax.broadcasted_iota(jnp.int32, (rows, 2 * rows), 0) < length
    for j in range(images):
        for c in range(0, width, PAIR):
            query = split_pair(proj_ref[j, :, c : c + PAIR] * jnp.asarray(SCALE, BF16))
            key = proj_ref[j, :, width + c : width + c + PAIR]
            value = proj_ref[j, :, 2 * width + c : 2 * width + c + PAIR]
            d_mixed = split_pair(d_mixed_ref[j, :, c : c + PAIR])
            scores = jnp.where(live, nt(key, query), -1e30)
            top = jnp.max(scores, axis=0, keepdims=True)
            weights = jnp.exp(scores - top)
            probs = weights * (1.0 / jnp.sum(weights, axis=0, keepdims=True))
            d_probs = nt(value, d_mixed)
            delta = jnp.sum(probs * d_probs, axis=0, keepdims=True)
            d_scores = (probs * (d_probs - delta)).astype(BF16)
            d_value = nn(probs.astype(BF16), d_mixed)
            d_key = nn(d_scores, query)
            d_query = join_pair(tn(d_scores, key)) * SCALE
            d_s[j, :, c : c + PAIR] = d_query.astype(BF16)
            d_s[j, :, width + c : width + c + PAIR] = d_key.astype(BF16)
            d_s[j, :, 2 * width + c : 2 * width + c + PAIR] = d_value.astype(BF16)


def back_kernel(
    length,
    index,
    tok_ref,
    proj_ref,
    normed_ref,
    d_mixed_ref,
    d_middle_ref,
    w_ref,
    vec_ref,
    head_ref,
    in_grad_ref,
    keep,
    send,
    a_qkv,
    a_proj,
    a_vec,
    d_s,
):
    step = pl.program_id(0)
    images, rows, wide = d_s.shape
    width = wide // 3
    total = images * rows

    @pl.when(step == 0)
    def _():
        for acc in (a_qkv, a_proj, a_vec):
            acc[...] = jnp.zeros_like(acc)
        d_s[...] = head_ref[...]

    @pl.when(step > 0)
    def _():
        attention_back(length, proj_ref, d_mixed_ref, d_s)

    d_proj = d_s[...].reshape(total, wide)
    a_qkv[...] += tn(normed_ref[...].reshape(total, width), d_proj)
    a_proj[...] += fold(d_proj.astype(F32))
    d_normed = nt(d_proj, w_ref[...])
    gain = vec_ref[0:1, :]
    for j in range(images):
        normal, inverse = normalise(tok_ref[j].astype(F32))
        grad = d_normed[j * rows : j * rows + length]
        in_grad_ref[j] = (
            d_middle_ref[j, 0:length, :] + norm_back(grad, normal, inverse, gain)
        ).astype(BF16)
        a_vec[0:1, :] += jnp.sum(grad * normal, axis=0, keepdims=True)
        a_vec[1:2, :] += jnp.sum(grad, axis=0, keepdims=True)

    @pl.when(step == pl.num_programs(0) - 1)
    def _():
        columns = jnp.sum(a_proj[...], axis=0, keepdims=True)
        vectors = jnp.concatenate(
            [columns[:, :width], columns[:, 2 * width :], a_vec[...], jnp.zeros((4, width), F32)],
            axis=0,
        ).astype(BF16)
        small = width // 8
        for place, half, core, side in quarters(index, keep, send):
            first_row = pl.multiple_of((2 * half + core) * 2 * small + side * small, 8)
            for k in range(3):
                place[k * small : (k + 1) * small, :] = a_qkv[
                    pl.ds(first_row, small), k * width : (k + 1) * width
                ].astype(BF16)
            place[3 * small :, :] = vectors


def placed(full, index, pieces, by_z=False):
    core, y = index[1], index[2]
    spots = ((core, y), (core, 1 - y), (1 - core, y), (1 - core, 1 - y))
    rows = pieces[0].shape[0]
    for (owner, side), piece in zip(spots, pieces):
        if by_z:
            half = rows // 2
            for k, z in ((0, index[3]), (1, 1 - index[3])):
                full[owner, side, pl.ds(pl.multiple_of(z * half, 8), half), :] = piece[
                    k * half : (k + 1) * half, :
                ].astype(F32)
        else:
            full[owner, side] = piece[...].astype(F32)


def own_half(index, row):
    half = row.shape[-1] // 2
    return jnp.where(index[0] == 0, row[:, :half], row[:, half:])[0]


def unpack_outer_kernel(index, *refs):
    g_drop, g_lift, g_out, g_out_bias, g_gain, g_shift, g_drop_bias, g_lift_bias, full = refs[4:]
    placed(full, index, refs[:4], by_z=True)
    width = g_out.shape[1]
    deep, tall, small = g_drop.shape[0] // 2, width // 4, width // 8
    blocks = g_lift.shape[1] // width
    for core in range(2):
        g_drop[core * deep : (core + 1) * deep, :] = full[core, 0, 0:deep, :]
        for k in range(blocks):
            g_lift[core * tall : (core + 1) * tall, k * width : (k + 1) * width] = full[
                core, 1, k * tall : (k + 1) * tall, :
            ]
        for side in range(2):
            first = core * tall + side * small
            g_out[first : first + small, :] = full[core, side, deep : deep + small, :]
    vectors = full[0, 0, deep + small :, :]
    for i, ref in enumerate((g_out_bias, g_gain, g_shift, g_drop_bias)):
        ref[...] = own_half(index, vectors[i : i + 1, :])
    for k in range(blocks // 2):
        row = jnp.where(
            index[0] == 0,
            vectors[4 + k : 5 + k, :],
            vectors[4 + blocks // 2 + k : 5 + blocks // 2 + k, :],
        )
        g_lift_bias[k * width : (k + 1) * width] = row[0]


def unpack_inner_kernel(index, *refs):
    g_qkv, g_query, g_value, g_gain, g_shift, full = refs[4:]
    placed(full, index, refs[:4])
    width = full.shape[3]
    small = width // 8
    for core in range(2):
        for side in range(2):
            first = (2 * core + side) * small
            for k in range(3):
                g_qkv[first : first + small, k * width : (k + 1) * width] = full[
                    core, side, k * small : (k + 1) * small, :
                ]
    vectors = full[0, 0, 3 * small :, :]
    for i, ref in enumerate((g_query, g_value, g_gain, g_shift)):
        ref[...] = own_half(index, vectors[i : i + 1, :])


VMEM_LIMIT = 67043328
PARAMS = pltpu.CompilerParams(vmem_limit_bytes=VMEM_LIMIT)
SCALARS = pl.BlockSpec(memory_space=pltpu.SMEM)


def whole(*shape):
    return pl.BlockSpec(shape, lambda i: (0,) * len(shape))


def whole_like(arrays):
    return [whole(*a.shape) for a in arrays]


def per_step(*shape):
    return pl.BlockSpec(shape, lambda i: (i,) + (0,) * (len(shape) - 1))


def shape_of(dtype, *shape):
    return jax.ShapeDtypeStruct(shape, dtype)


def cost(microseconds):
    return pl.CostEstimate(flops=int(microseconds * 1e3), bytes_accessed=1, transcendentals=0)


def pack_first(index, vectors, lift_bias, weight):
    rows, columns = weight.shape
    return pl.pallas_call(
        pack_first_kernel,
        grid=(1,),
        in_specs=[SCALARS, *whole_like((*vectors, lift_bias, weight))],
        out_specs=whole(rows // 2 + 8, columns),
        out_shape=shape_of(BF16, rows // 2 + 8, columns),
        compiler_params=PARAMS,
        cost_estimate=cost(1),
        name="pack_first",
    )(index, *vectors, lift_bias, weight)


def pack_rest(index, weights):
    out_weight, lift_weight, drop_weight = weights
    tall, width = out_weight.shape[0] // 2, out_weight.shape[1]
    shapes = [(tall, lift_weight.shape[1]), (drop_weight.shape[0] // 2 + tall, width)]
    return pl.pallas_call(
        pack_rest_kernel,
        grid=(1,),
        in_specs=[SCALARS, *whole_like(weights)],
        out_specs=[whole(*d) for d in shapes],
        out_shape=[shape_of(BF16, *d) for d in shapes],
        compiler_params=PARAMS,
        cost_estimate=cost(1),
        name="pack_rest",
    )(index, *weights)


def forward_attention(index, tokens, ff, packed, pieces):
    images, length, width = tokens.shape
    rows = -(-length // 16) * 16
    group = 4 if images % 4 == 0 else 1
    return pl.pallas_call(
        functools.partial(attend_kernel, length),
        grid=(images // group,),
        in_specs=[SCALARS, per_step(group, length, width), *whole_like((packed, *pieces))],
        out_specs=[
            per_step(group, rows, width),
            per_step(group, rows, 3 * width),
            per_step(group, rows, width),
            whole(width, 3 * width),
            whole(8 + ff // width, width),
        ],
        out_shape=[
            shape_of(BF16, images, rows, width),
            shape_of(BF16, images, rows, 3 * width),
            shape_of(BF16, images, rows, width),
            shape_of(BF16, width, 3 * width),
            shape_of(F32, 8 + ff // width, width),
        ],
        scratch_shapes=[pltpu.VMEM((group, rows, width), BF16)],
        compiler_params=PARAMS,
        cost_estimate=cost(1),
        name="attend",
    )(index, tokens, packed, *pieces)


def mlp_both_ways(index, tokens, cotangent, mixed, vectors, ff, pieces):
    images, length, width = tokens.shape
    rows = mixed.shape[1]
    group = 2 if images % 2 == 0 else 1
    eighth = (2, 2, ff // 4 + width // 8 + 16, width)
    return pl.pallas_call(
        functools.partial(mlp_kernel, length, 512),
        grid=(images // group,),
        in_specs=[
            SCALARS,
            per_step(group, length, width),
            per_step(group, length, width),
            per_step(group, rows, width),
            *whole_like((vectors, *pieces)),
        ],
        out_specs=[
            per_step(group, length, width),
            per_step(group, rows, width),
            per_step(group, rows, width),
            whole(*eighth),
            whole(*eighth),
        ],
        out_shape=[
            shape_of(BF16, images, length, width),
            shape_of(F32, images, rows, width),
            shape_of(BF16, images, rows, width),
            shape_of(BF16, *eighth),
            shape_of(BF16, *eighth),
        ],
        scratch_shapes=[
            pltpu.VMEM((group, rows, width), BF16),
            pltpu.VMEM((group, rows, width), BF16),
            pltpu.VMEM((width, width), BF16),
            pltpu.VMEM((width, ff), BF16),
            pltpu.VMEM((ff, width), BF16),
            pltpu.VMEM((1, ff), F32),
            pltpu.VMEM((ff, width), F32),
            pltpu.VMEM((width, ff), F32),
            pltpu.VMEM((width, width), F32),
            pltpu.VMEM((4, 8, width), F32),
            pltpu.VMEM((8, ff), F32),
        ],
        compiler_params=PARAMS,
        cost_estimate=cost(1),
        name="mlp",
    )(index, tokens, cotangent, mixed, vectors, *pieces)


def backward_head(projected, d_mixed, length):
    images, rows, wide = projected.shape
    group = 2 if images % 2 == 0 else 1
    return pl.pallas_call(
        functools.partial(attention_back, length),
        grid=(1,),
        in_specs=[per_step(group, rows, wide), per_step(group, rows, wide // 3)],
        out_specs=per_step(group, rows, wide),
        out_shape=shape_of(BF16, group, rows, wide),
        compiler_params=PARAMS,
        cost_estimate=cost(1),
        name="back_head",
    )(projected, d_mixed)


def backward(index, tokens, projected, normed, w_qkv, vectors, d_mixed, d_middle, head):
    images, length, width = tokens.shape
    group, rows, wide = head.shape
    chunk = (2, 2, 3 * width // 8 + 8, width)
    return pl.pallas_call(
        functools.partial(back_kernel, length),
        grid=(images // group,),
        in_specs=[
            SCALARS,
            per_step(group, length, width),
            per_step(group, rows, wide),
            per_step(group, rows, width),
            per_step(group, rows, width),
            per_step(group, rows, width),
            *whole_like((w_qkv, vectors, head)),
        ],
        out_specs=[per_step(group, length, width)] + [whole(*chunk)] * 2,
        out_shape=[shape_of(BF16, images, length, width)] + [shape_of(BF16, *chunk)] * 2,
        scratch_shapes=[
            pltpu.VMEM((width, wide), F32),
            pltpu.VMEM((8, wide), F32),
            pltpu.VMEM((2, width), F32),
            pltpu.VMEM((group, rows, wide), BF16),
        ],
        compiler_params=PARAMS,
        cost_estimate=cost(1),
        name="back",
    )(index, tokens, projected, normed, d_mixed, d_middle, w_qkv, vectors, head)


def unpack(kernel, name, index, pieces, shapes):
    return pl.pallas_call(
        kernel,
        grid=(1,),
        in_specs=[SCALARS, *whole_like(pieces)],
        out_specs=[whole(*d) for d in shapes],
        out_shape=[shape_of(F32, *d) for d in shapes],
        scratch_shapes=[pltpu.VMEM((2, 2) + pieces[0].shape, F32)],
        compiler_params=PARAMS,
        cost_estimate=cost(1),
        name=name,
    )(index, *pieces)


AXES = ("rep", "fsdp")


class Butterfly:
    def __init__(self):
        rep, x = lax.axis_index("rep"), lax.axis_index("fsdp")
        self.z = (rep >> 2) & 1
        self.index = jnp.stack([x, rep & 1, (rep >> 1) & 1, self.z]).astype(jnp.int32)

    def swap(self, v, rep_mask, x_mask=0):
        pairs = [
            (rep * 2 + x, (rep ^ rep_mask) * 2 + (x ^ x_mask)) for rep in range(16) for x in range(2)
        ]
        return lax.ppermute(v, AXES, pairs)

    def over_x(self, v):
        return self.swap(v, 0, 1)

    def over_core(self, v):
        return self.swap(v, 1)

    def over_y(self, v):
        return self.swap(v, 2)

    def over_z(self, v, mask):
        return self.swap(v, 4 * mask)

    def over_corner(self, v):
        return self.swap(v, 2, 1)

    def over_y_and_core(self, v):
        return self.swap(v, 3)

    def half(self, v, which):
        rows = v.shape[0] // 2
        return lax.dynamic_slice_in_dim(v, which * rows, rows, 0)

    def scatter(self, keep, got):
        total = [[keep[i, j] + got[i, j] for j in range(2)] for i in range(2)]
        return (total[1][0], total[0][1], total[1][1]), total[0][0]

    def send(self, parts):
        return self.over_x(parts[0]), self.over_y(parts[1]), self.over_corner(parts[2])


class Collective:
    def __init__(self):
        self.index = jnp.zeros((4,), jnp.int32)

    def gather_weight(self, own):
        full = lax.all_gather(own, "fsdp", axis=0, tiled=True)
        quarter = full.shape[0] // 4
        return full[: 2 * quarter], full[2 * quarter : 3 * quarter], full[3 * quarter :]

    def gather_vectors(self, vectors, lift_bias):
        whole_vectors = [lax.all_gather(v, "fsdp", axis=0, tiled=True) for v in vectors]
        whole_bias = lax.all_gather(lift_bias, "fsdp", axis=0, tiled=True)
        width = whole_vectors[0].shape[0]
        table = jnp.stack(whole_vectors).reshape(8, 2, width // 2)
        bias = whole_bias.reshape(2, -1, width)
        return (
            jnp.zeros((2, 8, 3 * width), BF16)
            .at[:, :, : width // 2]
            .set(table.transpose(1, 0, 2))
            .at[:, : bias.shape[1], width : 2 * width]
            .set(bias)
        )

    def reduce(self, v):
        owned = lax.psum_scatter(v.astype(BF16), "fsdp", scatter_dimension=0, tiled=True)
        return lax.psum(owned, "rep").astype(F32)


def after(*arrays):
    return lax.optimization_barrier(arrays)


def behind(arrays, *others):
    return lax.optimization_barrier((arrays, others))[0]


def settled(v):
    return with_layout_constraint(v.transpose(1, 0, 2), Layout(major_to_minor=(0, 1, 2)))


def in_order(keep, send):
    return [(q[0], q[1]) for q in (keep[0], send[0], keep[1], send[1])]


def per_device(
    tokens,
    gain_one,
    shift_one,
    qkv_weight,
    query_bias,
    value_bias,
    out_weight,
    out_bias,
    gain_two,
    shift_two,
    lift_weight,
    lift_bias,
    drop_weight,
    drop_bias,
    cotangent,
    swaps,
):
    length, width = tokens.shape[1:]
    plan = Butterfly() if swaps else Collective()
    index = plan.index
    small = (
        gain_one,
        shift_one,
        query_bias,
        value_bias,
        out_bias,
        gain_two,
        shift_two,
        drop_bias,
    )
    ff = lift_weight.shape[1]
    rest = (out_weight, lift_weight, drop_weight)
    if swaps:
        packed = pack_first(index, small, lift_bias, qkv_weight)
        tokens = with_layout_constraint(tokens, Layout(major_to_minor=(0, 1, 2)))
        near = behind(plan.over_x(packed), tokens)
        qkv = (qkv_weight, near, plan.over_core(near))
        rest_then, packed = after(rest, packed)
        nears = [plan.over_x(half) for half in pack_rest(index, rest_then)]
    else:
        packed, theirs = plan.gather_vectors(small, lift_bias)
        own, near, far = plan.gather_weight(qkv_weight)
        qkv = (own, jnp.concatenate([near, theirs]), far)
    normed, projected, mixed, full_qkv, vectors = forward_attention(
        index, tokens, ff, packed, qkv
    )
    if swaps:
        mixed, nears = after(mixed, nears)
        pieces = [piece for near in nears for piece in (near, plan.over_core(near))]
    else:
        (out_own, *outs), (lift_own, *lifts), (drop_own, *drops) = map(plan.gather_weight, rest)
        rest = (out_own, lift_own, drop_own)
        pieces = [*lifts, *(jnp.concatenate(both) for both in zip(drops, outs))]
    outer = (*rest, *pieces)
    output, d_middle, d_mixed, keep_a, send_a = mlp_both_ways(
        index, tokens, cotangent, mixed, vectors, ff, outer
    )
    head = backward_head(projected, d_mixed, length)
    rest_of_backward = functools.partial(
        backward, index, tokens, projected, normed, full_qkv, vectors, d_mixed, d_middle
    )
    half = width // 2
    if swaps:
        got_a = plan.over_core(send_a)
        head, got_a = after(head, got_a)
        parts_a, stay_a = plan.scatter(keep_a, got_a)
        head, parts_a = after(head, parts_a)
        more_a = plan.send(parts_a)
        input_grad, keep_c, send_c = rest_of_backward(head)
        send_c, more_a = after(send_c, more_a)
        got_c = plan.over_core(send_c)
        sum_a = stay_a + more_a[0] + more_a[1] + more_a[2]
        low_a, high_a = plan.half(sum_a, plan.z), plan.half(sum_a, 1 - plan.z)
        over_a = plan.over_z(high_a, 1)
        got_c = behind(got_c, low_a, high_a)
        parts_c, stay_c = plan.scatter(keep_c, got_c)
        over_a = behind(over_a, parts_c)
        more_c = plan.send(parts_c)
        low_a = low_a + over_a
        over_a = plan.over_z(low_a, 2)
        more_c = behind(more_c, low_a)
        sum_c = stay_c + more_c[0] + more_c[1] + more_c[2]
        over_a = behind(over_a, sum_c)
        over_c = plan.over_z(sum_c, 1)
        low_a = low_a + over_a
        over_a = plan.over_z(low_a, 1)
        over_c = behind(over_c, low_a)
        sum_c = sum_c + over_c
        over_a = behind(over_a, sum_c)
        over_c = plan.over_z(sum_c, 2)
        sum_a = jnp.concatenate([low_a, over_a])
        across_a, beside_a = plan.over_y(sum_a), plan.over_core(sum_a)
        output, input_grad = settled(output), settled(input_grad)
        over_c, output, input_grad = behind((over_c, output, input_grad), sum_a)
        output, input_grad = output.transpose(1, 0, 2), input_grad.transpose(1, 0, 2)
        sum_c = sum_c + over_c
        across_a = behind(across_a, sum_c)
        pieces_c = (sum_c, plan.over_y(sum_c), plan.over_core(sum_c), plan.over_y_and_core(sum_c))
        pieces_a = (sum_a, across_a, beside_a, plan.over_core(across_a))
        outer_grads = unpack(
            unpack_outer_kernel,
            "unpack_outer",
            index,
            pieces_a,
            [(ff // 2, width), (half, ff), (half, width)] + [(half,)] * 4 + [(ff // 2,)],
        )
        g_drop, g_lift, g_out, g_out_bias, g_gain_two, g_shift_two, g_drop_bias, g_lift_bias = (
            outer_grads
        )
        pieces_c = behind(pieces_c, g_drop)
        g_qkv, g_query, g_value, g_gain_one, g_shift_one = unpack(
            unpack_inner_kernel,
            "unpack_inner",
            index,
            pieces_c,
            [(half, 3 * width)] + [(half,)] * 4,
        )
    else:
        input_grad, keep_c, send_c = rest_of_backward(head)
        deep, tall, small = ff // 4, width // 4, width // 8
        eighths = in_order(keep_a, send_a)
        g_drop = plan.reduce(jnp.concatenate([q[0][:deep] for q in eighths]))
        g_lift = plan.reduce(
            jnp.concatenate(
                [
                    jnp.concatenate(
                        [q[1][k * tall : (k + 1) * tall] for k in range(ff // width)], axis=1
                    )
                    for q in eighths
                ]
            )
        )
        g_out = plan.reduce(
            jnp.concatenate([side[deep : deep + small] for q in eighths for side in q])
        )
        rows = eighths[0][0][deep + small : deep + small + 8]
        g_out_bias, g_gain_two, g_shift_two, g_drop_bias = (plan.reduce(rows[i]) for i in range(4))
        g_lift_bias = plan.reduce(rows[4:].reshape(-1))
        eighths = in_order(keep_c, send_c)
        g_qkv = plan.reduce(
            jnp.concatenate(
                [
                    jnp.concatenate([side[k * small : (k + 1) * small] for k in range(3)], axis=1)
                    for q in eighths
                    for side in q
                ]
            )
        )
        rows = eighths[0][0][3 * small :]
        g_query, g_value, g_gain_one, g_shift_one = (plan.reduce(rows[i]) for i in range(4))
    return (
        output,
        input_grad,
        g_gain_one,
        g_shift_one,
        g_qkv,
        g_query,
        g_value,
        g_out,
        g_out_bias,
        g_gain_two,
        g_shift_two,
        g_lift,
        g_lift_bias,
        g_drop,
        g_drop_bias,
    )


def solution(mesh):
    spread = P(("rep", "fsdp"), None, None)
    vector, matrix = P("fsdp"), P("fsdp", None)
    in_specs = (
        spread,
        vector,
        vector,
        matrix,
        vector,
        vector,
        matrix,
        vector,
        vector,
        vector,
        matrix,
        vector,
        matrix,
        vector,
        spread,
    )
    out_specs = (
        spread,
        spread,
        vector,
        vector,
        matrix,
        vector,
        vector,
        matrix,
        vector,
        vector,
        vector,
        matrix,
        vector,
        matrix,
        vector,
    )
    swaps = mesh.shape["rep"] == 16 and mesh.shape["fsdp"] == 2
    return jax.shard_map(
        functools.partial(per_device, swaps=swaps),
        mesh=mesh,
        in_specs=in_specs,
        out_specs=out_specs,
        check_vma=False,
    )
```

```python
import functools

import jax
import jax.numpy as jnp
from jax import lax
from jax.experimental import pallas as pl
from jax.experimental.layout import Layout, with_layout_constraint
from jax.experimental.pallas import tpu as pltpu
from jax.sharding import PartitionSpec as P

HEADS = 6
HEAD_DIM = 64
PAIR = 2 * HEAD_DIM
LANE = 128
EPS = 1e-06
ROOT_HALF = 0.7071067811865476
GAUSS = 0.3989422804014327
LOG2E = 1.4426950408889634
SCALE = HEAD_DIM ** (-0.5)
F32 = jnp.float32
BF16 = jnp.bfloat16


def nn(a, b):
    return lax.dot_general(a, b, (((1,), (0,)), ((), ())), preferred_element_type=F32)


def nt(a, b):
    return lax.dot_general(a, b, (((1,), (1,)), ((), ())), preferred_element_type=F32)


def tn(a, b):
    return lax.dot_general(a, b, (((0,), (0,)), ((), ())), preferred_element_type=F32)


def normalise(v):
    mean = jnp.mean(v, axis=-1, keepdims=True)
    centred = v - mean
    var = jnp.mean(centred * centred, axis=-1, keepdims=True)
    inverse = lax.rsqrt(var + EPS)
    return centred * inverse, inverse


def norm_back(grad, normal, inverse, gain):
    scaled = grad * gain
    return inverse * (
        scaled
        - jnp.mean(scaled, axis=-1, keepdims=True)
        - normal * jnp.mean(scaled * normal, axis=-1, keepdims=True)
    )


def fold(v):
    return jnp.sum(v.reshape(v.shape[0] // 8, 8, v.shape[1]), axis=0)


def pad_rows(scratch, ref, length):
    for j in range(ref.shape[0]):
        scratch[j, 0:length, :] = ref[j].astype(scratch.dtype)


def zero_tail(scratch, length):
    images, rows, columns = scratch.shape
    low = (length // 16) * 16
    scratch[:, low:rows, :] = jnp.zeros((images, rows - low, columns), scratch.dtype)


def split_pair(v):
    first = lax.broadcasted_iota(jnp.int32, v.shape, 1) < HEAD_DIM
    zero = jnp.zeros_like(v)
    return jnp.concatenate([jnp.where(first, v, zero), jnp.where(first, zero, v)], axis=0)


def join_pair(v):
    rows = v.shape[0] // 2
    first = lax.broadcasted_iota(jnp.int32, (rows, PAIR), 1) < HEAD_DIM
    return jnp.where(first, v[:rows], v[rows:])


def join_pieces(full, own, near, far, index, first=0):
    block = own.shape[0]
    half = block // 2
    x, core = index[0], index[1]
    other = (1 - x) * block
    full[pl.ds(pl.multiple_of(x * block, 16), block), :] = own[...]
    full[pl.ds(pl.multiple_of(other + core * half, 16), half), :] = near[first : first + half, :]
    full[pl.ds(pl.multiple_of(other + (1 - core) * half, 16), half), :] = far[first : first + half, :]


def quarters(index, keep, send):
    x, core, y = index[0], index[1], index[2]
    for dest, owner in ((keep, core), (send, 1 - core)):
        for slot, half in ((0, x), (1, 1 - x)):
            for side in range(2):
                yield dest.at[slot, jnp.where(y == side, 0, 1)], half, owner, side


def pack_first_kernel(index, *refs):
    vectors, lift_bias, weight, packed = refs[:8], *refs[8:]
    half = weight.shape[0] // 2
    shard, width = vectors[0].shape[0], weight.shape[1] // 3
    packed[0:half, :] = weight[pl.ds(pl.multiple_of(index[1] * half, 16), half), :]
    packed[half:, :] = jnp.zeros((8, 3 * width), BF16)
    for i, ref in enumerate(vectors):
        row = ref[...].astype(F32).reshape(1, shard)
        packed[half + i : half + i + 1, 0:shard] = row.astype(BF16)
    bias = lift_bias[...].astype(F32).reshape(1, lift_bias.shape[0]).astype(BF16)
    for k in range(lift_bias.shape[0] // width):
        packed[half + k : half + k + 1, width : 2 * width] = bias[:, k * width : (k + 1) * width]


def pack_rest_kernel(index, out_own, lift_own, drop_own, lift_half, both_half):
    tall, deep = lift_half.shape[0], drop_own.shape[0] // 2
    rows_of = pl.ds(pl.multiple_of(index[1] * tall, 16), tall)
    lift_half[...] = lift_own[rows_of, :]
    both_half[0:deep, :] = drop_own[pl.ds(pl.multiple_of(index[1] * deep, 16), deep), :]
    both_half[deep:, :] = out_own[rows_of, :]


def join_vectors(vec_ref, own, other, index):
    width = vec_ref.shape[1]
    half = width // 2
    mine, theirs = own[-8:, :].astype(F32), other[-8:, :].astype(F32)
    first = index[0] == 0
    low, high = jnp.where(first, mine, theirs), jnp.where(first, theirs, mine)
    vec_ref[0:8, :] = jnp.concatenate([low[:, :half], high[:, :half]], axis=1)
    blocks = vec_ref.shape[0] // 2 - 4
    vec_ref[8 : 8 + blocks, :] = low[:blocks, width : 2 * width]
    vec_ref[8 + blocks :, :] = high[:blocks, width : 2 * width]


def attend_kernel(
    length,
    index,
    tok_ref,
    packed,
    own,
    near,
    far,
    normed_ref,
    proj_ref,
    mixed_ref,
    w_ref,
    vec_ref,
    n_s,
):
    images, rows, width = n_s.shape

    @pl.when(pl.program_id(0) == 0)
    def _():
        zero_tail(n_s, length)
        join_pieces(w_ref, own, near, far, index)
        join_vectors(vec_ref, packed, near, index)

    gain, shift = vec_ref[0:1, :], vec_ref[1:2, :]
    bias = jnp.concatenate([vec_ref[2:3, :], jnp.zeros((1, width), F32), vec_ref[3:4, :]], axis=1)
    for j in range(images):
        normal, _ = normalise(tok_ref[j].astype(F32))
        n_s[j, 0:length, :] = (normal * gain + shift).astype(BF16)
    normed_ref[...] = n_s[...]
    flat = n_s[...].reshape(images * rows, width)
    proj_ref[...] = (nn(flat, w_ref[...]) + bias).astype(BF16).reshape(images, rows, 3 * width)
    live = lax.broadcasted_iota(jnp.int32, (2 * rows, rows), 1) < length
    ones = jnp.ones((rows, PAIR), BF16)
    for j in range(images):
        for c in range(0, width, PAIR):
            query = split_pair(proj_ref[j, :, c : c + PAIR] * jnp.asarray(SCALE, BF16))
            key = proj_ref[j, :, width + c : width + c + PAIR]
            value = proj_ref[j, :, 2 * width + c : 2 * width + c + PAIR]
            scores = jnp.where(live, nt(query, key), -1e30)
            top = jnp.max(scores, axis=-1, keepdims=True)
            weights = jnp.exp(scores - top).astype(BF16)
            both = nn(weights, jnp.concatenate([value, ones], axis=1))
            mixed_ref[j, :, c : c + PAIR] = join_pair(both[:, :PAIR] / both[:, PAIR:]).astype(BF16)


def mlp_kernel(
    length,
    chunk,
    index,
    tok_ref,
    cot_ref,
    mixed_ref,
    vec_ref,
    out_own,
    lift_own,
    drop_own,
    lift_near,
    lift_far,
    both_near,
    both_far,
    out_ref,
    d_middle_ref,
    d_mixed_ref,
    keep,
    send,
    x_s,
    z_s,
    w_out_ref,
    w_lift_ref,
    w_drop_ref,
    lift_bias_ref,
    a_drop,
    a_lift,
    a_out,
    a_vec,
    a_bias,
):
    step = pl.program_id(0)
    images, rows, width = x_s.shape
    total = images * rows
    hidden_width = w_lift_ref.shape[1]

    @pl.when(step == 0)
    def _():
        zero_tail(x_s, length)
        zero_tail(z_s, length)
        deep = drop_own.shape[0] // 2
        join_pieces(w_out_ref, out_own, both_near, both_far, index, deep)
        join_pieces(w_lift_ref, lift_own, lift_near, lift_far, index)
        join_pieces(w_drop_ref, drop_own, both_near, both_far, index)
        for k in range(hidden_width // width):
            lift_bias_ref[:, k * width : (k + 1) * width] = vec_ref[8 + k : 9 + k, :]
        for acc in (a_drop, a_lift, a_out, a_vec, a_bias):
            acc[...] = jnp.zeros_like(acc)

    pad_rows(x_s, tok_ref, length)
    pad_rows(z_s, cot_ref, length)
    out_bias, gain, shift, drop_bias = (vec_ref[i : i + 1, :] for i in range(4, 8))
    mixed = mixed_ref[...].reshape(total, width)
    dz = z_s[...].reshape(total, width)
    dz_f = dz.astype(F32)
    middle = x_s[...].reshape(total, width).astype(F32) + nn(mixed, w_out_ref[...]) + out_bias
    normal, inverse = normalise(middle)
    normed = (normal * gain + shift).astype(BF16)
    result = middle + drop_bias
    d_normed = jnp.zeros((total, width), F32)
    for c in range(0, hidden_width, chunk):
        part = slice(c, c + chunk)
        hidden = nn(normed, w_lift_ref[:, part]) + lift_bias_ref[:, part]
        cdf = 0.5 + 0.5 * lax.erf(hidden * ROOT_HALF)
        bell = jnp.exp(hidden * hidden * -0.5) * GAUSS
        active = (hidden * cdf).astype(BF16)
        d_active = nt(dz, w_drop_ref[part, :])
        d_hidden_f = d_active * (cdf + hidden * bell)
        d_hidden = d_hidden_f.astype(BF16)
        result = result + nn(active, w_drop_ref[part, :])
        d_normed = d_normed + nt(d_hidden, w_lift_ref[:, part])
        a_drop[part, :] += tn(active, dz)
        a_lift[:, part] += tn(normed, d_hidden)
        a_bias[:, part] += fold(d_hidden.astype(F32))
    out = result.astype(BF16)
    for j in range(images):
        out_ref[j] = out[j * rows : j * rows + length]
    d_middle = dz_f + norm_back(d_normed, normal, inverse, gain)
    d_middle_ref[...] = d_middle.reshape(images, rows, width)
    d_attended = d_middle.astype(BF16)
    d_mixed_ref[...] = nt(d_attended, w_out_ref[...]).astype(BF16).reshape(images, rows, width)
    a_out[...] += tn(mixed, d_attended)
    a_vec[0] += fold(d_attended.astype(F32))
    a_vec[1] += fold(d_normed * normal)
    a_vec[2] += fold(d_normed)
    a_vec[3] += fold(dz_f)

    @pl.when(step == pl.num_programs(0) - 1)
    def _():
        columns = jnp.sum(a_bias[...], axis=0, keepdims=True)
        vectors = jnp.concatenate(
            [jnp.sum(a_vec[...], axis=1)]
            + [columns[:, c : c + width] for c in range(0, hidden_width, width)],
            axis=0,
        ).astype(BF16)
        deep, tall, small = hidden_width // 4, width // 4, width // 8
        for place, half, core, side in quarters(index, keep, send):
            quarter = 2 * half + core
            if side == 0:
                first = pl.multiple_of(quarter * deep, 8)
                place[0:deep, :] = a_drop[pl.ds(first, deep), :].astype(BF16)
                place[deep + small : deep + small + 8, :] = vectors
                place[deep + small + 8 :, :] = jnp.zeros((8, width), BF16)
            else:
                rows_of = pl.ds(pl.multiple_of(quarter * tall, 8), tall)
                for k in range(hidden_width // width):
                    place[k * tall : (k + 1) * tall, :] = a_lift[
                        rows_of, k * width : (k + 1) * width
                    ].astype(BF16)
                place[deep + small :, :] = jnp.zeros((16, width), BF16)
            first = pl.multiple_of(quarter * tall + side * small, 8)
            place[deep : deep + small, :] = a_out[pl.ds(first, small), :].astype(BF16)


def back_kernel(
    length, first, last, index, tok_ref, proj_ref, normed_ref, d_mixed_ref, d_middle_ref, w_ref, vec_ref, *refs
):
    if not first:
        old, refs = refs[:3], refs[4:]
    in_grad_ref = refs[0]
    if last:
        keep, send = refs[1:3]
        sums, d_s = refs[3:6], refs[6]
    else:
        sums, d_s = refs[1:4], refs[4]
    a_qkv, a_proj, a_vec = sums
    images, rows, wide = d_s.shape
    width = wide // 3
    total = images * rows

    @pl.when(pl.program_id(0) == 0)
    def _():
        for i, acc in enumerate(sums):
            acc[...] = jnp.zeros_like(acc) if first else old[i][...]

    live = lax.broadcasted_iota(jnp.int32, (rows, 2 * rows), 0) < length
    for j in range(images):
        for c in range(0, width, PAIR):
            query = split_pair(proj_ref[j, :, c : c + PAIR] * jnp.asarray(SCALE, BF16))
            key = proj_ref[j, :, width + c : width + c + PAIR]
            value = proj_ref[j, :, 2 * width + c : 2 * width + c + PAIR]
            d_mixed = split_pair(d_mixed_ref[j, :, c : c + PAIR])
            scores = jnp.where(live, nt(key, query), -1e30)
            top = jnp.max(scores, axis=0, keepdims=True)
            weights = jnp.exp(scores - top)
            probs = weights * (1.0 / jnp.sum(weights, axis=0, keepdims=True))
            d_probs = nt(value, d_mixed)
            delta = jnp.sum(probs * d_probs, axis=0, keepdims=True)
            d_scores = (probs * (d_probs - delta)).astype(BF16)
            d_value = nn(probs.astype(BF16), d_mixed)
            d_key = nn(d_scores, query)
            d_query = join_pair(tn(d_scores, key)) * SCALE
            d_s[j, :, c : c + PAIR] = d_query.astype(BF16)
            d_s[j, :, width + c : width + c + PAIR] = d_key.astype(BF16)
            d_s[j, :, 2 * width + c : 2 * width + c + PAIR] = d_value.astype(BF16)
    d_proj = d_s[...].reshape(total, wide)
    a_qkv[...] += tn(normed_ref[...].reshape(total, width), d_proj)
    a_proj[...] += fold(d_proj.astype(F32))
    d_normed = nt(d_proj, w_ref[...])
    gain = vec_ref[0:1, :]
    for j in range(images):
        normal, inverse = normalise(tok_ref[j].astype(F32))
        grad = d_normed[j * rows : j * rows + length]
        in_grad_ref[j] = (
            d_middle_ref[j, 0:length, :] + norm_back(grad, normal, inverse, gain)
        ).astype(BF16)
        a_vec[0:1, :] += jnp.sum(grad * normal, axis=0, keepdims=True)
        a_vec[1:2, :] += jnp.sum(grad, axis=0, keepdims=True)
    if not last:
        return

    @pl.when(pl.program_id(0) == pl.num_programs(0) - 1)
    def _():
        columns = jnp.sum(a_proj[...], axis=0, keepdims=True)
        vectors = jnp.concatenate(
            [columns[:, :width], columns[:, 2 * width :], a_vec[...], jnp.zeros((4, width), F32)],
            axis=0,
        ).astype(BF16)
        small = width // 8
        for place, half, core, side in quarters(index, keep, send):
            first_row = pl.multiple_of((2 * half + core) * 2 * small + side * small, 8)
            for k in range(3):
                place[k * small : (k + 1) * small, :] = a_qkv[
                    pl.ds(first_row, small), k * width : (k + 1) * width
                ].astype(BF16)
            place[3 * small :, :] = vectors


def placed(full, index, pieces):
    core, y, z = index[1], index[2], index[3]
    rows = pieces[0].shape[0]
    spots = ((core, y), (core, 1 - y), (1 - core, y), (1 - core, 1 - y))
    if len(pieces) == 4:
        for (owner, side), piece in zip(spots, pieces):
            full[owner, side] = piece[...].astype(F32)
        return
    for i, (owner, side) in enumerate(spots):
        for piece, part in ((pieces[2 * i], z), (pieces[2 * i + 1], 1 - z)):
            place = pl.ds(pl.multiple_of(part * rows, 8), rows)
            full[owner, side, place, :] = piece[...].astype(F32)


def own_half(index, row):
    half = row.shape[-1] // 2
    return jnp.where(index[0] == 0, row[:, :half], row[:, half:])[0]


def unpack_kernel(index, *refs):
    unpack_outer(index, refs[0:8], refs[12:20], refs[25])
    unpack_inner(index, refs[8:12], refs[20:25], refs[26])


def unpack_outer(index, pieces, outs, full):
    g_drop, g_lift, g_out, g_out_bias, g_gain, g_shift, g_drop_bias, g_lift_bias = outs
    placed(full, index, pieces)
    width = g_out.shape[1]
    deep, tall, small = g_drop.shape[0] // 2, width // 4, width // 8
    blocks = g_lift.shape[1] // width
    for core in range(2):
        g_drop[core * deep : (core + 1) * deep, :] = full[core, 0, 0:deep, :]
        for k in range(blocks):
            g_lift[core * tall : (core + 1) * tall, k * width : (k + 1) * width] = full[
                core, 1, k * tall : (k + 1) * tall, :
            ]
        for side in range(2):
            first = core * tall + side * small
            g_out[first : first + small, :] = full[core, side, deep : deep + small, :]
    vectors = full[0, 0, deep + small :, :]
    for i, ref in enumerate((g_out_bias, g_gain, g_shift, g_drop_bias)):
        ref[...] = own_half(index, vectors[i : i + 1, :])
    for k in range(blocks // 2):
        row = jnp.where(
            index[0] == 0,
            vectors[4 + k : 5 + k, :],
            vectors[4 + blocks // 2 + k : 5 + blocks // 2 + k, :],
        )
        g_lift_bias[k * width : (k + 1) * width] = row[0]


def unpack_inner(index, pieces, outs, full):
    g_qkv, g_query, g_value, g_gain, g_shift = outs
    placed(full, index, pieces)
    width = full.shape[3]
    small = width // 8
    for core in range(2):
        for side in range(2):
            first = (2 * core + side) * small
            for k in range(3):
                g_qkv[first : first + small, k * width : (k + 1) * width] = full[
                    core, side, k * small : (k + 1) * small, :
                ]
    vectors = full[0, 0, 3 * small :, :]
    for i, ref in enumerate((g_query, g_value, g_gain, g_shift)):
        ref[...] = own_half(index, vectors[i : i + 1, :])


VMEM_LIMIT = 60 * 1024 * 1024
PARAMS = pltpu.CompilerParams(vmem_limit_bytes=VMEM_LIMIT)
SCALARS = pl.BlockSpec(memory_space=pltpu.SMEM)


def whole(*shape):
    return pl.BlockSpec(shape, lambda i: (0,) * len(shape))


def whole_like(arrays):
    return [whole(*a.shape) for a in arrays]


def per_step(*shape):
    return pl.BlockSpec(shape, lambda i: (i,) + (0,) * (len(shape) - 1))


def shape_of(dtype, *shape):
    return jax.ShapeDtypeStruct(shape, dtype)


def cost(microseconds):
    return pl.CostEstimate(flops=int(microseconds * 1e3), bytes_accessed=1, transcendentals=0)


def pack_first(index, vectors, lift_bias, weight):
    rows, columns = weight.shape
    return pl.pallas_call(
        pack_first_kernel,
        grid=(1,),
        in_specs=[SCALARS, *whole_like((*vectors, lift_bias, weight))],
        out_specs=whole(rows // 2 + 8, columns),
        out_shape=shape_of(BF16, rows // 2 + 8, columns),
        compiler_params=PARAMS,
        cost_estimate=cost(1),
        name="pack_first",
    )(index, *vectors, lift_bias, weight)


def pack_rest(index, weights):
    out_weight, lift_weight, drop_weight = weights
    tall, width = out_weight.shape[0] // 2, out_weight.shape[1]
    shapes = [(tall, lift_weight.shape[1]), (drop_weight.shape[0] // 2 + tall, width)]
    return pl.pallas_call(
        pack_rest_kernel,
        grid=(1,),
        in_specs=[SCALARS, *whole_like(weights)],
        out_specs=[whole(*d) for d in shapes],
        out_shape=[shape_of(BF16, *d) for d in shapes],
        compiler_params=PARAMS,
        cost_estimate=cost(1),
        name="pack_rest",
    )(index, *weights)


def forward_attention(index, tokens, ff, packed, pieces):
    images, length, width = tokens.shape
    rows = -(-length // 16) * 16
    group = 4 if images % 4 == 0 else 1
    return pl.pallas_call(
        functools.partial(attend_kernel, length),
        grid=(images // group,),
        in_specs=[SCALARS, per_step(group, length, width), *whole_like((packed, *pieces))],
        out_specs=[
            per_step(group, rows, width),
            per_step(group, rows, 3 * width),
            per_step(group, rows, width),
            whole(width, 3 * width),
            whole(8 + ff // width, width),
        ],
        out_shape=[
            shape_of(BF16, images, rows, width),
            shape_of(BF16, images, rows, 3 * width),
            shape_of(BF16, images, rows, width),
            shape_of(BF16, width, 3 * width),
            shape_of(F32, 8 + ff // width, width),
        ],
        scratch_shapes=[pltpu.VMEM((group, rows, width), BF16)],
        compiler_params=PARAMS,
        cost_estimate=cost(1),
        name="attend",
    )(index, tokens, packed, *pieces)


def mlp_both_ways(index, tokens, cotangent, mixed, vectors, ff, pieces):
    images, length, width = tokens.shape
    rows = mixed.shape[1]
    group = 2 if images % 2 == 0 else 1
    eighth = (2, 2, ff // 4 + width // 8 + 16, width)
    return pl.pallas_call(
        functools.partial(mlp_kernel, length, 512),
        grid=(images // group,),
        in_specs=[
            SCALARS,
            per_step(group, length, width),
            per_step(group, length, width),
            per_step(group, rows, width),
            *whole_like((vectors, *pieces)),
        ],
        out_specs=[
            per_step(group, length, width),
            per_step(group, rows, width),
            per_step(group, rows, width),
            whole(*eighth),
            whole(*eighth),
        ],
        out_shape=[
            shape_of(BF16, images, length, width),
            shape_of(F32, images, rows, width),
            shape_of(BF16, images, rows, width),
            shape_of(BF16, *eighth),
            shape_of(BF16, *eighth),
        ],
        scratch_shapes=[
            pltpu.VMEM((group, rows, width), BF16),
            pltpu.VMEM((group, rows, width), BF16),
            pltpu.VMEM((width, width), BF16),
            pltpu.VMEM((width, ff), BF16),
            pltpu.VMEM((ff, width), BF16),
            pltpu.VMEM((1, ff), F32),
            pltpu.VMEM((ff, width), F32),
            pltpu.VMEM((width, ff), F32),
            pltpu.VMEM((width, width), F32),
            pltpu.VMEM((4, 8, width), F32),
            pltpu.VMEM((8, ff), F32),
        ],
        compiler_params=PARAMS,
        cost_estimate=cost(1),
        name="mlp",
    )(index, tokens, cotangent, mixed, vectors, *pieces)


def attention_backward(
    index, tokens, projected, normed, w_qkv, vectors, d_mixed, d_middle, start, stop, earlier=()
):
    images, length, width = tokens.shape
    rows = normed.shape[1]
    wide = 3 * width
    group = 2 if images % 2 == 0 else 1
    offset = start // group
    first, last = not earlier, stop == images
    chunk = (2, 2, 3 * width // 8 + 8, width)
    sums = [(width, wide), (8, wide), (2, width)]

    def at(*shape):
        return pl.BlockSpec((group,) + shape, lambda i: (i + offset if offset else i, 0, 0))

    return pl.pallas_call(
        functools.partial(back_kernel, length, first, last),
        grid=((stop - start) // group,),
        in_specs=[
            SCALARS,
            at(length, width),
            at(rows, wide),
            at(rows, width),
            at(rows, width),
            at(rows, width),
            *whole_like((w_qkv, vectors)),
        ]
        + ([] if first else [whole(*d) for d in sums] + [pl.BlockSpec(memory_space=pl.ANY)]),
        out_specs=[at(length, width)]
        + ([whole(*chunk)] * 2 if last else [whole(*d) for d in sums]),
        out_shape=[shape_of(BF16, images, length, width)]
        + ([shape_of(BF16, *chunk)] * 2 if last else [shape_of(F32, *d) for d in sums]),
        scratch_shapes=([pltpu.VMEM(d, F32) for d in sums] if last else [])
        + [pltpu.VMEM((group, rows, wide), BF16)],
        input_output_aliases={} if first else {11: 0},
        compiler_params=PARAMS,
        cost_estimate=cost(1),
        name="back",
    )(index, tokens, projected, normed, d_mixed, d_middle, w_qkv, vectors, *earlier)


def unpack(index, outer, inner, shapes):
    rows, width = outer[0].shape
    return pl.pallas_call(
        unpack_kernel,
        grid=(1,),
        in_specs=[SCALARS, *whole_like((*outer, *inner))],
        out_specs=[whole(*d) for d in shapes],
        out_shape=[shape_of(F32, *d) for d in shapes],
        scratch_shapes=[
            pltpu.VMEM((2, 2, 2 * rows, width), F32),
            pltpu.VMEM((2, 2) + inner[0].shape, F32),
        ],
        compiler_params=PARAMS,
        cost_estimate=cost(1),
        name="unpack",
    )(index, *outer, *inner)


AXES = ("rep", "fsdp")


class Butterfly:
    def __init__(self):
        rep, x = lax.axis_index("rep"), lax.axis_index("fsdp")
        self.z = (rep >> 2) & 1
        self.index = jnp.stack([x, rep & 1, (rep >> 1) & 1, self.z]).astype(jnp.int32)

    def swap(self, v, rep_mask, x_mask=0):
        pairs = [
            (rep * 2 + x, (rep ^ rep_mask) * 2 + (x ^ x_mask)) for rep in range(16) for x in range(2)
        ]
        return lax.ppermute(v, AXES, pairs)

    def over_x(self, v):
        return self.swap(v, 0, 1)

    def over_core(self, v):
        return self.swap(v, 1)

    def over_y(self, v):
        return self.swap(v, 2)

    def over_z(self, v, mask):
        return self.swap(v, 4 * mask)

    def over_corner(self, v):
        return self.swap(v, 2, 1)

    def half(self, v, which):
        rows = v.shape[0] // 2
        return lax.dynamic_slice_in_dim(v, which * rows, rows, 0)

    def scatter(self, keep, got):
        total = [[keep[i, j] + got[i, j] for j in range(2)] for i in range(2)]
        return (total[1][0], total[0][1], total[1][1]), total[0][0]

    def send(self, parts):
        return self.over_x(parts[0]), self.over_y(parts[1]), self.over_corner(parts[2])


class Collective:
    def __init__(self):
        self.index = jnp.zeros((4,), jnp.int32)

    def gather_weight(self, own):
        full = lax.all_gather(own, "fsdp", axis=0, tiled=True)
        quarter = full.shape[0] // 4
        return full[: 2 * quarter], full[2 * quarter : 3 * quarter], full[3 * quarter :]

    def gather_vectors(self, vectors, lift_bias):
        whole_vectors = [lax.all_gather(v, "fsdp", axis=0, tiled=True) for v in vectors]
        whole_bias = lax.all_gather(lift_bias, "fsdp", axis=0, tiled=True)
        width = whole_vectors[0].shape[0]
        table = jnp.stack(whole_vectors).reshape(8, 2, width // 2)
        bias = whole_bias.reshape(2, -1, width)
        return (
            jnp.zeros((2, 8, 3 * width), BF16)
            .at[:, :, : width // 2]
            .set(table.transpose(1, 0, 2))
            .at[:, : bias.shape[1], width : 2 * width]
            .set(bias)
        )

    def reduce(self, v):
        owned = lax.psum_scatter(v.astype(BF16), "fsdp", scatter_dimension=0, tiled=True)
        return lax.psum(owned, "rep").astype(F32)


def after(*arrays):
    return lax.optimization_barrier(arrays)


def behind(arrays, *others):
    return lax.optimization_barrier((arrays, others))[0]


def settled(v):
    return with_layout_constraint(v.transpose(1, 0, 2), Layout(major_to_minor=(0, 1, 2)))


def in_order(keep, send):
    return [(q[0], q[1]) for q in (keep[0], send[0], keep[1], send[1])]


def per_device(
    tokens,
    gain_one,
    shift_one,
    qkv_weight,
    query_bias,
    value_bias,
    out_weight,
    out_bias,
    gain_two,
    shift_two,
    lift_weight,
    lift_bias,
    drop_weight,
    drop_bias,
    cotangent,
    swaps,
):
    length, width = tokens.shape[1:]
    plan = Butterfly() if swaps else Collective()
    index = plan.index
    small = (
        gain_one,
        shift_one,
        query_bias,
        value_bias,
        out_bias,
        gain_two,
        shift_two,
        drop_bias,
    )
    ff = lift_weight.shape[1]
    rest = (out_weight, lift_weight, drop_weight)
    if swaps:
        packed = pack_first(index, small, lift_bias, qkv_weight)
        tokens = with_layout_constraint(tokens, Layout(major_to_minor=(0, 1, 2)))
        near = behind(plan.over_x(packed), tokens)
        qkv = (qkv_weight, near, plan.over_core(near))
        rest_then, packed = after(rest, packed)
        nears = [plan.over_x(half) for half in pack_rest(index, rest_then)]
    else:
        packed, theirs = plan.gather_vectors(small, lift_bias)
        own, near, far = plan.gather_weight(qkv_weight)
        qkv = (own, jnp.concatenate([near, theirs]), far)
    normed, projected, mixed, full_qkv, vectors = forward_attention(
        index, tokens, ff, packed, qkv
    )
    if swaps:
        mixed, nears = after(mixed, nears)
        pieces = [piece for near in nears for piece in (near, plan.over_core(near))]
    else:
        (out_own, *outs), (lift_own, *lifts), (drop_own, *drops) = map(plan.gather_weight, rest)
        rest = (out_own, lift_own, drop_own)
        pieces = [*lifts, *(jnp.concatenate(both) for both in zip(drops, outs))]
    outer = (*rest, *pieces)
    output, d_middle, d_mixed, keep_a, send_a = mlp_both_ways(
        index, tokens, cotangent, mixed, vectors, ff, outer
    )
    backward = functools.partial(
        attention_backward, index, tokens, projected, normed, full_qkv, vectors
    )
    images, half = tokens.shape[0], width // 2
    if swaps:
        got_a = plan.over_core(send_a)
        input_grad, *sums = backward(d_mixed, d_middle, 0, 2)
        sums, got_a = after(sums, got_a)
        parts_a, stay_a = plan.scatter(keep_a, got_a)
        sums, parts_a = after(sums, parts_a)
        more_a = plan.send(parts_a)
        input_grad, keep_c, send_c = backward(
            d_mixed, d_middle, 2, images, (*sums, input_grad)
        )
        send_c, more_a = after(send_c, more_a)
        got_c = plan.over_core(send_c)
        sum_a = stay_a + more_a[0] + more_a[1] + more_a[2]
        low_a, high_a = plan.half(sum_a, plan.z), plan.half(sum_a, 1 - plan.z)
        over_a = plan.over_z(high_a, 1)
        got_c = behind(got_c, low_a, high_a)
        parts_c, stay_c = plan.scatter(keep_c, got_c)
        over_a = behind(over_a, parts_c)
        more_c = plan.send(parts_c)
        low_a = low_a + over_a
        over_a = plan.over_z(low_a, 2)
        more_c = behind(more_c, low_a)
        sum_c = stay_c + more_c[0] + more_c[1] + more_c[2]
        over_c = plan.over_z(sum_c, 1)
        over_a, over_c = after(over_a, over_c)
        low_a, sum_c = after(low_a + over_a, sum_c + over_c)
        high_a, over_c = plan.over_z(low_a, 1), plan.over_z(sum_c, 2)
        across_low, beside_low = plan.over_y(low_a), plan.over_core(low_a)
        output, input_grad = settled(output), settled(input_grad)
        high_a, over_c, across_low, beside_low, output, input_grad = after(
            high_a, over_c, across_low, beside_low, output, input_grad
        )
        output, input_grad = output.transpose(1, 0, 2), input_grad.transpose(1, 0, 2)
        across_high, beside_high = plan.over_y(high_a), plan.over_core(high_a)
        corner_low = plan.over_core(across_low)
        sum_c = sum_c + over_c
        across_c, beside_c = plan.over_y(sum_c), plan.over_core(sum_c)
        across_high, across_c, beside_c = after(across_high, across_c, beside_c)
        pieces_c = (sum_c, across_c, beside_c, plan.over_core(across_c))
        pieces_a = (
            low_a,
            high_a,
            across_low,
            across_high,
            beside_low,
            beside_high,
            corner_low,
            plan.over_core(across_high),
        )
        pieces_a, pieces_c = after(pieces_a, pieces_c)
        (
            g_drop,
            g_lift,
            g_out,
            g_out_bias,
            g_gain_two,
            g_shift_two,
            g_drop_bias,
            g_lift_bias,
            g_qkv,
            g_query,
            g_value,
            g_gain_one,
            g_shift_one,
        ) = unpack(
            index,
            pieces_a,
            pieces_c,
            [(ff // 2, width), (half, ff), (half, width)]
            + [(half,)] * 4
            + [(ff // 2,), (half, 3 * width)]
            + [(half,)] * 4,
        )
    else:
        input_grad, *sums = backward(d_mixed, d_middle, 0, images - 2)
        input_grad, keep_c, send_c = backward(
            d_mixed, d_middle, images - 2, images, (*sums, input_grad)
        )
        deep, tall, small = ff // 4, width // 4, width // 8
        eighths = in_order(keep_a, send_a)
        g_drop = plan.reduce(jnp.concatenate([q[0][:deep] for q in eighths]))
        g_lift = plan.reduce(
            jnp.concatenate(
                [
                    jnp.concatenate(
                        [q[1][k * tall : (k + 1) * tall] for k in range(ff // width)], axis=1
                    )
                    for q in eighths
                ]
            )
        )
        g_out = plan.reduce(
            jnp.concatenate([side[deep : deep + small] for q in eighths for side in q])
        )
        rows = eighths[0][0][deep + small : deep + small + 8]
        g_out_bias, g_gain_two, g_shift_two, g_drop_bias = (plan.reduce(rows[i]) for i in range(4))
        g_lift_bias = plan.reduce(rows[4:].reshape(-1))
        eighths = in_order(keep_c, send_c)
        g_qkv = plan.reduce(
            jnp.concatenate(
                [
                    jnp.concatenate([side[k * small : (k + 1) * small] for k in range(3)], axis=1)
                    for q in eighths
                    for side in q
                ]
            )
        )
        rows = eighths[0][0][3 * small :]
        g_query, g_value, g_gain_one, g_shift_one = (plan.reduce(rows[i]) for i in range(4))
    return (
        output,
        input_grad,
        g_gain_one,
        g_shift_one,
        g_qkv,
        g_query,
        g_value,
        g_out,
        g_out_bias,
        g_gain_two,
        g_shift_two,
        g_lift,
        g_lift_bias,
        g_drop,
        g_drop_bias,
    )


def solution(mesh):
    spread = P(("rep", "fsdp"), None, None)
    vector, matrix = P("fsdp"), P("fsdp", None)
    in_specs = (
        spread,
        vector,
        vector,
        matrix,
        vector,
        vector,
        matrix,
        vector,
        vector,
        vector,
        matrix,
        vector,
        matrix,
        vector,
        spread,
    )
    out_specs = (
        spread,
        spread,
        vector,
        vector,
        matrix,
        vector,
        vector,
        matrix,
        vector,
        vector,
        vector,
        matrix,
        vector,
        matrix,
        vector,
    )
    swaps = mesh.shape["rep"] == 16 and mesh.shape["fsdp"] == 2
    return jax.shard_map(
        functools.partial(per_device, swaps=swaps),
        mesh=mesh,
        in_specs=in_specs,
        out_specs=out_specs,
        check_vma=False,
    )
```

```python
import functools

import jax
import jax.numpy as jnp
from jax import lax
from jax.experimental import pallas as pl
from jax.experimental.layout import Layout, with_layout_constraint
from jax.experimental.pallas import tpu as pltpu
from jax.sharding import PartitionSpec as P

HEADS = 6
HEAD_DIM = 64
PAIR = 2 * HEAD_DIM
LANE = 128
EPS = 1e-06
ROOT_HALF = 0.7071067811865476
GAUSS = 0.3989422804014327
LOG2E = 1.4426950408889634
SCALE = HEAD_DIM ** (-0.5)
F32 = jnp.float32
BF16 = jnp.bfloat16


def nn(a, b):
    return lax.dot_general(a, b, (((1,), (0,)), ((), ())), preferred_element_type=F32)


def nt(a, b):
    return lax.dot_general(a, b, (((1,), (1,)), ((), ())), preferred_element_type=F32)


def tn(a, b):
    return lax.dot_general(a, b, (((0,), (0,)), ((), ())), preferred_element_type=F32)


def normalise(v):
    mean = jnp.mean(v, axis=-1, keepdims=True)
    centred = v - mean
    var = jnp.mean(centred * centred, axis=-1, keepdims=True)
    inverse = lax.rsqrt(var + EPS)
    return centred * inverse, inverse


def norm_back(grad, normal, inverse, gain):
    scaled = grad * gain
    return inverse * (
        scaled
        - jnp.mean(scaled, axis=-1, keepdims=True)
        - normal * jnp.mean(scaled * normal, axis=-1, keepdims=True)
    )


def fold(v):
    return jnp.sum(v.reshape(v.shape[0] // 8, 8, v.shape[1]), axis=0)


def pad_rows(scratch, ref, length):
    for j in range(ref.shape[0]):
        scratch[j, 0:length, :] = ref[j].astype(scratch.dtype)


def zero_tail(scratch, length):
    images, rows, columns = scratch.shape
    low = (length // 16) * 16
    scratch[:, low:rows, :] = jnp.zeros((images, rows - low, columns), scratch.dtype)


def split_pair(v):
    first = lax.broadcasted_iota(jnp.int32, v.shape, 1) < HEAD_DIM
    zero = jnp.zeros_like(v)
    return jnp.concatenate([jnp.where(first, v, zero), jnp.where(first, zero, v)], axis=0)


def join_pair(v):
    rows = v.shape[0] // 2
    first = lax.broadcasted_iota(jnp.int32, (rows, PAIR), 1) < HEAD_DIM
    return jnp.where(first, v[:rows], v[rows:])


def join_pieces(full, own, near, far, index, first=0):
    block = own.shape[0]
    half = block // 2
    x, core = index[0], index[1]
    other = (1 - x) * block
    full[pl.ds(pl.multiple_of(x * block, 16), block), :] = own[...]
    full[pl.ds(pl.multiple_of(other + core * half, 16), half), :] = near[first : first + half, :]
    full[pl.ds(pl.multiple_of(other + (1 - core) * half, 16), half), :] = far[first : first + half, :]


def quarters(index, keep, send):
    x, core, y = index[0], index[1], index[2]
    for dest, owner in ((keep, core), (send, 1 - core)):
        for slot, half in ((0, x), (1, 1 - x)):
            for side in range(2):
                yield dest.at[slot, jnp.where(y == side, 0, 1)], half, owner, side


def pack_first_kernel(index, *refs):
    vectors, lift_bias, weight, packed = refs[:8], *refs[8:]
    half = weight.shape[0] // 2
    shard, width = vectors[0].shape[0], weight.shape[1] // 3
    packed[0:half, :] = weight[pl.ds(pl.multiple_of(index[1] * half, 16), half), :]
    packed[half:, :] = jnp.zeros((8, 3 * width), BF16)
    for i, ref in enumerate(vectors):
        row = ref[...].astype(F32).reshape(1, shard)
        packed[half + i : half + i + 1, 0:shard] = row.astype(BF16)
    bias = lift_bias[...].astype(F32).reshape(1, lift_bias.shape[0]).astype(BF16)
    for k in range(lift_bias.shape[0] // width):
        packed[half + k : half + k + 1, width : 2 * width] = bias[:, k * width : (k + 1) * width]


def pack_rest_kernel(index, out_own, lift_own, drop_own, lift_half, both_half):
    tall, deep = lift_half.shape[0], drop_own.shape[0] // 2
    rows_of = pl.ds(pl.multiple_of(index[1] * tall, 16), tall)
    lift_half[...] = lift_own[rows_of, :]
    both_half[0:deep, :] = drop_own[pl.ds(pl.multiple_of(index[1] * deep, 16), deep), :]
    both_half[deep:, :] = out_own[rows_of, :]


def join_vectors(vec_ref, own, other, index):
    width = vec_ref.shape[1]
    half = width // 2
    mine, theirs = own[-8:, :].astype(F32), other[-8:, :].astype(F32)
    first = index[0] == 0
    low, high = jnp.where(first, mine, theirs), jnp.where(first, theirs, mine)
    vec_ref[0:8, :] = jnp.concatenate([low[:, :half], high[:, :half]], axis=1)
    blocks = vec_ref.shape[0] // 2 - 4
    vec_ref[8 : 8 + blocks, :] = low[:blocks, width : 2 * width]
    vec_ref[8 + blocks :, :] = high[:blocks, width : 2 * width]


def attend_kernel(
    length,
    index,
    tok_ref,
    packed,
    own,
    near,
    far,
    normed_ref,
    proj_ref,
    mixed_ref,
    w_ref,
    vec_ref,
    n_s,
):
    images, rows, width = n_s.shape

    @pl.when(pl.program_id(0) == 0)
    def _():
        zero_tail(n_s, length)
        join_pieces(w_ref, own, near, far, index)
        join_vectors(vec_ref, packed, near, index)

    gain, shift = vec_ref[0:1, :], vec_ref[1:2, :]
    bias = jnp.concatenate([vec_ref[2:3, :], jnp.zeros((1, width), F32), vec_ref[3:4, :]], axis=1)
    for j in range(images):
        normal, _ = normalise(tok_ref[j].astype(F32))
        n_s[j, 0:length, :] = (normal * gain + shift).astype(BF16)
    normed_ref[...] = n_s[...]
    flat = n_s[...].reshape(images * rows, width)
    proj_ref[...] = (nn(flat, w_ref[...]) + bias).astype(BF16).reshape(images, rows, 3 * width)
    live = lax.broadcasted_iota(jnp.int32, (2 * rows, rows), 1) < length
    ones = jnp.ones((rows, PAIR), BF16)
    for j in range(images):
        for c in range(0, width, PAIR):
            query = split_pair(proj_ref[j, :, c : c + PAIR] * jnp.asarray(SCALE, BF16))
            key = proj_ref[j, :, width + c : width + c + PAIR]
            value = proj_ref[j, :, 2 * width + c : 2 * width + c + PAIR]
            scores = jnp.where(live, nt(query, key), -1e30)
            top = jnp.max(scores, axis=-1, keepdims=True)
            weights = jnp.exp(scores - top).astype(BF16)
            both = nn(weights, jnp.concatenate([value, ones], axis=1))
            mixed_ref[j, :, c : c + PAIR] = (join_pair(both[:, :PAIR]) / join_pair(both[:, PAIR:])).astype(BF16)


def mlp_kernel(
    length,
    chunk,
    index,
    tok_ref,
    cot_ref,
    mixed_ref,
    vec_ref,
    out_own,
    lift_own,
    drop_own,
    lift_near,
    lift_far,
    both_near,
    both_far,
    out_ref,
    d_middle_ref,
    d_mixed_ref,
    keep,
    send,
    x_s,
    z_s,
    w_out_ref,
    w_lift_ref,
    w_drop_ref,
    lift_bias_ref,
    a_drop,
    a_lift,
    a_out,
    a_vec,
    a_bias,
):
    step = pl.program_id(0)
    images, rows, width = x_s.shape
    total = images * rows
    hidden_width = w_lift_ref.shape[1]

    @pl.when(step == 0)
    def _():
        zero_tail(x_s, length)
        zero_tail(z_s, length)
        deep = drop_own.shape[0] // 2
        join_pieces(w_out_ref, out_own, both_near, both_far, index, deep)
        join_pieces(w_lift_ref, lift_own, lift_near, lift_far, index)
        join_pieces(w_drop_ref, drop_own, both_near, both_far, index)
        for k in range(hidden_width // width):
            lift_bias_ref[:, k * width : (k + 1) * width] = vec_ref[8 + k : 9 + k, :]
        for acc in (a_drop, a_lift, a_out, a_vec, a_bias):
            acc[...] = jnp.zeros_like(acc)

    pad_rows(x_s, tok_ref, length)
    pad_rows(z_s, cot_ref, length)
    out_bias, gain, shift, drop_bias = (vec_ref[i : i + 1, :] for i in range(4, 8))
    mixed = mixed_ref[...].reshape(total, width)
    dz = z_s[...].reshape(total, width)
    dz_f = dz.astype(F32)
    middle = x_s[...].reshape(total, width).astype(F32) + nn(mixed, w_out_ref[...]) + out_bias
    normal, inverse = normalise(middle)
    normed = (normal * gain + shift).astype(BF16)
    result = middle + drop_bias
    d_normed = jnp.zeros((total, width), F32)
    for c in range(0, hidden_width, chunk):
        part = slice(c, c + chunk)
        hidden = nn(normed, w_lift_ref[:, part]) + lift_bias_ref[:, part]
        cdf = 0.5 + 0.5 * lax.erf(hidden * ROOT_HALF)
        bell = jnp.exp(hidden * hidden * -0.5) * GAUSS
        active = (hidden * cdf).astype(BF16)
        d_active = nt(dz, w_drop_ref[part, :])
        d_hidden_f = d_active * (cdf + hidden * bell)
        d_hidden = d_hidden_f.astype(BF16)
        result = result + nn(active, w_drop_ref[part, :])
        d_normed = d_normed + nt(d_hidden, w_lift_ref[:, part])
        a_drop[part, :] += tn(active, dz)
        a_lift[:, part] += tn(normed, d_hidden)
        a_bias[:, part] += fold(d_hidden.astype(F32))
    out = result.astype(BF16)
    for j in range(images):
        out_ref[j] = out[j * rows : j * rows + length]
    d_middle = dz_f + norm_back(d_normed, normal, inverse, gain)
    d_middle_ref[...] = d_middle.reshape(images, rows, width)
    d_attended = d_middle.astype(BF16)
    d_mixed_ref[...] = nt(d_attended, w_out_ref[...]).astype(BF16).reshape(images, rows, width)
    a_out[...] += tn(mixed, d_attended)
    a_vec[0] += fold(d_attended.astype(F32))
    a_vec[1] += fold(d_normed * normal)
    a_vec[2] += fold(d_normed)
    a_vec[3] += fold(dz_f)

    @pl.when(step == pl.num_programs(0) - 1)
    def _():
        columns = jnp.sum(a_bias[...], axis=0, keepdims=True)
        vectors = jnp.concatenate(
            [jnp.sum(a_vec[...], axis=1)]
            + [columns[:, c : c + width] for c in range(0, hidden_width, width)],
            axis=0,
        ).astype(BF16)
        deep, tall, small = hidden_width // 4, width // 4, width // 8
        for place, half, core, side in quarters(index, keep, send):
            quarter = 2 * half + core
            if side == 0:
                first = pl.multiple_of(quarter * deep, 8)
                place[0:deep, :] = a_drop[pl.ds(first, deep), :].astype(BF16)
                place[deep + small : deep + small + 8, :] = vectors
                place[deep + small + 8 :, :] = jnp.zeros((8, width), BF16)
            else:
                rows_of = pl.ds(pl.multiple_of(quarter * tall, 8), tall)
                for k in range(hidden_width // width):
                    place[k * tall : (k + 1) * tall, :] = a_lift[
                        rows_of, k * width : (k + 1) * width
                    ].astype(BF16)
                place[deep + small :, :] = jnp.zeros((16, width), BF16)
            first = pl.multiple_of(quarter * tall + side * small, 8)
            place[deep : deep + small, :] = a_out[pl.ds(first, small), :].astype(BF16)


def back_kernel(
    length, first, last, index, tok_ref, proj_ref, normed_ref, d_mixed_ref, d_middle_ref, w_ref, vec_ref, *refs
):
    if not first:
        old, refs = refs[:3], refs[4:]
    in_grad_ref = refs[0]
    if last:
        keep, send = refs[1:3]
        sums, d_s = refs[3:6], refs[6]
    else:
        sums, d_s = refs[1:4], refs[4]
    a_qkv, a_proj, a_vec = sums
    images, rows, wide = d_s.shape
    width = wide // 3
    total = images * rows

    @pl.when(pl.program_id(0) == 0)
    def _():
        for i, acc in enumerate(sums):
            acc[...] = jnp.zeros_like(acc) if first else old[i][...]

    live = lax.broadcasted_iota(jnp.int32, (rows, 2 * rows), 0) < length
    for j in range(images):
        for c in range(0, width, PAIR):
            query = split_pair(proj_ref[j, :, c : c + PAIR] * jnp.asarray(SCALE, BF16))
            key = proj_ref[j, :, width + c : width + c + PAIR]
            value = proj_ref[j, :, 2 * width + c : 2 * width + c + PAIR]
            d_mixed = split_pair(d_mixed_ref[j, :, c : c + PAIR])
            scores = jnp.where(live, nt(key, query), -1e30)
            top = jnp.max(scores, axis=0, keepdims=True)
            weights = jnp.exp(scores - top)
            probs = weights * (1.0 / jnp.sum(weights, axis=0, keepdims=True))
            d_probs = nt(value, d_mixed)
            delta = jnp.sum(probs * d_probs, axis=0, keepdims=True)
            d_scores = (probs * (d_probs - delta)).astype(BF16)
            d_value = nn(probs.astype(BF16), d_mixed)
            d_key = nn(d_scores, query)
            d_query = join_pair(tn(d_scores, key)) * SCALE
            d_s[j, :, c : c + PAIR] = d_query.astype(BF16)
            d_s[j, :, width + c : width + c + PAIR] = d_key.astype(BF16)
            d_s[j, :, 2 * width + c : 2 * width + c + PAIR] = d_value.astype(BF16)
    d_proj = d_s[...].reshape(total, wide)
    a_qkv[...] += tn(normed_ref[...].reshape(total, width), d_proj)
    a_proj[...] += fold(d_proj.astype(F32))
    d_normed = nt(d_proj, w_ref[...])
    gain = vec_ref[0:1, :]
    for j in range(images):
        normal, inverse = normalise(tok_ref[j].astype(F32))
        grad = d_normed[j * rows : j * rows + length]
        in_grad_ref[j] = (
            d_middle_ref[j, 0:length, :] + norm_back(grad, normal, inverse, gain)
        ).astype(BF16)
        a_vec[0:1, :] += jnp.sum(grad * normal, axis=0, keepdims=True)
        a_vec[1:2, :] += jnp.sum(grad, axis=0, keepdims=True)
    if not last:
        return

    @pl.when(pl.program_id(0) == pl.num_programs(0) - 1)
    def _():
        columns = jnp.sum(a_proj[...], axis=0, keepdims=True)
        vectors = jnp.concatenate(
            [columns[:, :width], columns[:, 2 * width :], a_vec[...], jnp.zeros((4, width), F32)],
            axis=0,
        ).astype(BF16)
        small = width // 8
        for place, half, core, side in quarters(index, keep, send):
            first_row = pl.multiple_of((2 * half + core) * 2 * small + side * small, 8)
            for k in range(3):
                place[k * small : (k + 1) * small, :] = a_qkv[
                    pl.ds(first_row, small), k * width : (k + 1) * width
                ].astype(BF16)
            place[3 * small :, :] = vectors


def placed(full, index, pieces):
    core, y, z = index[1], index[2], index[3]
    rows = pieces[0].shape[0]
    spots = ((core, y), (core, 1 - y), (1 - core, y), (1 - core, 1 - y))
    if len(pieces) == 4:
        for (owner, side), piece in zip(spots, pieces):
            full[owner, side] = piece[...].astype(F32)
        return
    for i, (owner, side) in enumerate(spots):
        for piece, part in ((pieces[2 * i], z), (pieces[2 * i + 1], 1 - z)):
            place = pl.ds(pl.multiple_of(part * rows, 8), rows)
            full[owner, side, place, :] = piece[...].astype(F32)


def own_half(index, row):
    half = row.shape[-1] // 2
    return jnp.where(index[0] == 0, row[:, :half], row[:, half:])[0]


def unpack_kernel(index, *refs):
    unpack_outer(index, refs[0:8], refs[12:20], refs[25])
    unpack_inner(index, refs[8:12], refs[20:25], refs[26])


def unpack_outer(index, pieces, outs, full):
    g_drop, g_lift, g_out, g_out_bias, g_gain, g_shift, g_drop_bias, g_lift_bias = outs
    placed(full, index, pieces)
    width = g_out.shape[1]
    deep, tall, small = g_drop.shape[0] // 2, width // 4, width // 8
    blocks = g_lift.shape[1] // width
    for core in range(2):
        g_drop[core * deep : (core + 1) * deep, :] = full[core, 0, 0:deep, :]
        for k in range(blocks):
            g_lift[core * tall : (core + 1) * tall, k * width : (k + 1) * width] = full[
                core, 1, k * tall : (k + 1) * tall, :
            ]
        for side in range(2):
            first = core * tall + side * small
            g_out[first : first + small, :] = full[core, side, deep : deep + small, :]
    vectors = full[0, 0, deep + small :, :]
    for i, ref in enumerate((g_out_bias, g_gain, g_shift, g_drop_bias)):
        ref[...] = own_half(index, vectors[i : i + 1, :])
    for k in range(blocks // 2):
        row = jnp.where(
            index[0] == 0,
            vectors[4 + k : 5 + k, :],
            vectors[4 + blocks // 2 + k : 5 + blocks // 2 + k, :],
        )
        g_lift_bias[k * width : (k + 1) * width] = row[0]


def unpack_inner(index, pieces, outs, full):
    g_qkv, g_query, g_value, g_gain, g_shift = outs
    placed(full, index, pieces)
    width = full.shape[3]
    small = width // 8
    for core in range(2):
        for side in range(2):
            first = (2 * core + side) * small
            for k in range(3):
                g_qkv[first : first + small, k * width : (k + 1) * width] = full[
                    core, side, k * small : (k + 1) * small, :
                ]
    vectors = full[0, 0, 3 * small :, :]
    for i, ref in enumerate((g_query, g_value, g_gain, g_shift)):
        ref[...] = own_half(index, vectors[i : i + 1, :])


VMEM_LIMIT = 60 * 1024 * 1024
PARAMS = pltpu.CompilerParams(vmem_limit_bytes=VMEM_LIMIT)
SCALARS = pl.BlockSpec(memory_space=pltpu.SMEM)


def whole(*shape):
    return pl.BlockSpec(shape, lambda i: (0,) * len(shape))


def whole_like(arrays):
    return [whole(*a.shape) for a in arrays]


def per_step(*shape):
    return pl.BlockSpec(shape, lambda i: (i,) + (0,) * (len(shape) - 1))


def shape_of(dtype, *shape):
    return jax.ShapeDtypeStruct(shape, dtype)


def cost(microseconds):
    return pl.CostEstimate(flops=int(microseconds * 1e3), bytes_accessed=1, transcendentals=0)


def pack_first(index, vectors, lift_bias, weight):
    rows, columns = weight.shape
    return pl.pallas_call(
        pack_first_kernel,
        grid=(1,),
        in_specs=[SCALARS, *whole_like((*vectors, lift_bias, weight))],
        out_specs=whole(rows // 2 + 8, columns),
        out_shape=shape_of(BF16, rows // 2 + 8, columns),
        compiler_params=PARAMS,
        cost_estimate=cost(1),
        name="pack_first",
    )(index, *vectors, lift_bias, weight)


def pack_rest(index, weights):
    out_weight, lift_weight, drop_weight = weights
    tall, width = out_weight.shape[0] // 2, out_weight.shape[1]
    shapes = [(tall, lift_weight.shape[1]), (drop_weight.shape[0] // 2 + tall, width)]
    return pl.pallas_call(
        pack_rest_kernel,
        grid=(1,),
        in_specs=[SCALARS, *whole_like(weights)],
        out_specs=[whole(*d) for d in shapes],
        out_shape=[shape_of(BF16, *d) for d in shapes],
        compiler_params=PARAMS,
        cost_estimate=cost(1),
        name="pack_rest",
    )(index, *weights)


def forward_attention(index, tokens, ff, packed, pieces):
    images, length, width = tokens.shape
    rows = -(-length // 16) * 16
    group = 4 if images % 4 == 0 else 1
    return pl.pallas_call(
        functools.partial(attend_kernel, length),
        grid=(images // group,),
        in_specs=[SCALARS, per_step(group, length, width), *whole_like((packed, *pieces))],
        out_specs=[
            per_step(group, rows, width),
            per_step(group, rows, 3 * width),
            per_step(group, rows, width),
            whole(width, 3 * width),
            whole(8 + ff // width, width),
        ],
        out_shape=[
            shape_of(BF16, images, rows, width),
            shape_of(BF16, images, rows, 3 * width),
            shape_of(BF16, images, rows, width),
            shape_of(BF16, width, 3 * width),
            shape_of(F32, 8 + ff // width, width),
        ],
        scratch_shapes=[pltpu.VMEM((group, rows, width), BF16)],
        compiler_params=PARAMS,
        cost_estimate=cost(1),
        name="attend",
    )(index, tokens, packed, *pieces)


def mlp_both_ways(index, tokens, cotangent, mixed, vectors, ff, pieces):
    images, length, width = tokens.shape
    rows = mixed.shape[1]
    group = 2 if images % 2 == 0 else 1
    eighth = (2, 2, ff // 4 + width // 8 + 16, width)
    return pl.pallas_call(
        functools.partial(mlp_kernel, length, 512),
        grid=(images // group,),
        in_specs=[
            SCALARS,
            per_step(group, length, width),
            per_step(group, length, width),
            per_step(group, rows, width),
            *whole_like((vectors, *pieces)),
        ],
        out_specs=[
            per_step(group, length, width),
            per_step(group, rows, width),
            per_step(group, rows, width),
            whole(*eighth),
            whole(*eighth),
        ],
        out_shape=[
            shape_of(BF16, images, length, width),
            shape_of(F32, images, rows, width),
            shape_of(BF16, images, rows, width),
            shape_of(BF16, *eighth),
            shape_of(BF16, *eighth),
        ],
        scratch_shapes=[
            pltpu.VMEM((group, rows, width), BF16),
            pltpu.VMEM((group, rows, width), BF16),
            pltpu.VMEM((width, width), BF16),
            pltpu.VMEM((width, ff), BF16),
            pltpu.VMEM((ff, width), BF16),
            pltpu.VMEM((1, ff), F32),
            pltpu.VMEM((ff, width), F32),
            pltpu.VMEM((width, ff), F32),
            pltpu.VMEM((width, width), F32),
            pltpu.VMEM((4, 8, width), F32),
            pltpu.VMEM((8, ff), F32),
        ],
        compiler_params=PARAMS,
        cost_estimate=cost(1),
        name="mlp",
    )(index, tokens, cotangent, mixed, vectors, *pieces)


def attention_backward(
    index, tokens, projected, normed, w_qkv, vectors, d_mixed, d_middle, start, stop, earlier=()
):
    images, length, width = tokens.shape
    rows = normed.shape[1]
    wide = 3 * width
    group = 2 if images % 2 == 0 else 1
    offset = start // group
    first, last = not earlier, stop == images
    chunk = (2, 2, 3 * width // 8 + 8, width)
    sums = [(width, wide), (8, wide), (2, width)]

    def at(*shape):
        return pl.BlockSpec((group,) + shape, lambda i: (i + offset if offset else i, 0, 0))

    return pl.pallas_call(
        functools.partial(back_kernel, length, first, last),
        grid=((stop - start) // group,),
        in_specs=[
            SCALARS,
            at(length, width),
            at(rows, wide),
            at(rows, width),
            at(rows, width),
            at(rows, width),
            *whole_like((w_qkv, vectors)),
        ]
        + ([] if first else [whole(*d) for d in sums] + [pl.BlockSpec(memory_space=pl.ANY)]),
        out_specs=[at(length, width)]
        + ([whole(*chunk)] * 2 if last else [whole(*d) for d in sums]),
        out_shape=[shape_of(BF16, images, length, width)]
        + ([shape_of(BF16, *chunk)] * 2 if last else [shape_of(F32, *d) for d in sums]),
        scratch_shapes=([pltpu.VMEM(d, F32) for d in sums] if last else [])
        + [pltpu.VMEM((group, rows, wide), BF16)],
        input_output_aliases={} if first else {11: 0},
        compiler_params=PARAMS,
        cost_estimate=cost(1),
        name="back",
    )(index, tokens, projected, normed, d_mixed, d_middle, w_qkv, vectors, *earlier)


def unpack(index, outer, inner, shapes):
    rows, width = outer[0].shape
    return pl.pallas_call(
        unpack_kernel,
        grid=(1,),
        in_specs=[SCALARS, *whole_like((*outer, *inner))],
        out_specs=[whole(*d) for d in shapes],
        out_shape=[shape_of(F32, *d) for d in shapes],
        scratch_shapes=[
            pltpu.VMEM((2, 2, 2 * rows, width), F32),
            pltpu.VMEM((2, 2) + inner[0].shape, F32),
        ],
        compiler_params=PARAMS,
        cost_estimate=cost(1),
        name="unpack",
    )(index, *outer, *inner)


AXES = ("rep", "fsdp")


class Butterfly:
    def __init__(self):
        rep, x = lax.axis_index("rep"), lax.axis_index("fsdp")
        self.z = (rep >> 2) & 1
        self.index = jnp.stack([x, rep & 1, (rep >> 1) & 1, self.z]).astype(jnp.int32)

    def swap(self, v, rep_mask, x_mask=0):
        pairs = [
            (rep * 2 + x, (rep ^ rep_mask) * 2 + (x ^ x_mask)) for rep in range(16) for x in range(2)
        ]
        return lax.ppermute(v, AXES, pairs)

    def over_x(self, v):
        return self.swap(v, 0, 1)

    def over_core(self, v):
        return self.swap(v, 1)

    def over_y(self, v):
        return self.swap(v, 2)

    def over_z(self, v, mask):
        return self.swap(v, 4 * mask)

    def over_corner(self, v):
        return self.swap(v, 2, 1)

    def half(self, v, which):
        rows = v.shape[0] // 2
        return lax.dynamic_slice_in_dim(v, which * rows, rows, 0)

    def scatter(self, keep, got):
        total = [[keep[i, j] + got[i, j] for j in range(2)] for i in range(2)]
        return (total[1][0], total[0][1], total[1][1]), total[0][0]

    def send(self, parts):
        return self.over_x(parts[0]), self.over_y(parts[1]), self.over_corner(parts[2])


class Collective:
    def __init__(self):
        self.index = jnp.zeros((4,), jnp.int32)

    def gather_weight(self, own):
        full = lax.all_gather(own, "fsdp", axis=0, tiled=True)
        quarter = full.shape[0] // 4
        return full[: 2 * quarter], full[2 * quarter : 3 * quarter], full[3 * quarter :]

    def gather_vectors(self, vectors, lift_bias):
        whole_vectors = [lax.all_gather(v, "fsdp", axis=0, tiled=True) for v in vectors]
        whole_bias = lax.all_gather(lift_bias, "fsdp", axis=0, tiled=True)
        width = whole_vectors[0].shape[0]
        table = jnp.stack(whole_vectors).reshape(8, 2, width // 2)
        bias = whole_bias.reshape(2, -1, width)
        return (
            jnp.zeros((2, 8, 3 * width), BF16)
            .at[:, :, : width // 2]
            .set(table.transpose(1, 0, 2))
            .at[:, : bias.shape[1], width : 2 * width]
            .set(bias)
        )

    def reduce(self, v):
        owned = lax.psum_scatter(v.astype(BF16), "fsdp", scatter_dimension=0, tiled=True)
        return lax.psum(owned, "rep").astype(F32)


def after(*arrays):
    return lax.optimization_barrier(arrays)


def behind(arrays, *others):
    return lax.optimization_barrier((arrays, others))[0]


def settled(v):
    return with_layout_constraint(v.transpose(1, 0, 2), Layout(major_to_minor=(0, 1, 2)))


def in_order(keep, send):
    return [(q[0], q[1]) for q in (keep[0], send[0], keep[1], send[1])]


def per_device(
    tokens,
    gain_one,
    shift_one,
    qkv_weight,
    query_bias,
    value_bias,
    out_weight,
    out_bias,
    gain_two,
    shift_two,
    lift_weight,
    lift_bias,
    drop_weight,
    drop_bias,
    cotangent,
    swaps,
):
    length, width = tokens.shape[1:]
    plan = Butterfly() if swaps else Collective()
    index = plan.index
    small = (
        gain_one,
        shift_one,
        query_bias,
        value_bias,
        out_bias,
        gain_two,
        shift_two,
        drop_bias,
    )
    ff = lift_weight.shape[1]
    rest = (out_weight, lift_weight, drop_weight)
    if swaps:
        packed = pack_first(index, small, lift_bias, qkv_weight)
        tokens = with_layout_constraint(tokens, Layout(major_to_minor=(0, 1, 2)))
        near = behind(plan.over_x(packed), tokens)
        qkv = (qkv_weight, near, plan.over_core(near))
        rest_then, packed = after(rest, packed)
        nears = [plan.over_x(half) for half in pack_rest(index, rest_then)]
    else:
        packed, theirs = plan.gather_vectors(small, lift_bias)
        own, near, far = plan.gather_weight(qkv_weight)
        qkv = (own, jnp.concatenate([near, theirs]), far)
    normed, projected, mixed, full_qkv, vectors = forward_attention(
        index, tokens, ff, packed, qkv
    )
    if swaps:
        mixed, nears = after(mixed, nears)
        pieces = [piece for near in nears for piece in (near, plan.over_core(near))]
    else:
        (out_own, *outs), (lift_own, *lifts), (drop_own, *drops) = map(plan.gather_weight, rest)
        rest = (out_own, lift_own, drop_own)
        pieces = [*lifts, *(jnp.concatenate(both) for both in zip(drops, outs))]
    outer = (*rest, *pieces)
    output, d_middle, d_mixed, keep_a, send_a = mlp_both_ways(
        index, tokens, cotangent, mixed, vectors, ff, outer
    )
    backward = functools.partial(
        attention_backward, index, tokens, projected, normed, full_qkv, vectors
    )
    images, half = tokens.shape[0], width // 2
    if swaps:
        got_a = plan.over_core(send_a)
        input_grad, *sums = backward(d_mixed, d_middle, 0, 2)
        sums, got_a = after(sums, got_a)
        parts_a, stay_a = plan.scatter(keep_a, got_a)
        sums, parts_a = after(sums, parts_a)
        more_a = plan.send(parts_a)
        input_grad, keep_c, send_c = backward(
            d_mixed, d_middle, 2, images, (*sums, input_grad)
        )
        send_c, more_a = after(send_c, more_a)
        got_c = plan.over_core(send_c)
        terms = (stay_a, *more_a)
        high_a = sum(plan.half(v, 1 - plan.z) for v in terms)
        over_a = plan.over_z(high_a, 1)
        got_c = behind(got_c, high_a)
        parts_c, stay_c = plan.scatter(keep_c, got_c)
        over_a = behind(over_a, parts_c)
        more_c = plan.send(parts_c)
        low_a = sum(plan.half(v, plan.z) for v in terms) + over_a
        over_a = plan.over_z(low_a, 2)
        more_c = behind(more_c, low_a)
        sum_c = stay_c + more_c[0] + more_c[1] + more_c[2]
        over_c = plan.over_z(sum_c, 1)
        over_a, over_c = after(over_a, over_c)
        low_a, sum_c = after(low_a + over_a, sum_c + over_c)
        high_a, over_c = plan.over_z(low_a, 1), plan.over_z(sum_c, 2)
        across_low, beside_low = plan.over_y(low_a), plan.over_core(low_a)
        output, input_grad = settled(output), settled(input_grad)
        high_a, over_c, across_low, beside_low, output, input_grad = after(
            high_a, over_c, across_low, beside_low, output, input_grad
        )
        output, input_grad = output.transpose(1, 0, 2), input_grad.transpose(1, 0, 2)
        across_high, beside_high = plan.over_y(high_a), plan.over_core(high_a)
        corner_low = plan.over_core(across_low)
        sum_c = sum_c + over_c
        across_c, beside_c = plan.over_y(sum_c), plan.over_core(sum_c)
        across_high, across_c, beside_c = after(across_high, across_c, beside_c)
        pieces_c = (sum_c, across_c, beside_c, plan.over_core(across_c))
        pieces_a = (
            low_a,
            high_a,
            across_low,
            across_high,
            beside_low,
            beside_high,
            corner_low,
            plan.over_core(across_high),
        )
        pieces_a, pieces_c = after(pieces_a, pieces_c)
        (
            g_drop,
            g_lift,
            g_out,
            g_out_bias,
            g_gain_two,
            g_shift_two,
            g_drop_bias,
            g_lift_bias,
            g_qkv,
            g_query,
            g_value,
            g_gain_one,
            g_shift_one,
        ) = unpack(
            index,
            pieces_a,
            pieces_c,
            [(ff // 2, width), (half, ff), (half, width)]
            + [(half,)] * 4
            + [(ff // 2,), (half, 3 * width)]
            + [(half,)] * 4,
        )
    else:
        input_grad, *sums = backward(d_mixed, d_middle, 0, images - 2)
        input_grad, keep_c, send_c = backward(
            d_mixed, d_middle, images - 2, images, (*sums, input_grad)
        )
        deep, tall, small = ff // 4, width // 4, width // 8
        eighths = in_order(keep_a, send_a)
        g_drop = plan.reduce(jnp.concatenate([q[0][:deep] for q in eighths]))
        g_lift = plan.reduce(
            jnp.concatenate(
                [
                    jnp.concatenate(
                        [q[1][k * tall : (k + 1) * tall] for k in range(ff // width)], axis=1
                    )
                    for q in eighths
                ]
            )
        )
        g_out = plan.reduce(
            jnp.concatenate([side[deep : deep + small] for q in eighths for side in q])
        )
        rows = eighths[0][0][deep + small : deep + small + 8]
        g_out_bias, g_gain_two, g_shift_two, g_drop_bias = (plan.reduce(rows[i]) for i in range(4))
        g_lift_bias = plan.reduce(rows[4:].reshape(-1))
        eighths = in_order(keep_c, send_c)
        g_qkv = plan.reduce(
            jnp.concatenate(
                [
                    jnp.concatenate([side[k * small : (k + 1) * small] for k in range(3)], axis=1)
                    for q in eighths
                    for side in q
                ]
            )
        )
        rows = eighths[0][0][3 * small :]
        g_query, g_value, g_gain_one, g_shift_one = (plan.reduce(rows[i]) for i in range(4))
    return (
        output,
        input_grad,
        g_gain_one,
        g_shift_one,
        g_qkv,
        g_query,
        g_value,
        g_out,
        g_out_bias,
        g_gain_two,
        g_shift_two,
        g_lift,
        g_lift_bias,
        g_drop,
        g_drop_bias,
    )


def solution(mesh):
    spread = P(("rep", "fsdp"), None, None)
    vector, matrix = P("fsdp"), P("fsdp", None)
    in_specs = (
        spread,
        vector,
        vector,
        matrix,
        vector,
        vector,
        matrix,
        vector,
        vector,
        vector,
        matrix,
        vector,
        matrix,
        vector,
        spread,
    )
    out_specs = (
        spread,
        spread,
        vector,
        vector,
        matrix,
        vector,
        vector,
        matrix,
        vector,
        vector,
        vector,
        matrix,
        vector,
        matrix,
        vector,
    )
    swaps = mesh.shape["rep"] == 16 and mesh.shape["fsdp"] == 2
    return jax.shard_map(
        functools.partial(per_device, swaps=swaps),
        mesh=mesh,
        in_specs=in_specs,
        out_specs=out_specs,
        check_vma=False,
    )
```

```python
import functools

import jax
import jax.numpy as jnp
from jax import lax
from jax.experimental import pallas as pl
from jax.experimental.layout import Layout, with_layout_constraint
from jax.experimental.pallas import tpu as pltpu
from jax.sharding import PartitionSpec as P

HEADS = 6
HEAD_DIM = 64
PAIR = 2 * HEAD_DIM
LANE = 128
EPS = 1e-06
ROOT_HALF = 0.7071067811865476
GAUSS = 0.3989422804014327
LOG2E = 1.4426950408889634
SCALE = HEAD_DIM ** (-0.5)
F32 = jnp.float32
BF16 = jnp.bfloat16


def nn(a, b):
    return lax.dot_general(a, b, (((1,), (0,)), ((), ())), preferred_element_type=F32)


def nt(a, b):
    return lax.dot_general(a, b, (((1,), (1,)), ((), ())), preferred_element_type=F32)


def tn(a, b):
    return lax.dot_general(a, b, (((0,), (0,)), ((), ())), preferred_element_type=F32)


def normalise(v):
    mean = jnp.mean(v, axis=-1, keepdims=True)
    centred = v - mean
    var = jnp.mean(centred * centred, axis=-1, keepdims=True)
    inverse = lax.rsqrt(var + EPS)
    return centred * inverse, inverse


def norm_back(grad, normal, inverse, gain):
    scaled = grad * gain
    return inverse * (
        scaled
        - jnp.mean(scaled, axis=-1, keepdims=True)
        - normal * jnp.mean(scaled * normal, axis=-1, keepdims=True)
    )


def fold(v):
    return jnp.sum(v.reshape(v.shape[0] // 8, 8, v.shape[1]), axis=0)


def pad_rows(scratch, ref, length):
    for j in range(ref.shape[0]):
        scratch[j, 0:length, :] = ref[j].astype(scratch.dtype)


def zero_tail(scratch, length):
    images, rows, columns = scratch.shape
    low = (length // 16) * 16
    scratch[:, low:rows, :] = jnp.zeros((images, rows - low, columns), scratch.dtype)


def split_pair(v):
    first = lax.broadcasted_iota(jnp.int32, v.shape, 1) < HEAD_DIM
    zero = jnp.zeros_like(v)
    return jnp.concatenate([jnp.where(first, v, zero), jnp.where(first, zero, v)], axis=0)


def join_pair(v):
    rows = v.shape[0] // 2
    first = lax.broadcasted_iota(jnp.int32, (rows, PAIR), 1) < HEAD_DIM
    return jnp.where(first, v[:rows], v[rows:])


def join_pieces(full, own, near, far, index, first=0):
    block = own.shape[0]
    half = block // 2
    x, core = index[0], index[1]
    other = (1 - x) * block
    full[pl.ds(pl.multiple_of(x * block, 16), block), :] = own[...]
    full[pl.ds(pl.multiple_of(other + core * half, 16), half), :] = near[first : first + half, :]
    full[pl.ds(pl.multiple_of(other + (1 - core) * half, 16), half), :] = far[first : first + half, :]


def quarters(index, keep, send):
    x, core, y = index[0], index[1], index[2]
    for dest, owner in ((keep, core), (send, 1 - core)):
        for slot, half in ((0, x), (1, 1 - x)):
            for side in range(2):
                yield dest.at[slot, jnp.where(y == side, 0, 1)], half, owner, side


def pack_first_kernel(index, *refs):
    vectors, lift_bias, weight, packed = refs[:8], *refs[8:]
    half = weight.shape[0] // 2
    shard, width = vectors[0].shape[0], weight.shape[1] // 3
    packed[0:half, :] = weight[pl.ds(pl.multiple_of(index[1] * half, 16), half), :]
    packed[half:, :] = jnp.zeros((8, 3 * width), BF16)
    for i, ref in enumerate(vectors):
        row = ref[...].astype(F32).reshape(1, shard)
        packed[half + i : half + i + 1, 0:shard] = row.astype(BF16)
    bias = lift_bias[...].astype(F32).reshape(1, lift_bias.shape[0]).astype(BF16)
    for k in range(lift_bias.shape[0] // width):
        packed[half + k : half + k + 1, width : 2 * width] = bias[:, k * width : (k + 1) * width]


def pack_rest_kernel(index, out_own, lift_own, drop_own, lift_half, both_half):
    tall, deep = lift_half.shape[0], drop_own.shape[0] // 2
    rows_of = pl.ds(pl.multiple_of(index[1] * tall, 16), tall)
    lift_half[...] = lift_own[rows_of, :]
    both_half[0:deep, :] = drop_own[pl.ds(pl.multiple_of(index[1] * deep, 16), deep), :]
    both_half[deep:, :] = out_own[rows_of, :]


def join_vectors(vec_ref, own, other, index):
    width = vec_ref.shape[1]
    half = width // 2
    mine, theirs = own[-8:, :].astype(F32), other[-8:, :].astype(F32)
    first = index[0] == 0
    low, high = jnp.where(first, mine, theirs), jnp.where(first, theirs, mine)
    vec_ref[0:8, :] = jnp.concatenate([low[:, :half], high[:, :half]], axis=1)
    blocks = vec_ref.shape[0] // 2 - 4
    vec_ref[8 : 8 + blocks, :] = low[:blocks, width : 2 * width]
    vec_ref[8 + blocks :, :] = high[:blocks, width : 2 * width]


def attend_kernel(
    length,
    index,
    tok_ref,
    packed,
    own,
    near,
    far,
    normed_ref,
    proj_ref,
    mixed_ref,
    w_ref,
    vec_ref,
    n_s,
):
    images, rows, width = n_s.shape

    @pl.when(pl.program_id(0) == 0)
    def _():
        zero_tail(n_s, length)
        join_pieces(w_ref, own, near, far, index)
        join_vectors(vec_ref, packed, near, index)

    gain, shift = vec_ref[0:1, :], vec_ref[1:2, :]
    bias = jnp.concatenate([vec_ref[2:3, :], jnp.zeros((1, width), F32), vec_ref[3:4, :]], axis=1)
    for j in range(images):
        normal, _ = normalise(tok_ref[j].astype(F32))
        n_s[j, 0:length, :] = (normal * gain + shift).astype(BF16)
    normed_ref[...] = n_s[...]
    flat = n_s[...].reshape(images * rows, width)
    proj_ref[...] = (nn(flat, w_ref[...]) + bias).astype(BF16).reshape(images, rows, 3 * width)
    live = lax.broadcasted_iota(jnp.int32, (2 * rows, rows), 1) < length
    ones = jnp.ones((rows, PAIR), BF16)
    for j in range(images):
        for c in range(0, width, PAIR):
            query = split_pair(proj_ref[j, :, c : c + PAIR] * jnp.asarray(SCALE, BF16))
            key = proj_ref[j, :, width + c : width + c + PAIR]
            value = proj_ref[j, :, 2 * width + c : 2 * width + c + PAIR]
            scores = jnp.where(live, nt(query, key), -1e30)
            top = jnp.max(scores, axis=-1, keepdims=True)
            weights = jnp.exp(scores - top).astype(BF16)
            both = nn(weights, jnp.concatenate([value, ones], axis=1))
            mixed_ref[j, :, c : c + PAIR] = join_pair(both[:, :PAIR] / both[:, PAIR:]).astype(BF16)


def mlp_kernel(
    length,
    chunk,
    index,
    tok_ref,
    cot_ref,
    mixed_ref,
    vec_ref,
    out_own,
    lift_own,
    drop_own,
    lift_near,
    lift_far,
    both_near,
    both_far,
    out_ref,
    d_middle_ref,
    d_mixed_ref,
    keep,
    send,
    x_s,
    z_s,
    w_out_ref,
    w_lift_ref,
    w_drop_ref,
    lift_bias_ref,
    a_drop,
    a_lift,
    a_out,
    a_vec,
    a_bias,
):
    step = pl.program_id(0)
    images, rows, width = x_s.shape
    total = images * rows
    hidden_width = w_lift_ref.shape[1]

    @pl.when(step == 0)
    def _():
        zero_tail(x_s, length)
        zero_tail(z_s, length)
        deep = drop_own.shape[0] // 2
        join_pieces(w_out_ref, out_own, both_near, both_far, index, deep)
        join_pieces(w_lift_ref, lift_own, lift_near, lift_far, index)
        join_pieces(w_drop_ref, drop_own, both_near, both_far, index)
        for k in range(hidden_width // width):
            lift_bias_ref[:, k * width : (k + 1) * width] = vec_ref[8 + k : 9 + k, :]
        for acc in (a_drop, a_lift, a_out, a_vec, a_bias):
            acc[...] = jnp.zeros_like(acc)

    pad_rows(x_s, tok_ref, length)
    pad_rows(z_s, cot_ref, length)
    out_bias, gain, shift, drop_bias = (vec_ref[i : i + 1, :] for i in range(4, 8))
    mixed = mixed_ref[...].reshape(total, width)
    dz = z_s[...].reshape(total, width)
    dz_f = dz.astype(F32)
    middle = x_s[...].reshape(total, width).astype(F32) + nn(mixed, w_out_ref[...]) + out_bias
    normal, inverse = normalise(middle)
    normed = (normal * gain + shift).astype(BF16)
    result = middle + drop_bias
    d_normed = jnp.zeros((total, width), F32)
    for c in range(0, hidden_width, chunk):
        part = slice(c, c + chunk)
        hidden = nn(normed, w_lift_ref[:, part]) + lift_bias_ref[:, part]
        cdf = 0.5 + 0.5 * lax.erf(hidden * ROOT_HALF)
        bell = jnp.exp(hidden * hidden * -0.5) * GAUSS
        active = (hidden * cdf).astype(BF16)
        d_active = nt(dz, w_drop_ref[part, :])
        d_hidden_f = d_active * (cdf + hidden * bell)
        d_hidden = d_hidden_f.astype(BF16)
        result = result + nn(active, w_drop_ref[part, :])
        d_normed = d_normed + nt(d_hidden, w_lift_ref[:, part])
        a_drop[part, :] += tn(active, dz)
        a_lift[:, part] += tn(normed, d_hidden)
        a_bias[:, part] += fold(d_hidden.astype(F32))
    out = result.astype(BF16)
    for j in range(images):
        out_ref[j] = out[j * rows : j * rows + length]
    d_middle = dz_f + norm_back(d_normed, normal, inverse, gain)
    d_middle_ref[...] = d_middle.reshape(images, rows, width)
    d_attended = d_middle.astype(BF16)
    d_mixed_ref[...] = nt(d_attended, w_out_ref[...]).astype(BF16).reshape(images, rows, width)
    a_out[...] += tn(mixed, d_attended)
    a_vec[0] += fold(d_attended.astype(F32))
    a_vec[1] += fold(d_normed * normal)
    a_vec[2] += fold(d_normed)
    a_vec[3] += fold(dz_f)

    @pl.when(step == pl.num_programs(0) - 1)
    def _():
        columns = jnp.sum(a_bias[...], axis=0, keepdims=True)
        vectors = jnp.concatenate(
            [jnp.sum(a_vec[...], axis=1)]
            + [columns[:, c : c + width] for c in range(0, hidden_width, width)],
            axis=0,
        ).astype(BF16)
        deep, tall, small = hidden_width // 4, width // 4, width // 8
        for place, half, core, side in quarters(index, keep, send):
            quarter = 2 * half + core
            if side == 0:
                first = pl.multiple_of(quarter * deep, 8)
                place[0:deep, :] = a_drop[pl.ds(first, deep), :].astype(BF16)
                place[deep + small : deep + small + 8, :] = vectors
                place[deep + small + 8 :, :] = jnp.zeros((8, width), BF16)
            else:
                rows_of = pl.ds(pl.multiple_of(quarter * tall, 8), tall)
                for k in range(hidden_width // width):
                    place[k * tall : (k + 1) * tall, :] = a_lift[
                        rows_of, k * width : (k + 1) * width
                    ].astype(BF16)
                place[deep + small :, :] = jnp.zeros((16, width), BF16)
            first = pl.multiple_of(quarter * tall + side * small, 8)
            place[deep : deep + small, :] = a_out[pl.ds(first, small), :].astype(BF16)


def back_kernel(
    length, first, last, index, tok_ref, proj_ref, normed_ref, d_mixed_ref, d_middle_ref, w_ref, vec_ref, *refs
):
    if not first:
        old, refs = refs[:3], refs[4:]
    in_grad_ref = refs[0]
    if last:
        keep, send = refs[1:3]
        sums, d_s = refs[3:6], refs[6]
    else:
        sums, d_s = refs[1:4], refs[4]
    a_qkv, a_proj, a_vec = sums
    images, rows, wide = d_s.shape
    width = wide // 3
    total = images * rows

    @pl.when(pl.program_id(0) == 0)
    def _():
        for i, acc in enumerate(sums):
            acc[...] = jnp.zeros_like(acc) if first else old[i][...]

    live = lax.broadcasted_iota(jnp.int32, (rows, 2 * rows), 0) < length
    for j in range(images):
        for c in range(0, width, PAIR):
            query = split_pair(proj_ref[j, :, c : c + PAIR] * jnp.asarray(SCALE, BF16))
            key = proj_ref[j, :, width + c : width + c + PAIR]
            value = proj_ref[j, :, 2 * width + c : 2 * width + c + PAIR]
            d_mixed = split_pair(d_mixed_ref[j, :, c : c + PAIR])
            scores = jnp.where(live, nt(key, query), -1e30)
            top = jnp.max(scores, axis=0, keepdims=True)
            weights = jnp.exp(scores - top)
            probs = weights * (1.0 / jnp.sum(weights, axis=0, keepdims=True))
            d_probs = nt(value, d_mixed)
            delta = jnp.sum(probs * d_probs, axis=0, keepdims=True)
            d_scores = (probs * (d_probs - delta)).astype(BF16)
            d_value = nn(probs.astype(BF16), d_mixed)
            d_key = nn(d_scores, query)
            d_query = join_pair(tn(d_scores, key)) * SCALE
            d_s[j, :, c : c + PAIR] = d_query.astype(BF16)
            d_s[j, :, width + c : width + c + PAIR] = d_key.astype(BF16)
            d_s[j, :, 2 * width + c : 2 * width + c + PAIR] = d_value.astype(BF16)
    d_proj = d_s[...].reshape(total, wide)
    a_qkv[...] += tn(normed_ref[...].reshape(total, width), d_proj)
    a_proj[...] += fold(d_proj.astype(F32))
    d_normed = nt(d_proj, w_ref[...])
    gain = vec_ref[0:1, :]
    for j in range(images):
        normal, inverse = normalise(tok_ref[j].astype(F32))
        grad = d_normed[j * rows : j * rows + length]
        in_grad_ref[j] = (
            d_middle_ref[j, 0:length, :] + norm_back(grad, normal, inverse, gain)
        ).astype(BF16)
        a_vec[0:1, :] += jnp.sum(grad * normal, axis=0, keepdims=True)
        a_vec[1:2, :] += jnp.sum(grad, axis=0, keepdims=True)
    if not last:
        return

    @pl.when(pl.program_id(0) == pl.num_programs(0) - 1)
    def _():
        columns = jnp.sum(a_proj[...], axis=0, keepdims=True)
        vectors = jnp.concatenate(
            [columns[:, :width], columns[:, 2 * width :], a_vec[...], jnp.zeros((4, width), F32)],
            axis=0,
        ).astype(BF16)
        small = width // 8
        for place, half, core, side in quarters(index, keep, send):
            first_row = pl.multiple_of((2 * half + core) * 2 * small + side * small, 8)
            for k in range(3):
                place[k * small : (k + 1) * small, :] = a_qkv[
                    pl.ds(first_row, small), k * width : (k + 1) * width
                ].astype(BF16)
            place[3 * small :, :] = vectors


def placed(full, index, pieces):
    core, y, z = index[1], index[2], index[3]
    rows = pieces[0].shape[0]
    spots = ((core, y), (core, 1 - y), (1 - core, y), (1 - core, 1 - y))
    if len(pieces) == 4:
        for (owner, side), piece in zip(spots, pieces):
            full[owner, side] = piece[...].astype(F32)
        return
    for i, (owner, side) in enumerate(spots):
        for piece, part in ((pieces[2 * i], z), (pieces[2 * i + 1], 1 - z)):
            place = pl.ds(pl.multiple_of(part * rows, 8), rows)
            full[owner, side, place, :] = piece[...].astype(F32)


def own_half(index, row):
    half = row.shape[-1] // 2
    return jnp.where(index[0] == 0, row[:, :half], row[:, half:])[0]


def unpack_kernel(index, *refs):
    unpack_outer(index, refs[0:8], refs[12:20], refs[25])
    unpack_inner(index, refs[8:12], refs[20:25], refs[26])


def unpack_outer(index, pieces, outs, full):
    g_drop, g_lift, g_out, g_out_bias, g_gain, g_shift, g_drop_bias, g_lift_bias = outs
    placed(full, index, pieces)
    width = g_out.shape[1]
    deep, tall, small = g_drop.shape[0] // 2, width // 4, width // 8
    blocks = g_lift.shape[1] // width
    for core in range(2):
        g_drop[core * deep : (core + 1) * deep, :] = full[core, 0, 0:deep, :]
        for k in range(blocks):
            g_lift[core * tall : (core + 1) * tall, k * width : (k + 1) * width] = full[
                core, 1, k * tall : (k + 1) * tall, :
            ]
        for side in range(2):
            first = core * tall + side * small
            g_out[first : first + small, :] = full[core, side, deep : deep + small, :]
    vectors = full[0, 0, deep + small :, :]
    for i, ref in enumerate((g_out_bias, g_gain, g_shift, g_drop_bias)):
        ref[...] = own_half(index, vectors[i : i + 1, :])
    for k in range(blocks // 2):
        row = jnp.where(
            index[0] == 0,
            vectors[4 + k : 5 + k, :],
            vectors[4 + blocks // 2 + k : 5 + blocks // 2 + k, :],
        )
        g_lift_bias[k * width : (k + 1) * width] = row[0]


def unpack_inner(index, pieces, outs, full):
    g_qkv, g_query, g_value, g_gain, g_shift = outs
    placed(full, index, pieces)
    width = full.shape[3]
    small = width // 8
    for core in range(2):
        for side in range(2):
            first = (2 * core + side) * small
            for k in range(3):
                g_qkv[first : first + small, k * width : (k + 1) * width] = full[
                    core, side, k * small : (k + 1) * small, :
                ]
    vectors = full[0, 0, 3 * small :, :]
    for i, ref in enumerate((g_query, g_value, g_gain, g_shift)):
        ref[...] = own_half(index, vectors[i : i + 1, :])


VMEM_LIMIT = 40 * 1024 * 1024
PARAMS = pltpu.CompilerParams(vmem_limit_bytes=VMEM_LIMIT)
SCALARS = pl.BlockSpec(memory_space=pltpu.SMEM)


def whole(*shape):
    return pl.BlockSpec(shape, lambda i: (0,) * len(shape))


def whole_like(arrays):
    return [whole(*a.shape) for a in arrays]


def per_step(*shape):
    return pl.BlockSpec(shape, lambda i: (i,) + (0,) * (len(shape) - 1))


def shape_of(dtype, *shape):
    return jax.ShapeDtypeStruct(shape, dtype)


def cost(microseconds):
    return pl.CostEstimate(flops=int(microseconds * 1e3), bytes_accessed=1, transcendentals=0)


def pack_first(index, vectors, lift_bias, weight):
    rows, columns = weight.shape
    return pl.pallas_call(
        pack_first_kernel,
        grid=(1,),
        in_specs=[SCALARS, *whole_like((*vectors, lift_bias, weight))],
        out_specs=whole(rows // 2 + 8, columns),
        out_shape=shape_of(BF16, rows // 2 + 8, columns),
        compiler_params=PARAMS,
        cost_estimate=cost(1),
        name="pack_first",
    )(index, *vectors, lift_bias, weight)


def pack_rest(index, weights):
    out_weight, lift_weight, drop_weight = weights
    tall, width = out_weight.shape[0] // 2, out_weight.shape[1]
    shapes = [(tall, lift_weight.shape[1]), (drop_weight.shape[0] // 2 + tall, width)]
    return pl.pallas_call(
        pack_rest_kernel,
        grid=(1,),
        in_specs=[SCALARS, *whole_like(weights)],
        out_specs=[whole(*d) for d in shapes],
        out_shape=[shape_of(BF16, *d) for d in shapes],
        compiler_params=PARAMS,
        cost_estimate=cost(1),
        name="pack_rest",
    )(index, *weights)


def forward_attention(index, tokens, ff, packed, pieces):
    images, length, width = tokens.shape
    rows = -(-length // 16) * 16
    group = 4 if images % 4 == 0 else 1
    return pl.pallas_call(
        functools.partial(attend_kernel, length),
        grid=(images // group,),
        in_specs=[SCALARS, per_step(group, length, width), *whole_like((packed, *pieces))],
        out_specs=[
            per_step(group, rows, width),
            per_step(group, rows, 3 * width),
            per_step(group, rows, width),
            whole(width, 3 * width),
            whole(8 + ff // width, width),
        ],
        out_shape=[
            shape_of(BF16, images, rows, width),
            shape_of(BF16, images, rows, 3 * width),
            shape_of(BF16, images, rows, width),
            shape_of(BF16, width, 3 * width),
            shape_of(F32, 8 + ff // width, width),
        ],
        scratch_shapes=[pltpu.VMEM((group, rows, width), BF16)],
        compiler_params=PARAMS,
        cost_estimate=cost(1),
        name="attend",
    )(index, tokens, packed, *pieces)


def mlp_both_ways(index, tokens, cotangent, mixed, vectors, ff, pieces):
    images, length, width = tokens.shape
    rows = mixed.shape[1]
    group = 2 if images % 2 == 0 else 1
    eighth = (2, 2, ff // 4 + width // 8 + 16, width)
    return pl.pallas_call(
        functools.partial(mlp_kernel, length, 512),
        grid=(images // group,),
        in_specs=[
            SCALARS,
            per_step(group, length, width),
            per_step(group, length, width),
            per_step(group, rows, width),
            *whole_like((vectors, *pieces)),
        ],
        out_specs=[
            per_step(group, length, width),
            per_step(group, rows, width),
            per_step(group, rows, width),
            whole(*eighth),
            whole(*eighth),
        ],
        out_shape=[
            shape_of(BF16, images, length, width),
            shape_of(F32, images, rows, width),
            shape_of(BF16, images, rows, width),
            shape_of(BF16, *eighth),
            shape_of(BF16, *eighth),
        ],
        scratch_shapes=[
            pltpu.VMEM((group, rows, width), BF16),
            pltpu.VMEM((group, rows, width), BF16),
            pltpu.VMEM((width, width), BF16),
            pltpu.VMEM((width, ff), BF16),
            pltpu.VMEM((ff, width), BF16),
            pltpu.VMEM((1, ff), F32),
            pltpu.VMEM((ff, width), F32),
            pltpu.VMEM((width, ff), F32),
            pltpu.VMEM((width, width), F32),
            pltpu.VMEM((4, 8, width), F32),
            pltpu.VMEM((8, ff), F32),
        ],
        compiler_params=PARAMS,
        cost_estimate=cost(1),
        name="mlp",
    )(index, tokens, cotangent, mixed, vectors, *pieces)


def attention_backward(
    index, tokens, projected, normed, w_qkv, vectors, d_mixed, d_middle, start, stop, earlier=()
):
    images, length, width = tokens.shape
    rows = normed.shape[1]
    wide = 3 * width
    group = 2 if images % 2 == 0 else 1
    offset = start // group
    first, last = not earlier, stop == images
    chunk = (2, 2, 3 * width // 8 + 8, width)
    sums = [(width, wide), (8, wide), (2, width)]

    def at(*shape):
        return pl.BlockSpec((group,) + shape, lambda i: (i + offset if offset else i, 0, 0))

    return pl.pallas_call(
        functools.partial(back_kernel, length, first, last),
        grid=((stop - start) // group,),
        in_specs=[
            SCALARS,
            at(length, width),
            at(rows, wide),
            at(rows, width),
            at(rows, width),
            at(rows, width),
            *whole_like((w_qkv, vectors)),
        ]
        + ([] if first else [whole(*d) for d in sums] + [pl.BlockSpec(memory_space=pl.ANY)]),
        out_specs=[at(length, width)]
        + ([whole(*chunk)] * 2 if last else [whole(*d) for d in sums]),
        out_shape=[shape_of(BF16, images, length, width)]
        + ([shape_of(BF16, *chunk)] * 2 if last else [shape_of(F32, *d) for d in sums]),
        scratch_shapes=([pltpu.VMEM(d, F32) for d in sums] if last else [])
        + [pltpu.VMEM((group, rows, wide), BF16)],
        input_output_aliases={} if first else {11: 0},
        compiler_params=PARAMS,
        cost_estimate=cost(1),
        name="back",
    )(index, tokens, projected, normed, d_mixed, d_middle, w_qkv, vectors, *earlier)


def unpack(index, outer, inner, shapes):
    rows, width = outer[0].shape
    return pl.pallas_call(
        unpack_kernel,
        grid=(1,),
        in_specs=[SCALARS, *whole_like((*outer, *inner))],
        out_specs=[whole(*d) for d in shapes],
        out_shape=[shape_of(F32, *d) for d in shapes],
        scratch_shapes=[
            pltpu.VMEM((2, 2, 2 * rows, width), F32),
            pltpu.VMEM((2, 2) + inner[0].shape, F32),
        ],
        compiler_params=PARAMS,
        cost_estimate=cost(1),
        name="unpack",
    )(index, *outer, *inner)


AXES = ("rep", "fsdp")


class Butterfly:
    def __init__(self):
        rep, x = lax.axis_index("rep"), lax.axis_index("fsdp")
        self.z = (rep >> 2) & 1
        self.index = jnp.stack([x, rep & 1, (rep >> 1) & 1, self.z]).astype(jnp.int32)

    def swap(self, v, rep_mask, x_mask=0):
        pairs = [
            (rep * 2 + x, (rep ^ rep_mask) * 2 + (x ^ x_mask)) for rep in range(16) for x in range(2)
        ]
        return lax.ppermute(v, AXES, pairs)

    def over_x(self, v):
        return self.swap(v, 0, 1)

    def over_core(self, v):
        return self.swap(v, 1)

    def over_y(self, v):
        return self.swap(v, 2)

    def over_z(self, v, mask):
        return self.swap(v, 4 * mask)

    def over_corner(self, v):
        return self.swap(v, 2, 1)

    def half(self, v, which):
        rows = v.shape[0] // 2
        return lax.dynamic_slice_in_dim(v, which * rows, rows, 0)

    def scatter(self, keep, got):
        total = [[keep[i, j] + got[i, j] for j in range(2)] for i in range(2)]
        return (total[1][0], total[0][1], total[1][1]), total[0][0]

    def send(self, parts):
        return self.over_x(parts[0]), self.over_y(parts[1]), self.over_corner(parts[2])


class Collective:
    def __init__(self):
        self.index = jnp.zeros((4,), jnp.int32)

    def gather_weight(self, own):
        full = lax.all_gather(own, "fsdp", axis=0, tiled=True)
        quarter = full.shape[0] // 4
        return full[: 2 * quarter], full[2 * quarter : 3 * quarter], full[3 * quarter :]

    def gather_vectors(self, vectors, lift_bias):
        whole_vectors = [lax.all_gather(v, "fsdp", axis=0, tiled=True) for v in vectors]
        whole_bias = lax.all_gather(lift_bias, "fsdp", axis=0, tiled=True)
        width = whole_vectors[0].shape[0]
        table = jnp.stack(whole_vectors).reshape(8, 2, width // 2)
        bias = whole_bias.reshape(2, -1, width)
        return (
            jnp.zeros((2, 8, 3 * width), BF16)
            .at[:, :, : width // 2]
            .set(table.transpose(1, 0, 2))
            .at[:, : bias.shape[1], width : 2 * width]
            .set(bias)
        )

    def reduce(self, v):
        owned = lax.psum_scatter(v.astype(BF16), "fsdp", scatter_dimension=0, tiled=True)
        return lax.psum(owned, "rep").astype(F32)


def after(*arrays):
    return lax.optimization_barrier(arrays)


def behind(arrays, *others):
    return lax.optimization_barrier((arrays, others))[0]


def settled(v):
    return with_layout_constraint(v.transpose(1, 0, 2), Layout(major_to_minor=(0, 1, 2)))


def in_order(keep, send):
    return [(q[0], q[1]) for q in (keep[0], send[0], keep[1], send[1])]


def per_device(
    tokens,
    gain_one,
    shift_one,
    qkv_weight,
    query_bias,
    value_bias,
    out_weight,
    out_bias,
    gain_two,
    shift_two,
    lift_weight,
    lift_bias,
    drop_weight,
    drop_bias,
    cotangent,
    swaps,
):
    length, width = tokens.shape[1:]
    plan = Butterfly() if swaps else Collective()
    index = plan.index
    small = (
        gain_one,
        shift_one,
        query_bias,
        value_bias,
        out_bias,
        gain_two,
        shift_two,
        drop_bias,
    )
    ff = lift_weight.shape[1]
    rest = (out_weight, lift_weight, drop_weight)
    if swaps:
        packed = pack_first(index, small, lift_bias, qkv_weight)
        tokens = with_layout_constraint(tokens, Layout(major_to_minor=(0, 1, 2)))
        near = behind(plan.over_x(packed), tokens)
        qkv = (qkv_weight, near, plan.over_core(near))
        rest_then, packed = after(rest, packed)
        nears = [plan.over_x(half) for half in pack_rest(index, rest_then)]
    else:
        packed, theirs = plan.gather_vectors(small, lift_bias)
        own, near, far = plan.gather_weight(qkv_weight)
        qkv = (own, jnp.concatenate([near, theirs]), far)
    normed, projected, mixed, full_qkv, vectors = forward_attention(
        index, tokens, ff, packed, qkv
    )
    if swaps:
        mixed, nears = after(mixed, nears)
        pieces = [piece for near in nears for piece in (near, plan.over_core(near))]
    else:
        (out_own, *outs), (lift_own, *lifts), (drop_own, *drops) = map(plan.gather_weight, rest)
        rest = (out_own, lift_own, drop_own)
        pieces = [*lifts, *(jnp.concatenate(both) for both in zip(drops, outs))]
    outer = (*rest, *pieces)
    output, d_middle, d_mixed, keep_a, send_a = mlp_both_ways(
        index, tokens, cotangent, mixed, vectors, ff, outer
    )
    backward = functools.partial(
        attention_backward, index, tokens, projected, normed, full_qkv, vectors
    )
    images, half = tokens.shape[0], width // 2
    if swaps:
        got_a = plan.over_core(send_a)
        input_grad, *sums = backward(d_mixed, d_middle, 0, 2)
        sums, got_a = after(sums, got_a)
        parts_a, stay_a = plan.scatter(keep_a, got_a)
        sums, parts_a = after(sums, parts_a)
        more_a = plan.send(parts_a)
        input_grad, keep_c, send_c = backward(
            d_mixed, d_middle, 2, images, (*sums, input_grad)
        )
        send_c, more_a = after(send_c, more_a)
        got_c = plan.over_core(send_c)
        sum_a = stay_a + more_a[0] + more_a[1] + more_a[2]
        low_a, high_a = plan.half(sum_a, plan.z), plan.half(sum_a, 1 - plan.z)
        over_a = plan.over_z(high_a, 1)
        got_c = behind(got_c, low_a, high_a)
        parts_c, stay_c = plan.scatter(keep_c, got_c)
        over_a = behind(over_a, parts_c)
        more_c = plan.send(parts_c)
        low_a = low_a + over_a
        over_a = plan.over_z(low_a, 2)
        more_c = behind(more_c, low_a)
        sum_c = stay_c + more_c[0] + more_c[1] + more_c[2]
        over_c = plan.over_z(sum_c, 1)
        over_a, over_c = after(over_a, over_c)
        low_a, sum_c = after(low_a + over_a, sum_c + over_c)
        high_a, over_c = plan.over_z(low_a, 1), plan.over_z(sum_c, 2)
        across_low, beside_low = plan.over_y(low_a), plan.over_core(low_a)
        output, input_grad = settled(output), settled(input_grad)
        high_a, over_c, across_low, beside_low, output, input_grad = after(
            high_a, over_c, across_low, beside_low, output, input_grad
        )
        output, input_grad = output.transpose(1, 0, 2), input_grad.transpose(1, 0, 2)
        across_high, beside_high = plan.over_y(high_a), plan.over_core(high_a)
        corner_low = plan.over_core(across_low)
        sum_c = sum_c + over_c
        across_c, beside_c = plan.over_y(sum_c), plan.over_core(sum_c)
        across_high, across_c, beside_c = after(across_high, across_c, beside_c)
        pieces_c = (sum_c, across_c, beside_c, plan.over_core(across_c))
        pieces_a = (
            low_a,
            high_a,
            across_low,
            across_high,
            beside_low,
            beside_high,
            corner_low,
            plan.over_core(across_high),
        )
        pieces_a, pieces_c = after(pieces_a, pieces_c)
        (
            g_drop,
            g_lift,
            g_out,
            g_out_bias,
            g_gain_two,
            g_shift_two,
            g_drop_bias,
            g_lift_bias,
            g_qkv,
            g_query,
            g_value,
            g_gain_one,
            g_shift_one,
        ) = unpack(
            index,
            pieces_a,
            pieces_c,
            [(ff // 2, width), (half, ff), (half, width)]
            + [(half,)] * 4
            + [(ff // 2,), (half, 3 * width)]
            + [(half,)] * 4,
        )
    else:
        input_grad, *sums = backward(d_mixed, d_middle, 0, images - 2)
        input_grad, keep_c, send_c = backward(
            d_mixed, d_middle, images - 2, images, (*sums, input_grad)
        )
        deep, tall, small = ff // 4, width // 4, width // 8
        eighths = in_order(keep_a, send_a)
        g_drop = plan.reduce(jnp.concatenate([q[0][:deep] for q in eighths]))
        g_lift = plan.reduce(
            jnp.concatenate(
                [
                    jnp.concatenate(
                        [q[1][k * tall : (k + 1) * tall] for k in range(ff // width)], axis=1
                    )
                    for q in eighths
                ]
            )
        )
        g_out = plan.reduce(
            jnp.concatenate([side[deep : deep + small] for q in eighths for side in q])
        )
        rows = eighths[0][0][deep + small : deep + small + 8]
        g_out_bias, g_gain_two, g_shift_two, g_drop_bias = (plan.reduce(rows[i]) for i in range(4))
        g_lift_bias = plan.reduce(rows[4:].reshape(-1))
        eighths = in_order(keep_c, send_c)
        g_qkv = plan.reduce(
            jnp.concatenate(
                [
                    jnp.concatenate([side[k * small : (k + 1) * small] for k in range(3)], axis=1)
                    for q in eighths
                    for side in q
                ]
            )
        )
        rows = eighths[0][0][3 * small :]
        g_query, g_value, g_gain_one, g_shift_one = (plan.reduce(rows[i]) for i in range(4))
    return (
        output,
        input_grad,
        g_gain_one,
        g_shift_one,
        g_qkv,
        g_query,
        g_value,
        g_out,
        g_out_bias,
        g_gain_two,
        g_shift_two,
        g_lift,
        g_lift_bias,
        g_drop,
        g_drop_bias,
    )


def solution(mesh):
    spread = P(("rep", "fsdp"), None, None)
    vector, matrix = P("fsdp"), P("fsdp", None)
    in_specs = (
        spread,
        vector,
        vector,
        matrix,
        vector,
        vector,
        matrix,
        vector,
        vector,
        vector,
        matrix,
        vector,
        matrix,
        vector,
        spread,
    )
    out_specs = (
        spread,
        spread,
        vector,
        vector,
        matrix,
        vector,
        vector,
        matrix,
        vector,
        vector,
        vector,
        matrix,
        vector,
        matrix,
        vector,
    )
    swaps = mesh.shape["rep"] == 16 and mesh.shape["fsdp"] == 2
    return jax.shard_map(
        functools.partial(per_device, swaps=swaps),
        mesh=mesh,
        in_specs=in_specs,
        out_specs=out_specs,
        check_vma=False,
    )
```
